512 devices in a mesh: tile: 64 (over y, z_lo, core), img: 8 (over z_hi, x).
Axes of the slice: x: 4, y: 8, z: 8 (z_hi: 2, z_lo: 4; z = z_hi * 4 + z_lo), core: 2. Of those that a mesh axis runs over, the one named last changes fastest.
Arguments:
- heights: float32 [64, 64, 128], P('tile'), may hold values from -1.5 to 1.5
- albedo: float32 [64, 64, 128], P('tile'), may hold values from 0.5 to 1.5
- blocks: bfloat16 [64, 8, 64, 64, 128], P('tile', 'img'), may hold values from 0 to 1
- block_params: bfloat16 [64, 8, 64, 8], P('tile', 'img'), may hold values from -1 to 2, as said below
- block_dest: int32 [64, 8, 64, 1], P('tile', 'img'), may hold values from 0 to 63; in each aligned block of 64 rows (0 to 63, 64 to 127, ..., all dimensions but the last counted through in order) at most 2 rows name the same one
Outputs:
- grad_heights: float32 [64, 64, 128], P('tile', 'img')
- grad_albedo: float32 [64, 64, 128], P('tile', 'img')
The draws below stay inside these ranges and needn't reach their ends.
Inputs may be any that keep to these rules, and one draw needn't show every extreme that they name: `block_params`: columns 0 to 2 are a unit sun vector whose third entry lies between 0.05 and 0.43, columns 3 to 5 a unit view vector whose first two entries lie within -0.15 and 0.15, column 6 lies between 0.2 and 0.9 and column 7 between 0.5 and 2. `block_dest`: of the blocks held by one device, at most 2 lie on any one tile, and in every draw some device holds exactly 2 blocks of some tile.
All inputs are finite; a program needn't handle non-finite values.
Results may differ from the reference program's by a relative error of at most 0.0003.
Values may be sent and summed in bfloat16 or wider, within the bound.
No kernel may reach another device: no remote copies, remote signals or barrier semaphores. Data moves between devices by JAX's collectives and lax.ppermute only.
A program may use at most 64 MiB of HBM per device.

```python
import math
import jax
import jax.numpy as jnp
import numpy as np
from jax import lax

TH = 64
TW = 128
BLK_DEV = 64
TCOLS = 8
TILES = 64
GROUPS = 8
TROWS = 8
CAP = 2


def draw_block_params(key, part):
    block_shape = (TILES, GROUPS, BLK_DEV)
    subkeys = jax.random.split(key, 6)
    sun_height = jax.random.uniform(subkeys[0], block_shape, jnp.float32, 0.0523, 0.4226)
    azimuth = jax.random.uniform(subkeys[1], block_shape, jnp.float32, -math.pi, math.pi)
    horizon = jnp.sqrt(1.0 - sun_height * sun_height)
    sun_x = horizon * jnp.cos(azimuth)
    sun_y = horizon * jnp.sin(azimuth)
    view_x = jax.random.uniform(subkeys[2], block_shape, jnp.float32, -0.15, 0.15)
    view_y = jax.random.uniform(subkeys[3], block_shape, jnp.float32, -0.15, 0.15)
    view_z = jnp.sqrt(1.0 - view_x * view_x - view_y * view_y)
    lambert_mix = jax.random.uniform(subkeys[4], block_shape, jnp.float32, 0.2, 0.9)
    exposure = jnp.exp(jax.random.uniform(subkeys[5], block_shape, jnp.float32, math.log(0.5), math.log(2.0)))
    stacked = jnp.stack([sun_x, sun_y, sun_height, view_x, view_y, view_z, lambert_mix, exposure], axis=-1)
    return stacked.astype(jnp.float32).astype(jnp.bfloat16)


def shard_levels(stream_key, extent, cuts, least, top_value):
    loudness, own = 1.0, jax.random.fold_in(stream_key, 6)
    for position, parts in cuts:
        draws = jnp.exp(jax.random.uniform(jax.random.fold_in(own, position), (parts,), jnp.float32, least / len(cuts), top_value / len(cuts)))
        loudness = loudness * jnp.repeat(draws, extent[position] // parts).reshape([-1 if axis == position else 1 for axis in range(len(extent))])
    return loudness


def assign_block(stream_key, own, number, rows, number_of, top, limit, lean):
    ranking = jax.random.permutation(stream_key, number_of)
    packed, common = load_shares(number_of, rows * top, limit, lean, True), load_shares(number_of, rows * top, limit, lean, False)
    places = jnp.arange(number_of)

    def named(sizes, turn):
        used = int((sizes > 0).sum())
        fixed = max(1, used // 4)
        shifted = fixed + (places - fixed + turn * (used - fixed)) % max(1, number_of - fixed)
        return jnp.zeros((number_of,), jnp.int32).at[ranking[jnp.where(places < fixed, places, shifted)]].set(jnp.asarray(sizes, jnp.int32))

    sizes = jnp.where(number % 4 == 0, named(packed, number // 4), named(common, number - number // 4 - 1))
    mixed = jax.random.permutation(jax.random.fold_in(own, 3), number_of)
    donor, taker = mixed[0:number_of // 2 * 2:2], mixed[1:number_of // 2 * 2:2]
    margin = jnp.minimum(sizes[donor] - 1, limit - sizes[taker]) // 2
    margin = jnp.where((donor == ranking[0]) | (taker == ranking[0]) | (sizes[taker] == 0), 0, jnp.maximum(margin, 0))
    shifted = jax.random.randint(jax.random.fold_in(own, 4), (number_of // 2,), 0, 1 << 20) % (margin + 1)
    sizes = sizes.at[donor].add(-shifted).at[taker].add(shifted)
    labels = jnp.searchsorted(jnp.cumsum(sizes), jnp.arange(rows * top), side="right").astype(jnp.int32)
    table = labels.reshape(top, rows).T
    table = table[jax.random.permutation(jax.random.fold_in(own, 1), rows)]
    turn = jax.random.randint(jax.random.fold_in(own, 2), (rows, 1), 0, top)
    return jnp.take_along_axis(table, (jnp.arange(top)[None, :] + turn) % top, axis=1)


def load_shares(number_of, total, most, lean, full):
    portions = [(1 << 20) // math.isqrt(standing ** lean) + 1 for standing in range(1, number_of + 1)]
    largest = most if full else min(most, max(-(-total // number_of), total * portions[0] // sum(portions)))
    least = 1 if total - largest >= number_of - 1 else 0
    holding, spare = [largest] + [least] * (number_of - 1), total - largest - least * (number_of - 1)
    while spare > 0:
        candidates = [i for i in range(1, number_of) if holding[i] < largest] or [i for i in range(1, number_of) if holding[i] < most]
        pool, left = sum([portions[i] for i in candidates]), spare
        for i in candidates:
            extra = min(most - holding[i], max(1, left * portions[i] // pool), spare)
            holding[i] = holding[i] + extra
            spare = spare - extra
    return np.array(holding)


def gaussian(rng, dims, spread, most, shards=(), kind=jnp.bfloat16):
    result = spread * jax.random.normal(rng, dims, jnp.float32)
    if shards:
        result = result * shard_levels(rng, dims, shards, -0.22, 0.18)
    return jnp.clip(result, -most, most).astype(kind)


def setup_inputs(seed: int = 0) -> dict:
    seeds = jax.random.split(jax.random.key(seed), 6)
    heights = gaussian(seeds[0], (TILES, TH, TW), 0.25, 1.5, ((0, 64),), jnp.float32)
    albedo = jnp.clip(1.0 + 0.1 * jax.random.normal(seeds[1], (TILES, TH, TW), jnp.float32), 0.5, 1.5)
    blocks = jnp.clip(1.0 * jax.random.uniform(seeds[2], (TILES, GROUPS, BLK_DEV, TH, TW), jnp.float32) ** shard_levels(seeds[2], (TILES, GROUPS, BLK_DEV, TH, TW), ((0, 64), (1, 8)), -0.2, 0.2), 0.0, 1.0).astype(jnp.bfloat16)
    block_params = draw_block_params(jax.random.fold_in(seeds[5], 71), 0)
    block_dest_keys = jax.random.split(jax.random.fold_in(seeds[4], 1), TILES * GROUPS * BLK_DEV // BLK_DEV)
    block_dest_turns = jax.random.permutation(jax.random.fold_in(seeds[4], 3), TILES * GROUPS * BLK_DEV // BLK_DEV)
    block_dest = jax.vmap(lambda own, number: assign_block(jax.random.fold_in(seeds[4], 2), own, number, BLK_DEV, TILES, 1, CAP, 2))(block_dest_keys, block_dest_turns).reshape((TILES, GROUPS, BLK_DEV, 1))
    return {"heights": heights, "albedo": albedo, "blocks": blocks, "block_params": block_params, "block_dest": block_dest}


SMOOTH = 0.0025

def slot_terms(slope_x, slope_y, shrink, albedo_map, bright, params, inv_count):
    params = params.astype(jnp.float32)

    def column(channel):
        return params[..., channel][..., None, None]
    sun_x, sun_y, sun_z = (column(0), column(1), column(2))
    view_x, view_y, view_z = (column(3), column(4), column(5))
    lambert_mix, exposure = (column(6), column(7))
    toward_sun = sun_z - slope_x * sun_x - slope_y * sun_y
    toward_view = view_z - slope_x * view_x - slope_y * view_y
    cos_inc = toward_sun * shrink
    cos_emit = toward_view * shrink
    smooth_root = jnp.sqrt(cos_inc * cos_inc + SMOOTH)
    lighted = 0.5 * (cos_inc + smooth_root)
    denom_sum = lighted + cos_emit
    shading = 2.0 * lambert_mix * lighted / denom_sum + (1.0 - lambert_mix) * lighted
    misfit = exposure * albedo_map * shading - bright
    scaled = exposure * misfit * inv_count
    grad_shade = scaled * albedo_map
    albedo_term = scaled * shading
    denom_square = denom_sum * denom_sum
    grad_lit = grad_shade * (2.0 * lambert_mix * cos_emit / denom_square + 1.0 - lambert_mix)
    grad_inc = grad_lit * 0.5 * (1.0 + cos_inc / smooth_root)
    grad_emit = grad_shade * (-2.0 * lambert_mix * lighted / denom_square)
    grad_shrink = grad_inc * toward_sun + grad_emit * toward_view
    grad_sun = grad_inc * shrink
    grad_view = grad_emit * shrink
    term_x = -(sun_x * grad_sun + view_x * grad_view)
    term_y = -(sun_y * grad_sun + view_y * grad_view)
    return (term_x, term_y, grad_shrink, albedo_term)

def to_grid(tiled):
    return tiled.reshape(TROWS, TCOLS, TH, TW).transpose(0, 2, 1, 3).reshape(TROWS * TH, TCOLS * TW)

def to_tiles(grid):
    return grid.reshape(TROWS, TH, TCOLS, TW).transpose(0, 2, 1, 3).reshape(TILES, TH, TW)

def slopes(heights):
    padded = jnp.pad(to_grid(heights), 1, mode='edge')
    slope_x = (padded[1:-1, 2:] - padded[1:-1, :-2]) * 0.5
    slope_y = (padded[2:, 1:-1] - padded[:-2, 1:-1]) * 0.5
    return (to_tiles(slope_x), to_tiles(slope_y))

def reference(heights, albedo, blocks, block_params, block_dest):
    (slope_x, slope_y), pullback = jax.vjp(slopes, heights)
    shrink = 1.0 / jnp.sqrt(1.0 + slope_x * slope_x + slope_y * slope_y)
    sources = TILES * GROUPS
    flat_bright = blocks.reshape(sources, BLK_DEV, TH, TW)
    flat_params = block_params.reshape(sources, BLK_DEV, 8)
    flat_dest = block_dest.reshape(sources, BLK_DEV).astype(jnp.int32)
    inv_count = 1.0 / BLK_DEV

    def visit_source(totals, inputs):
        bright, params, target = inputs
        pieces = slot_terms(slope_x[target], slope_y[target], shrink[target], albedo[target], bright.astype(jnp.float32), params, inv_count)
        return (totals.at[:, target].add(jnp.stack(pieces)), None)
    totals, unused = lax.scan(visit_source, jnp.zeros((4, TILES, TH, TW), jnp.float32), (flat_bright, flat_params, flat_dest))
    shrink_cube = shrink * shrink * shrink
    grad_x = totals[0] - slope_x * shrink_cube * totals[2]
    grad_y = totals[1] - slope_y * shrink_cube * totals[2]
    grad_heights, = pullback((grad_x, grad_y))
    return (grad_heights, totals[3])
```

```python
import functools

import jax
import jax.numpy as jnp
from jax import lax
from jax.experimental import pallas as pl
from jax.experimental.pallas import tpu as pltpu
from jax.sharding import PartitionSpec as P

TCOLS = 8
SMOOTH = 0.0025
PARAMS = 8
EXTRA = 8


def shifted(value, axis, steps):
    count = lax.axis_size(axis)
    leading, last = (max(0, -steps), min(count, count - steps))
    return lax.ppermute(value, axis, [(source, source + steps) for source in range(leading, last)])


def pack_kernel(dest_ref, params_ref, blocks_ref, send_ref, count, rows):
    tiles, tile_rows = send_ref.shape[0], blocks_ref.shape[1]
    number = blocks_ref.shape[0]

    def clear(tile, carry):
        count[tile] = 0
        return carry

    lax.fori_loop(0, tiles, clear, 0)
    rows[...] = jnp.zeros_like(rows)

    def place(index, carry):
        tile = dest_ref[index]
        slot = count[tile]
        count[tile] = slot + 1
        start = pl.multiple_of(slot * tile_rows, tile_rows)
        send_ref[tile, pl.ds(start, tile_rows), :] = blocks_ref[index]
        rows[tile, pl.ds(slot, 1), :] = params_ref[pl.ds(index, 1), :]
        return carry

    lax.fori_loop(0, number, place, 0)

    def fill(tile, carry):
        for slot in (0, 1):

            @pl.when(count[tile] <= slot)
            def _():
                send_ref[tile, slot * tile_rows : (slot + 1) * tile_rows, :] = jnp.zeros(
                    (tile_rows, send_ref.shape[2]), send_ref.dtype
                )

        send_ref[tile, 2 * tile_rows :, :] = rows[tile].astype(send_ref.dtype)
        return carry

    lax.fori_loop(0, tiles, fill, 0)


def terms_kernel(params_ref, maps_ref, got_ref, out_ref):
    senders = got_ref.shape[0]
    tile_rows = maps_ref.shape[1]
    step = 16
    groups = tile_rows // 8

    def strip(index, carry):
        first = pl.multiple_of(index * step, step)
        p = maps_ref[0, pl.ds(first, step), :]
        q = maps_ref[1, pl.ds(first, step), :]
        w = maps_ref[2, pl.ds(first, step), :]
        albedo = maps_ref[3, pl.ds(first, step), :]
        pw = p * w
        qw = q * w

        def sender(source, totals):
            north, east, up, shade = totals
            for slot in (0, 1):
                base = source * (2 * PARAMS) + slot * PARAMS
                sx, sy, sz, vx, vy, vz, mix, gain = [params_ref[base + k] for k in range(PARAMS)]
                mix2 = mix * 2.0
                rest = 1.0 - mix
                bright = got_ref[source, pl.ds(pl.multiple_of(slot * tile_rows + first, step), step), :].astype(jnp.float32)
                ci = sz * w - sx * pw - sy * qw
                ce = vz * w - vx * pw - vy * qw
                square = ci * ci + SMOOTH
                inv_root = lax.rsqrt(square)
                mu = (ci + square * inv_root) * 0.5
                inv = 1.0 / (mu + ce)
                k = mix2 * inv
                u = mu * inv
                c = ce * inv
                shading = mu * (k + rest)
                misfit = (gain * albedo) * shading - bright
                scaled = gain * misfit
                shade = shade + scaled * shading
                gs = scaled * albedo
                gk = gs * k
                gl = gk * c + gs * rest
                gi = gl * (mu * inv_root)
                ge = gk * u
                north = north + (gi * sx - ge * vx)
                east = east + (gi * sy - ge * vy)
                up = up + (gi * sz - ge * vz)
            return (north, east, up, shade)

        zero = jnp.zeros((step, maps_ref.shape[2]), jnp.float32)
        nx, ny, nz, shade = lax.fori_loop(0, senders, sender, (zero, zero, zero, zero), unroll=2)
        up = nz - p * nx - q * ny
        cube = w * w * w
        scale = 1.0 / 64.0
        gx = (-(w * nx) - p * cube * up) * scale
        gy = (-(w * ny) - q * cube * up) * scale
        shade = shade * scale
        for half in (0, 1):
            group = index * 2 + half
            part = slice(half * 8, half * 8 + 8)
            out_ref[group, 0:8, :] = gx[part]
            out_ref[group, 8:16, :] = gy[part]
            out_ref[group, 16:24, :] = shade[part]
        return carry

    lax.fori_loop(0, tile_rows // step, strip, 0)


def body(heights, albedo, blocks, block_params, block_dest):
    tiles_count = lax.axis_size("tile")
    groups = lax.axis_size("img")
    tile_index = lax.axis_index("tile")
    group = lax.axis_index("img")
    tile_row = tile_index // TCOLS
    tile_col = tile_index % TCOLS
    last_row = tiles_count // TCOLS - 1
    height = heights[0]
    albedo_map = albedo[0]
    tile_rows, tile_cols = height.shape
    block_count = block_dest.shape[2]

    params_wide = jnp.pad(
        block_params.reshape(block_count, PARAMS).astype(jnp.float32), ((0, 0), (0, tile_cols - PARAMS))
    )
    message = 2 * tile_rows + EXTRA
    send = pl.pallas_call(
        pack_kernel,
        out_shape=jax.ShapeDtypeStruct((tiles_count, message, tile_cols), jnp.bfloat16),
        in_specs=[
            pl.BlockSpec(memory_space=pltpu.SMEM),
            pl.BlockSpec(memory_space=pltpu.VMEM),
            pl.BlockSpec(memory_space=pltpu.VMEM),
        ],
        out_specs=pl.BlockSpec(memory_space=pltpu.VMEM),
        scratch_shapes=[
            pltpu.SMEM((tiles_count,), jnp.int32),
            pltpu.VMEM((tiles_count, EXTRA, tile_cols), jnp.float32),
        ],
        name="pack",
    )(block_dest.reshape(block_count), params_wide, blocks.reshape(block_count, tile_rows, tile_cols))
    got = lax.all_to_all(send, "tile", split_axis=0, concat_axis=0, tiled=True)

    fetched = []
    for edge_piece, offset in (
        (height[-1], TCOLS),
        (height[0], -TCOLS),
        (height[:, -1], 1),
        (height[:, 0], -1),
    ):
        fetched.append(shifted(edge_piece, "tile", offset))
    north_edge = jnp.where(tile_row > 0, fetched[0], height[0])
    south_edge = jnp.where(tile_row < last_row, fetched[1], height[-1])
    west_edge = jnp.where(tile_col > 0, fetched[2], height[:, 0])
    east_edge = jnp.where(tile_col < TCOLS - 1, fetched[3], height[:, -1])
    widened = jnp.concatenate([west_edge[:, None], height, east_edge[:, None]], axis=1)
    taller = jnp.concatenate([north_edge[None], height, south_edge[None]], axis=0)
    slope_x = (widened[:, 2:] - widened[:, :-2]) * 0.5
    slope_y = (taller[2:] - taller[:-2]) * 0.5
    shrink = 1.0 / jnp.sqrt(1.0 + slope_x * slope_x + slope_y * slope_y)
    maps = jnp.stack([slope_x, slope_y, shrink, albedo_map])

    params_in = got[:, 2 * tile_rows : 2 * tile_rows + 2, :PARAMS].astype(jnp.float32).reshape(-1)
    parts = pl.pallas_call(
        terms_kernel,
        out_shape=jax.ShapeDtypeStruct((groups, 24, tile_cols), jnp.float32),
        in_specs=[
            pl.BlockSpec(memory_space=pltpu.SMEM),
            pl.BlockSpec(memory_space=pltpu.VMEM),
            pl.BlockSpec(memory_space=pltpu.VMEM),
        ],
        out_specs=pl.BlockSpec(memory_space=pltpu.VMEM),
        name="terms",
    )(params_in, maps, got)

    summed = jnp.sum(lax.all_to_all(parts, "img", split_axis=0, concat_axis=0, tiled=True), axis=0)
    grad_x, grad_y, grad_albedo = (summed[0:8], summed[8:16], summed[16:24])

    def strip_shift(value, steps):
        axes = ("tile", "img")
        pairs = []
        for source in range(tiles_count * groups):
            tile, part = divmod(source, groups)
            row, col = divmod(tile, TCOLS)
            strip = row * groups + part + steps
            if 0 <= strip < (tiles_count // TCOLS) * groups:
                pairs.append((source, ((strip // groups) * TCOLS + col) * groups + strip % groups))
        return lax.ppermute(value, axes, pairs)

    from_north = strip_shift(grad_y[-1], 1)
    from_south = strip_shift(grad_y[0], -1)
    columns = tile_col
    east_pairs = [(t, t + 1) for t in range(tiles_count) if t % TCOLS < TCOLS - 1]
    from_west = lax.ppermute(grad_x[:, -1], "tile", east_pairs)
    from_east = lax.ppermute(grad_x[:, 0], "tile", [(b, a) for a, b in east_pairs])
    top = (tile_row == 0) & (group == 0)
    bottom = (tile_row == last_row) & (group == groups - 1)
    above = jnp.where(top, -grad_y[0], from_north)
    below = jnp.where(bottom, -grad_y[-1], from_south)
    before = jnp.where(columns == 0, -grad_x[:, 0], from_west)
    after = jnp.where(columns == TCOLS - 1, -grad_x[:, -1], from_east)
    wide = jnp.concatenate([before[:, None], grad_x, after[:, None]], axis=1)
    tall = jnp.concatenate([above[None], grad_y, below[None]], axis=0)
    grad_heights = 0.5 * (wide[:, :-2] - wide[:, 2:] + tall[:-2] - tall[2:])
    return (grad_heights[None], grad_albedo[None])


def solution(mesh):
    placed = (
        P("tile", None, None),
        P("tile", None, None),
        P("tile", "img", None, None, None),
        P("tile", "img", None, None),
        P("tile", "img", None, None),
    )
    return jax.shard_map(
        body,
        mesh=mesh,
        in_specs=placed,
        out_specs=(P("tile", "img", None), P("tile", "img", None)),
        check_vma=False,
    )
```

```python
import jax
import jax.numpy as jnp
from jax import lax
from jax.experimental import pallas as pl
from jax.experimental.pallas import tpu as pltpu
from jax.sharding import PartitionSpec as P

TCOLS = 8
SMOOTH = 0.0025
PARAMS = 8
EXTRA = 8
STRIP = 16

SMEM = pl.BlockSpec(memory_space=pltpu.SMEM)
VMEM = pl.BlockSpec(memory_space=pltpu.VMEM)


def tile_shift(value, rows, cols):
    count = lax.axis_size("tile")
    pairs = []
    for source in range(count):
        row, col = divmod(source, TCOLS)
        if 0 <= row + rows < count // TCOLS and 0 <= col + cols < TCOLS:
            pairs.append((source, source + rows * TCOLS + cols))
    return lax.ppermute(value, "tile", pairs)


def fill_table(dest_ref, table):
    number = dest_ref.shape[0]

    def clear(index, carry):
        table[index] = -1
        return carry

    lax.fori_loop(0, table.shape[0], clear, 0, unroll=8)

    def note(index, carry):
        place = dest_ref[index] * 2
        second = (table[place] >= 0).astype(jnp.int32)
        table[place + second] = index
        return carry

    lax.fori_loop(0, number, note, 0, unroll=4)


def pack_kernel(dest_ref, params_ref, blocks_ref, send_ref, table, near, far):
    tile_rows = blocks_ref.shape[1]
    fill_table(dest_ref, table)
    near[...] = params_ref[...]
    far[...] = pltpu.roll(params_ref[...], PARAMS, 1)

    def place(tile, carry):
        line = jnp.zeros((1, near.shape[1]), jnp.float32)
        for slot, rows in ((0, near), (1, far)):
            block = table[2 * tile + slot]
            kept = block >= 0
            block = jnp.maximum(block, 0)
            values = blocks_ref[block]
            send_ref[tile, slot * tile_rows : (slot + 1) * tile_rows, :] = jnp.where(kept, values, jnp.zeros_like(values))
            line = line + jnp.where(kept, rows[pl.ds(block, 1), :], 0.0)
        send_ref[tile, 2 * tile_rows :, :] = jnp.broadcast_to(line, (EXTRA, line.shape[1])).astype(send_ref.dtype)
        return carry

    lax.fori_loop(0, send_ref.shape[0], place, 0, unroll=2)


def pack(tiles, dest, params_wide, blocks):
    number, tile_rows, tile_cols = blocks.shape
    return pl.pallas_call(
        pack_kernel,
        out_shape=jax.ShapeDtypeStruct((tiles, 2 * tile_rows + EXTRA, tile_cols), jnp.bfloat16),
        in_specs=[SMEM, VMEM, VMEM],
        out_specs=VMEM,
        scratch_shapes=[pltpu.SMEM((2 * tiles,), jnp.int32)] + [pltpu.VMEM(params_wide.shape, jnp.float32)] * 2,
        name="pack",
    )(dest, params_wide, blocks)


def add_terms(params_ref, maps_ref, got_ref, first):
    tile_rows = maps_ref.shape[1]
    p = maps_ref[0, pl.ds(first, STRIP), :]
    q = maps_ref[1, pl.ds(first, STRIP), :]
    w = maps_ref[2, pl.ds(first, STRIP), :]
    albedo = maps_ref[3, pl.ds(first, STRIP), :]
    pw = p * w
    qw = q * w

    def sender(source, totals):
        sum_x, sum_y, sum_z, shade = totals
        for slot in (0, 1):
            base = source * (2 * PARAMS) + slot * PARAMS
            sx, sy, sz, vx, vy, vz, mix, gain = [params_ref[base + k] for k in range(PARAMS)]
            mix2 = mix * 2.0
            rest = 1.0 - mix
            bright = got_ref[source, pl.ds(pl.multiple_of(slot * tile_rows + first, STRIP), STRIP), :].astype(jnp.float32)
            ci = sz * w - sx * pw - sy * qw
            ce = vz * w - vx * pw - vy * qw
            square = ci * ci + SMOOTH
            inv_root = lax.rsqrt(square)
            mu = (ci + square * inv_root) * 0.5
            inv = 1.0 / (mu + ce)
            k = mix2 * inv
            u = mu * inv
            c = ce * inv
            shading = mu * (k + rest)
            misfit = (gain * albedo) * shading - bright
            scaled = gain * misfit
            shade = shade + scaled * shading
            gs = scaled * albedo
            gk = gs * k
            gl = gk * c + gs * rest
            gi = gl * (mu * inv_root)
            ge = gk * u
            sum_x = sum_x + (gi * sx - ge * vx)
            sum_y = sum_y + (gi * sy - ge * vy)
            sum_z = sum_z + (gi * sz - ge * vz)
        return (sum_x, sum_y, sum_z, shade)

    zero = jnp.zeros((STRIP, maps_ref.shape[2]), jnp.float32)
    return lax.fori_loop(0, got_ref.shape[0], sender, (zero,) * 4, unroll=2)


def terms_kernel(scale, params_ref, maps_ref, got_ref, out_ref):
    def strip(index, carry):
        first = pl.multiple_of(index * STRIP, STRIP)
        part = pl.ds(first, STRIP)
        nx, ny, nz, shade = add_terms(params_ref, maps_ref, got_ref, first)
        p, q, w = (maps_ref[k, part, :] for k in range(3))
        up = (w * w * w) * (nz - p * nx - q * ny)
        out_ref[0, part, :] = (-(w * nx) - p * up) * (0.5 * scale)
        out_ref[1, part, :] = (-(w * ny) - q * up) * (0.5 * scale)
        out_ref[2, part, :] = shade * scale
        return carry

    lax.fori_loop(0, maps_ref.shape[1] // STRIP, strip, 0)


def body(heights, albedo, blocks, block_params, block_dest):
    tiles_count = lax.axis_size("tile")
    groups = lax.axis_size("img")
    tile_index = lax.axis_index("tile")
    tile_row = tile_index // TCOLS
    tile_col = tile_index % TCOLS
    last_row = tiles_count // TCOLS - 1
    last_col = TCOLS - 1
    height = heights[0]
    albedo_map = albedo[0]
    tile_rows, tile_cols = height.shape
    block_count = block_dest.shape[2]

    params_wide = jnp.pad(
        block_params.reshape(block_count, PARAMS).astype(jnp.float32), ((0, 0), (0, tile_cols - PARAMS))
    )
    dest = block_dest.reshape(block_count)
    images = blocks.reshape(block_count, tile_rows, tile_cols)
    send = pack(tiles_count, dest, params_wide, images)
    got = lax.all_to_all(send, "tile", split_axis=0, concat_axis=0, tiled=True)

    north_edge = jnp.where(tile_row > 0, tile_shift(height[-1], 1, 0), height[0])
    south_edge = jnp.where(tile_row < last_row, tile_shift(height[0], -1, 0), height[-1])
    west_edge = jnp.where(tile_col > 0, tile_shift(height[:, -1], 0, 1), height[:, 0])
    east_edge = jnp.where(tile_col < last_col, tile_shift(height[:, 0], 0, -1), height[:, -1])
    widened = jnp.concatenate([west_edge[:, None], height, east_edge[:, None]], axis=1)
    taller = jnp.concatenate([north_edge[None], height, south_edge[None]], axis=0)
    slope_x = (widened[:, 2:] - widened[:, :-2]) * 0.5
    slope_y = (taller[2:] - taller[:-2]) * 0.5
    shrink = 1.0 / jnp.sqrt(1.0 + slope_x * slope_x + slope_y * slope_y)
    maps = jnp.stack([slope_x, slope_y, shrink, albedo_map])

    params_in = got[:, 2 * tile_rows, : 2 * PARAMS].astype(jnp.float32).reshape(-1)
    half_x, half_y, albedo_grad = pl.pallas_call(
        lambda *refs: terms_kernel(1.0 / block_count, *refs),
        out_shape=jax.ShapeDtypeStruct((3, tile_rows, tile_cols), jnp.float32),
        in_specs=[SMEM, VMEM, VMEM],
        out_specs=VMEM,
        name="terms",
    )(params_in, maps, got)

    from_north = tile_shift(half_y[-1], 1, 0)
    from_south = tile_shift(half_y[0], -1, 0)
    from_west = tile_shift(half_x[:, -1], 0, 1)
    from_east = tile_shift(half_x[:, 0], 0, -1)
    above = jnp.where(tile_row == 0, -half_y[0], from_north)
    below = jnp.where(tile_row == last_row, -half_y[-1], from_south)
    before = jnp.where(tile_col == 0, -half_x[:, 0], from_west)
    after = jnp.where(tile_col == last_col, -half_x[:, -1], from_east)
    wide = jnp.concatenate([before[:, None], half_x, after[:, None]], axis=1)
    tall = jnp.concatenate([above[None], half_y, below[None]], axis=0)
    height_grad = wide[:, :-2] - wide[:, 2:] + tall[:-2] - tall[2:]
    both = jnp.stack([height_grad, albedo_grad]).reshape(2, groups, tile_rows // groups, tile_cols)
    swapped = lax.all_to_all(both.swapaxes(0, 1), "img", split_axis=0, concat_axis=0, tiled=True)
    summed = jnp.sum(swapped, axis=0)
    return (summed[:1], summed[1:])


def solution(mesh):
    placed = (
        P("tile", None, None),
        P("tile", None, None),
        P("tile", "img", None, None, None),
        P("tile", "img", None, None),
        P("tile", "img", None, None),
    )
    return jax.shard_map(
        body,
        mesh=mesh,
        in_specs=placed,
        out_specs=(P("tile", "img", None), P("tile", "img", None)),
        check_vma=False,
    )
```

```python
import jax
import jax.numpy as jnp
from jax import lax
from jax.experimental import pallas as pl
from jax.experimental.pallas import tpu as pltpu
from jax.sharding import Mesh
from jax.sharding import PartitionSpec as P

SMOOTH = 0.0025
PARAMS = 8
STRIP = 16
ROWS, CLASSES, CORES, HALVES, DEPTH = 8, 4, 2, 2, 4
RING = CLASSES * HALVES
TILE = ("y", "zl", "c")
IMG = ("zh", "x")

SMEM = pl.BlockSpec(memory_space=pltpu.SMEM)
VMEM = pl.BlockSpec(memory_space=pltpu.VMEM)


def ring_shift(value, steps):
    pairs = []
    for low in range(CLASSES):
        for core in range(CORES):
            for high in range(HALVES):
                z = (high * CLASSES + low + steps) % RING
                source = (low * CORES + core) * HALVES + high
                pairs.append((source, ((z % CLASSES) * CORES + core) * HALVES + z // CLASSES))
    return lax.ppermute(value, ("zl", "c", "zh"), pairs)


def column_shift(value, steps):
    count = CLASSES * CORES
    pairs = [(k, k + steps) for k in range(count) if 0 <= k + steps < count]
    return lax.ppermute(value, ("zl", "c"), pairs)


def fill_table(dest_ref, table):
    def clear(index, carry):
        table[index] = -1
        return carry

    lax.fori_loop(0, table.shape[0], clear, 0, unroll=8)

    def note(index, carry):
        place = dest_ref[index] * 2
        second = (table[place] >= 0).astype(jnp.int32)
        table[place + second] = index
        return carry

    lax.fori_loop(0, dest_ref.shape[0], note, 0, unroll=4)


def pack_kernel(here_ref, dest_ref, params_ref, blocks_ref, near_ref, own_ref, other_ref, table, lines):
    tile_rows = blocks_ref.shape[1]
    fill_table(dest_ref, table)
    low, core = here_ref[0], here_ref[1]

    def target(kind, d):
        if kind == 1:
            return other_ref.at[d]
        return near_ref if d == 0 else own_ref.at[d - 1]

    for kind in range(CORES):
        for d in range(CLASSES):
            column = ((low + d) % CLASSES) * CORES + (core + kind) % CORES
            unit = target(kind, d)

            def place(row, carry):
                tile = row * (CLASSES * CORES) + column
                for slot in (0, 1):
                    block = table[2 * tile + slot]
                    kept = block >= 0
                    block = jnp.maximum(block, 0)
                    values = blocks_ref[block]
                    first = pl.multiple_of(row * tile_rows, tile_rows)
                    unit[slot, pl.ds(first, tile_rows), :] = jnp.where(kept, values, jnp.zeros_like(values))
                    lines[slot, pl.ds(row, 1), :] = jnp.where(kept, params_ref[pl.ds(block, 1), :], 0.0)
                return carry

            lax.fori_loop(0, ROWS, place, 0)
            for slot in (0, 1):
                unit[slot, ROWS * tile_rows :, :] = lines[slot].astype(unit.dtype)


def pack(here, dest, params_wide, blocks):
    number, tile_rows, tile_cols = blocks.shape
    unit = (2, ROWS * tile_rows + ROWS, tile_cols)
    return pl.pallas_call(
        pack_kernel,
        out_shape=[jax.ShapeDtypeStruct(lead + unit, jnp.bfloat16) for lead in ((), (CLASSES - 1,), (CLASSES,))],
        in_specs=[SMEM, SMEM, VMEM, VMEM],
        out_specs=[VMEM] * 3,
        scratch_shapes=[
            pltpu.SMEM((2 * ROWS * CLASSES * CORES,), jnp.int32),
            pltpu.VMEM((2, ROWS, tile_cols), jnp.float32),
        ],
        cost_estimate=pl.CostEstimate(flops=0, bytes_accessed=6 << 20, transcendentals=0),
        name="pack",
    )(here, dest, params_wide, blocks)


def terms_kernel(scale, with_sums, *refs):
    maps_ref, *refs = refs
    sums_ref = None
    if with_sums:
        sums_ref, *refs = refs
    *got, out_ref, lines, params, sem = refs
    units = [ref.at[k] for ref in got for k in range(ref.shape[0])]
    pixels = maps_ref.shape[1]
    for index, unit in enumerate(units):
        lines[index * ROWS : (index + 1) * ROWS, :] = unit[pixels:, :].astype(jnp.float32)
    copy = pltpu.make_async_copy(lines, params, sem)
    copy.start()
    copy.wait()

    def strip(index, carry):
        first = pl.multiple_of(index * STRIP, STRIP)
        part = pl.ds(first, STRIP)
        row = index // (pixels // ROWS // STRIP)
        p, q, w, albedo = (maps_ref[k, part, :] for k in range(4))
        pw = p * w
        qw = q * w
        if with_sums:
            sum_x, sum_y, sum_z, shade = (sums_ref[k, part, :] for k in range(4))
        else:
            sum_x = sum_y = sum_z = shade = jnp.zeros((STRIP, maps_ref.shape[2]), jnp.float32)
        for number, unit in enumerate(units):
            sx, sy, sz, vx, vy, vz, mix, gain = [params[number * ROWS + row, k] for k in range(PARAMS)]
            mix2 = mix * 2.0
            rest = 1.0 - mix
            bright = unit[part, :].astype(jnp.float32)
            ci = sz * w - sx * pw - sy * qw
            ce = vz * w - vx * pw - vy * qw
            square = ci * ci + SMOOTH
            inv_root = lax.rsqrt(square)
            mu = (ci + square * inv_root) * 0.5
            inv = 1.0 / (mu + ce)
            k = mix2 * inv
            u = mu * inv
            c = ce * inv
            shading = mu * (k + rest)
            misfit = (gain * albedo) * shading - bright
            scaled = gain * misfit
            shade = shade + scaled * shading
            gs = scaled * albedo
            gk = gs * k
            gl = gk * c + gs * rest
            gi = gl * (mu * inv_root)
            ge = gk * u
            sum_x = sum_x + (gi * sx - ge * vx)
            sum_y = sum_y + (gi * sy - ge * vy)
            sum_z = sum_z + (gi * sz - ge * vz)
        if scale is None:
            for k, total in enumerate((sum_x, sum_y, sum_z, shade)):
                out_ref[k, part, :] = total
        else:
            up = (w * w * w) * (sum_z - p * sum_x - q * sum_y)
            out_ref[0, part, :] = (-(w * sum_x) - p * up) * (0.5 * scale)
            out_ref[1, part, :] = (-(w * sum_y) - q * up) * (0.5 * scale)
            out_ref[2, part, :] = shade * scale
        return carry

    lax.fori_loop(0, pixels // STRIP, strip, 0)


def terms(maps, sums, got, scale, name):
    got = [g.reshape((-1,) + g.shape[-2:]) for g in got]
    count = sum(g.shape[0] for g in got)
    given = [maps] + ([] if sums is None else [sums]) + got
    pixels, cols = maps.shape[1:]
    return pl.pallas_call(
        lambda *refs: terms_kernel(scale, sums is not None, *refs),
        out_shape=jax.ShapeDtypeStruct((4 if scale is None else 3, pixels, cols), jnp.float32),
        in_specs=[VMEM] * len(given),
        out_specs=VMEM,
        scratch_shapes=[
            pltpu.VMEM((count * ROWS, cols), jnp.float32),
            pltpu.SMEM((count * ROWS, cols), jnp.float32),
            pltpu.SemaphoreType.DMA,
        ],
        cost_estimate=pl.CostEstimate(flops=60 * count * pixels * cols, bytes_accessed=4 << 20, transcendentals=0),
        name=name,
    )(*given)


def body(heights, albedo, blocks, block_params, block_dest):
    row_here = lax.axis_index("y")
    column_here = lax.axis_index(("zl", "c"))
    last_column = CLASSES * CORES - 1
    tile_rows, tile_cols = heights.shape[1:]
    block_count = block_dest.shape[2]
    pixels = ROWS * tile_rows

    params_wide = jnp.pad(
        block_params.reshape(block_count, PARAMS).astype(jnp.float32), ((0, 0), (0, tile_cols - PARAMS))
    )
    here = jnp.stack([lax.axis_index("zl"), lax.axis_index("c")]).astype(jnp.int32)
    near, own, other = pack(
        here,
        block_dest.reshape(block_count),
        params_wide,
        blocks.reshape(block_count, tile_rows, tile_cols),
    )
    swapped = lax.ppermute(other, "c", [(0, 1), (1, 0)])
    both = jnp.stack([own, swapped[1:]], axis=1)
    right = ring_shift(both[0], 1)
    left = ring_shift(both[2], -1)
    right2 = ring_shift(both[1, :, 0], 2)
    left2 = ring_shift(both[1, :, 1], -2)

    here_maps = jnp.concatenate([heights[0], albedo[0]])
    gathered = lax.all_to_all(
        jnp.broadcast_to(here_maps[None], (ROWS,) + here_maps.shape), "y", split_axis=0, concat_axis=0, tiled=True
    )
    height = gathered[:, :tile_rows].reshape(pixels, tile_cols)
    albedo_map = gathered[:, tile_rows:].reshape(pixels, tile_cols)
    west = jnp.where(column_here > 0, column_shift(height[:, -1], 1), height[:, 0])
    east = jnp.where(column_here < last_column, column_shift(height[:, 0], -1), height[:, -1])
    widened = jnp.concatenate([west[:, None], height, east[:, None]], axis=1)
    taller = jnp.concatenate([height[:1], height, height[-1:]], axis=0)
    slope_x = (widened[:, 2:] - widened[:, :-2]) * 0.5
    slope_y = (taller[2:] - taller[:-2]) * 0.5
    shrink = 1.0 / jnp.sqrt(1.0 + slope_x * slope_x + slope_y * slope_y)
    maps = jnp.stack([slope_x, slope_y, shrink, albedo_map])

    sums = terms(maps, None, [near, swapped[0]], None, "terms_local")
    sums = terms(maps, sums, [right, left], None, "terms_next")
    half_x, half_y, albedo_grad = terms(maps, sums, [right2, left2], 1.0 / block_count, "terms_far")

    before = jnp.where(column_here == 0, -half_x[:, 0], column_shift(half_x[:, -1], 1))
    after = jnp.where(column_here == last_column, -half_x[:, -1], column_shift(half_x[:, 0], -1))
    wide = jnp.concatenate([before[:, None], half_x, after[:, None]], axis=1)
    tall = jnp.concatenate([-half_y[:1], half_y, -half_y[-1:]], axis=0)
    height_grad = wide[:, :-2] - wide[:, 2:] + tall[:-2] - tall[2:]
    groups = HALVES * DEPTH
    parts = [g.reshape(ROWS * groups, 1, tile_rows // groups, tile_cols) for g in (height_grad, albedo_grad)]
    swapped_parts = lax.all_to_all(
        jnp.concatenate(parts, axis=1), ("y",) + IMG, split_axis=0, concat_axis=0, tiled=True
    )
    summed = jnp.sum(swapped_parts, axis=0)
    return (summed[:1], summed[1:])


def solution(mesh):
    physical = Mesh(mesh.devices.reshape(ROWS, CLASSES, CORES, HALVES, DEPTH), TILE + IMG)
    placed = (
        P(TILE, None, None),
        P(TILE, None, None),
        P(TILE, IMG, None, None, None),
        P(TILE, IMG, None, None),
        P(TILE, IMG, None, None),
    )
    return jax.shard_map(
        body,
        mesh=physical,
        in_specs=placed,
        out_specs=(P(TILE, IMG, None), P(TILE, IMG, None)),
        check_vma=False,
    )
```

```python
import jax
import jax.numpy as jnp
from jax import lax
from jax.experimental import pallas as pl
from jax.experimental.pallas import tpu as pltpu
from jax.sharding import Mesh
from jax.sharding import PartitionSpec as P


SMOOTH = 0.0025
PARAMS = 8
STRIP = 16
ROWS, CLASSES, CORES, HALVES, DEPTH = 8, 4, 2, 2, 4
RING = CLASSES * HALVES
TILE = ("y", "zl", "c")
IMG = ("zh", "x")

SMEM = pl.BlockSpec(memory_space=pltpu.SMEM)
VMEM = pl.BlockSpec(memory_space=pltpu.VMEM)


def ring_shift(value, steps):
    pairs = []
    for low in range(CLASSES):
        for core in range(CORES):
            for high in range(HALVES):
                z = (high * CLASSES + low + steps) % RING
                source = (low * CORES + core) * HALVES + high
                pairs.append((source, ((z % CLASSES) * CORES + core) * HALVES + z // CLASSES))
    return lax.ppermute(value, ("zl", "c", "zh"), pairs)


def column_shift(value, steps):
    count = CLASSES * CORES
    pairs = [(k, k + steps) for k in range(count) if 0 <= k + steps < count]
    return lax.ppermute(value, ("zl", "c"), pairs)


def in_vmem(*arrays):
    return [pltpu.with_memory_space_constraint(a, pltpu.VMEM) for a in arrays]


def fill_table(dest_ref, table):
    def clear(index, carry):
        table[index] = -1
        return carry

    lax.fori_loop(0, table.shape[0], clear, 0, unroll=8)

    def note(index, carry):
        place = dest_ref[index] * 2
        second = (table[place] >= 0).astype(jnp.int32)
        table[place + second] = index
        return carry

    lax.fori_loop(0, dest_ref.shape[0], note, 0, unroll=4)


def pack_kernel(here_ref, dest_ref, params_ref, blocks_ref, near_ref, own_ref, other_ref, table, lines):
    tile_rows = blocks_ref.shape[1]
    fill_table(dest_ref, table)
    low, core = here_ref[0], here_ref[1]

    def target(kind, d):
        if kind == 1:
            return other_ref.at[d]
        return near_ref if d == 0 else own_ref.at[d - 1]

    for kind in range(CORES):
        for d in range(CLASSES):
            column = ((low + d) % CLASSES) * CORES + (core + kind) % CORES
            unit = target(kind, d)

            def place(row, carry):
                tile = row * (CLASSES * CORES) + column
                for slot in (0, 1):
                    block = table[2 * tile + slot]
                    kept = block >= 0
                    block = jnp.maximum(block, 0)
                    values = blocks_ref[block]
                    first = pl.multiple_of(row * tile_rows, tile_rows)
                    unit[slot, pl.ds(first, tile_rows), :] = jnp.where(kept, values, jnp.zeros_like(values))
                    lines[slot, pl.ds(row, 1), :] = jnp.where(kept, params_ref[pl.ds(block, 1), :], 0.0)
                return carry

            lax.fori_loop(0, ROWS, place, 0)
            for slot in (0, 1):
                unit[slot, ROWS * tile_rows :, :] = lines[slot].astype(unit.dtype)


def pack(here, dest, params_wide, blocks):
    _, tile_rows, tile_cols = blocks.shape
    unit = (2, ROWS * tile_rows + ROWS, tile_cols)
    return pl.pallas_call(
        pack_kernel,
        out_shape=[pltpu.VMEM(lead + unit, jnp.bfloat16) for lead in ((), (CLASSES - 1,), (CLASSES,))],
        in_specs=[SMEM, SMEM, VMEM, VMEM],
        out_specs=[VMEM] * 3,
        scratch_shapes=[
            pltpu.SMEM((2 * ROWS * CLASSES * CORES,), jnp.int32),
            pltpu.VMEM((2, ROWS, tile_cols), jnp.float32),
        ],
        cost_estimate=pl.CostEstimate(flops=0, bytes_accessed=6 << 20, transcendentals=0),
        compiler_params=pltpu.CompilerParams(vmem_limit_bytes=4 << 20),
        name="pack",
    )(here, dest, *in_vmem(params_wide, blocks))


def terms_kernel(scale, with_sums, picks, *refs):
    maps_ref, *refs = refs
    sums_ref = None
    if with_sums:
        sums_ref, *refs = refs
    *got, out_ref, lines, params, sem = refs
    units = [ref.at[pick] for ref, some in zip(got, picks) for pick in some]
    pixels = maps_ref.shape[1]
    for index, unit in enumerate(units):
        lines[index * ROWS : (index + 1) * ROWS, :] = unit[pixels:, :].astype(jnp.float32)
    copy = pltpu.make_async_copy(lines, params, sem)
    copy.start()
    copy.wait()

    def strip(index, carry):
        first = pl.multiple_of(index * STRIP, STRIP)
        part = pl.ds(first, STRIP)
        row = index // (pixels // ROWS // STRIP)
        p, q, w, albedo = (maps_ref[k, part, :] for k in range(4))
        pw = p * w
        qw = q * w
        if with_sums:
            sum_x, sum_y, sum_z, shade = (sums_ref[k, part, :] for k in range(4))
        else:
            sum_x = sum_y = sum_z = shade = jnp.zeros((STRIP, maps_ref.shape[2]), jnp.float32)
        for number, unit in enumerate(units):
            sx, sy, sz, vx, vy, vz, mix, gain = [params[number * ROWS + row, k] for k in range(PARAMS)]
            mix2 = mix * 2.0
            rest = 1.0 - mix
            bright = unit[part, :].astype(jnp.float32)
            ci = sz * w - sx * pw - sy * qw
            ce = vz * w - vx * pw - vy * qw
            square = ci * ci + SMOOTH
            inv_root = lax.rsqrt(square)
            mu = (ci + square * inv_root) * 0.5
            inv = 1.0 / (mu + ce)
            k = mix2 * inv
            u = mu * inv
            c = ce * inv
            shading = mu * (k + rest)
            misfit = (gain * albedo) * shading - bright
            scaled = gain * misfit
            shade = shade + scaled * shading
            gs = scaled * albedo
            gk = gs * k
            gl = gk * c + gs * rest
            gi = gl * (mu * inv_root)
            ge = gk * u
            sum_x = sum_x + (gi * sx - ge * vx)
            sum_y = sum_y + (gi * sy - ge * vy)
            sum_z = sum_z + (gi * sz - ge * vz)
        if scale is None:
            for k, total in enumerate((sum_x, sum_y, sum_z, shade)):
                out_ref[k, part, :] = total
        else:
            up = (w * w * w) * (sum_z - p * sum_x - q * sum_y)
            out_ref[0, part, :] = (-(w * sum_x) - p * up) * (0.5 * scale)
            out_ref[1, part, :] = (-(w * sum_y) - q * up) * (0.5 * scale)
            out_ref[2, part, :] = shade * scale
        return carry

    lax.fori_loop(0, pixels // STRIP, strip, 0)


def terms(maps, sums, got, scale):
    arrays, picks = zip(*got)
    count = sum(len(some) for some in picks)
    given = [maps] + ([] if sums is None else [sums]) + list(arrays)
    pixels, cols = maps.shape[1:]
    return pl.pallas_call(
        lambda *refs: terms_kernel(scale, sums is not None, picks, *refs),
        out_shape=pltpu.VMEM((4 if scale is None else 3, pixels, cols), jnp.float32),
        in_specs=[VMEM] * len(given),
        out_specs=VMEM,
        scratch_shapes=[
            pltpu.VMEM((count * ROWS, cols), jnp.float32),
            pltpu.SMEM((count * ROWS, cols), jnp.float32),
            pltpu.SemaphoreType.DMA,
        ],
        cost_estimate=pl.CostEstimate(flops=60 * count * pixels * cols, bytes_accessed=4 << 20, transcendentals=0),
        compiler_params=pltpu.CompilerParams(vmem_limit_bytes=4 << 20),
    )(*in_vmem(*given))


EACH2 = [(0,), (1,)]
EACH4 = EACH2 + [(2,), (3,)]


def body(heights, albedo, blocks, block_params, block_dest):
    column_here = lax.axis_index(("zl", "c"))
    last_column = CLASSES * CORES - 1
    tile_rows, tile_cols = heights.shape[1:]
    block_count = block_dest.shape[2]
    pixels = ROWS * tile_rows

    params_wide = jnp.pad(
        block_params.reshape(block_count, PARAMS).astype(jnp.float32), ((0, 0), (0, tile_cols - PARAMS))
    )
    here = jnp.stack([lax.axis_index("zl"), lax.axis_index("c")]).astype(jnp.int32)
    near, own, other = pack(
        here,
        block_dest.reshape(block_count),
        params_wide,
        blocks.reshape(block_count, tile_rows, tile_cols),
    )
    swapped = lax.ppermute(other, "c", [(0, 1), (1, 0)])
    to_right = jnp.concatenate([own[0], swapped[1]])
    to_left = jnp.concatenate([own[2], swapped[3]])
    to_right2 = jnp.stack([own[1, 0], swapped[2, 0]])
    to_left2 = jnp.stack([own[1, 1], swapped[2, 1]])
    right = ring_shift(to_right, 1)
    left = ring_shift(to_left, -1)
    right2 = ring_shift(to_right2, 2)
    left2 = ring_shift(to_left2, -2)

    here_maps = jnp.concatenate([heights[0], albedo[0]])
    copies = jnp.broadcast_to(here_maps[None], (ROWS,) + here_maps.shape)
    gathered = lax.all_to_all(copies, "y", split_axis=0, concat_axis=0, tiled=True)
    height = gathered[:, :tile_rows].reshape(pixels, tile_cols)
    albedo_map = gathered[:, tile_rows:].reshape(pixels, tile_cols)
    first_column, final_column = height[:, 0], height[:, -1]
    from_west = column_shift(final_column, 1)
    from_east = column_shift(first_column, -1)
    west = jnp.where(column_here > 0, from_west, first_column)
    east = jnp.where(column_here < last_column, from_east, final_column)
    widened = jnp.concatenate([west[:, None], height, east[:, None]], axis=1)
    taller = jnp.concatenate([height[:1], height, height[-1:]], axis=0)
    slope_x = (widened[:, 2:] - widened[:, :-2]) * 0.5
    slope_y = (taller[2:] - taller[:-2]) * 0.5
    shrink = 1.0 / jnp.sqrt(1.0 + slope_x * slope_x + slope_y * slope_y)
    maps = jnp.stack([slope_x, slope_y, shrink, albedo_map])

    sums = terms(maps, None, [(near, [(0,), (1,)]), (swapped, [(0, 0), (0, 1)])], None)
    sums = terms(maps, sums, [(right, EACH4), (left, EACH4)], None)
    half_x, half_y, albedo_grad = terms(maps, sums, [(right2, EACH2), (left2, EACH2)], 1.0 / block_count)

    before = jnp.where(column_here == 0, -half_x[:, 0], column_shift(half_x[:, -1], 1))
    after = jnp.where(column_here == last_column, -half_x[:, -1], column_shift(half_x[:, 0], -1))
    wide = jnp.concatenate([before[:, None], half_x, after[:, None]], axis=1)
    tall = jnp.concatenate([-half_y[:1], half_y, -half_y[-1:]], axis=0)
    height_grad = wide[:, :-2] - wide[:, 2:] + tall[:-2] - tall[2:]
    groups = HALVES * DEPTH
    parts = [g.reshape(ROWS * groups, 1, tile_rows // groups, tile_cols) for g in (height_grad, albedo_grad)]
    swapped_parts = lax.all_to_all(
        jnp.concatenate(parts, axis=1), ("y",) + IMG, split_axis=0, concat_axis=0, tiled=True
    )
    summed = jnp.sum(swapped_parts, axis=0)
    return (summed[:1], summed[1:])


def solution(mesh):
    physical = Mesh(mesh.devices.reshape(ROWS, CLASSES, CORES, HALVES, DEPTH), TILE + IMG)
    placed = (
        P(TILE, None, None),
        P(TILE, None, None),
        P(TILE, IMG, None, None, None),
        P(TILE, IMG, None, None),
        P(TILE, IMG, None, None),
    )

    return jax.shard_map(
        body,
        mesh=physical,
        in_specs=placed,
        out_specs=(P(TILE, IMG, None), P(TILE, IMG, None)),
        check_vma=False,
    )
```

```python
import jax
import jax.numpy as jnp
from jax import lax
from jax.experimental import pallas as pl
from jax.experimental.pallas import tpu as pltpu
from jax.sharding import Mesh
from jax.sharding import PartitionSpec as P


SMOOTH = 0.0025
PARAMS = 8
STRIP = 16
ROWS, CLASSES, CORES, HALVES, DEPTH = 8, 4, 2, 2, 4
RING = CLASSES * HALVES
TILE = ("y", "zl", "c")
IMG = ("zh", "x")

SMEM = pl.BlockSpec(memory_space=pltpu.SMEM)
VMEM = pl.BlockSpec(memory_space=pltpu.VMEM)


def ring_shift(value, steps):
    pairs = []
    for low in range(CLASSES):
        for core in range(CORES):
            for high in range(HALVES):
                z = (high * CLASSES + low + steps) % RING
                source = (low * CORES + core) * HALVES + high
                pairs.append((source, ((z % CLASSES) * CORES + core) * HALVES + z // CLASSES))
    return lax.ppermute(value, ("zl", "c", "zh"), pairs)


def column_shift(value, steps):
    count = CLASSES * CORES
    pairs = [(k, k + steps) for k in range(count) if 0 <= k + steps < count]
    return lax.ppermute(value, ("zl", "c"), pairs)


def in_vmem(*arrays):
    return [pltpu.with_memory_space_constraint(a, pltpu.VMEM) for a in arrays]


def fill_table(dest_ref, table):
    def clear(index, carry):
        table[index] = -1
        return carry

    lax.fori_loop(0, table.shape[0], clear, 0, unroll=8)

    def note(index, carry):
        place = dest_ref[index] * 2
        second = (table[place] >= 0).astype(jnp.int32)
        table[place + second] = index
        return carry

    lax.fori_loop(0, dest_ref.shape[0], note, 0, unroll=4)


def pack_kernel(here_ref, dest_ref, params_ref, blocks_ref, near_ref, own_ref, other_ref, table, shifted, columns, rim, lines):
    number, tile_rows, tile_cols = blocks_ref.shape
    fill_table(dest_ref, table)
    for k in range(3):
        shifted[k] = params_ref[...] if k == 0 else pltpu.roll(params_ref[...], k * PARAMS, 1)

    lane8 = lax.broadcasted_iota(jnp.int32, (8, tile_cols), 1)
    sub8 = lax.broadcasted_iota(jnp.int32, (8, tile_cols), 0)
    pick = jnp.where(((sub8 == 0) & (lane8 == tile_cols - 1)) | ((sub8 == 1) & (lane8 == 0)), 1.0, 0.0).astype(jnp.bfloat16)
    flat = lax.dot_general(
        pick,
        blocks_ref[...].reshape(number * tile_rows, tile_cols),
        (((1,), (1,)), ((), ())),
        preferred_element_type=jnp.float32,
    )
    pairs = number // 2
    for m in range(pairs):
        part = slice(m * tile_cols, (m + 1) * tile_cols)
        columns[0, m : m + 1, :] = flat[0:1, part]
        columns[1, m : m + 1, :] = flat[1:2, part]
    left_half = lax.broadcasted_iota(jnp.int32, (pairs, tile_cols), 1) < tile_rows
    last, first = columns[0], columns[1]
    rim[0] = jnp.where(left_half, last, pltpu.roll(first, tile_rows, 1))
    rim[1] = jnp.where(left_half, pltpu.roll(last, tile_rows, 1), first)

    low, core = here_ref[0], here_ref[1]
    count = CLASSES * CORES
    west_half = lax.broadcasted_iota(jnp.int32, (1, tile_cols), 1) < tile_rows
    pixels = ROWS * tile_rows

    for kind in range(CORES):
        for d in range(CLASSES):
            column = ((low + d) % CLASSES) * CORES + (core + kind) % CORES
            unit = other_ref.at[d] if kind == 1 else near_ref if d == 0 else own_ref.at[d - 1]

            def place(row, carry):
                tile = row * count + column
                for slot in (0, 1):
                    block = table[2 * tile + slot]
                    west = jnp.where(column > 0, table[jnp.maximum(2 * tile - 2, 0) + slot], -1)
                    east = jnp.where(column < count - 1, table[jnp.minimum(2 * tile + 2, 2 * ROWS * count - 2) + slot], -1)
                    values = blocks_ref[jnp.maximum(block, 0)]
                    start = pl.multiple_of(row * tile_rows, tile_rows)
                    unit[slot, pl.ds(start, tile_rows), :] = jnp.where(block >= 0, values, jnp.zeros_like(values))
                    sides = []
                    line = jnp.zeros((1, tile_cols), jnp.float32)
                    for k, index in enumerate((block, west, east)):
                        safe = jnp.maximum(index, 0)
                        line = line + jnp.where(index >= 0, shifted[k, pl.ds(safe, 1), :], 0.0)
                        if k:
                            sides.append(jnp.where(index >= 0, rim[safe % 2, pl.ds(safe // 2, 1), :], 0.0))
                    lines[0, slot, pl.ds(row, 1), :] = jnp.where(west_half, sides[0], sides[1])
                    lines[1, slot, pl.ds(row, 1), :] = line
                return carry

            lax.fori_loop(0, ROWS, place, 0)
            for slot in (0, 1):
                for k in (0, 1):
                    unit[slot, pixels + k * ROWS : pixels + (k + 1) * ROWS, :] = lines[k, slot].astype(unit.dtype)


def pack(here, dest, params_wide, blocks):
    number, tile_rows, tile_cols = blocks.shape
    unit = (2, ROWS * tile_rows + 2 * ROWS, tile_cols)
    return pl.pallas_call(
        pack_kernel,
        out_shape=[pltpu.VMEM(lead + unit, jnp.bfloat16) for lead in ((), (CLASSES - 1,), (CLASSES,))],
        in_specs=[SMEM, SMEM, VMEM, VMEM],
        out_specs=[VMEM] * 3,
        scratch_shapes=[
            pltpu.SMEM((2 * ROWS * CLASSES * CORES,), jnp.int32),
            pltpu.VMEM((3,) + params_wide.shape, jnp.float32),
            pltpu.VMEM((2, number // 2, tile_cols), jnp.float32),
            pltpu.VMEM((2, number // 2, tile_cols), jnp.float32),
            pltpu.VMEM((2, 2, ROWS, tile_cols), jnp.float32),
        ],
        cost_estimate=pl.CostEstimate(flops=0, bytes_accessed=6 << 20, transcendentals=0),
        compiler_params=pltpu.CompilerParams(vmem_limit_bytes=8 << 20),
        name="pack",
    )(here, dest, *in_vmem(params_wide, blocks))


def turned(rows):
    size = rows.shape[1]
    return jnp.transpose(jnp.concatenate([rows, jnp.zeros((size - rows.shape[0], size), rows.dtype)]))


def maps_kernel(column_ref, got_ref, maps_ref, tall, side):
    tile_cols = got_ref.shape[2]
    tile_rows = (got_ref.shape[1] - ROWS) // 2
    pixels = ROWS * tile_rows
    column = column_ref[0]
    lane = lax.broadcasted_iota(jnp.int32, (tile_rows, tile_cols), 1)

    def finish(part, p, q, albedo):
        maps_ref[0, part, :] = p
        maps_ref[1, part, :] = q
        maps_ref[2, part, :] = 1.0 / jnp.sqrt(1.0 + p * p + q * q)
        maps_ref[3, part, :] = albedo

    for row in range(ROWS):
        tall[8 + row * tile_rows : 8 + (row + 1) * tile_rows, :] = got_ref[row, :tile_rows, :]
    tall[7:8, :] = got_ref[0, 0:1, :]
    tall[8 + pixels : 9 + pixels, :] = got_ref[ROWS - 1, tile_rows - 1 : tile_rows, :]
    beside, beyond, shade, mine = [
        jnp.concatenate([got_ref[row, 2 * tile_rows + k : 2 * tile_rows + k + 1, :] for row in range(ROWS)]) for k in range(4)
    ]
    side[...] = turned(beside)
    for row in range(ROWS):
        start = 8 + row * tile_rows
        height = tall[start : start + tile_rows, :]
        west = pltpu.roll(side[:tile_rows, :], (tile_cols - row) % tile_cols, 1)
        east = pltpu.roll(side[tile_rows:, :], tile_cols - 1 - row, 1)
        before = jnp.where(lane == 0, jnp.where(column == 0, height, west), pltpu.roll(height, 1, 1))
        after = jnp.where(
            lane == tile_cols - 1,
            jnp.where(column == CLASSES * CORES - 1, height, east),
            pltpu.roll(height, tile_cols - 1, 1),
        )
        p = (after - before) * 0.5
        q = (tall[start + 1 : start + 1 + tile_rows, :] - tall[start - 1 : start - 1 + tile_rows, :]) * 0.5
        finish(slice(row * tile_rows, (row + 1) * tile_rows), p, q, got_ref[row, tile_rows : 2 * tile_rows, :])

    lane = lax.broadcasted_iota(jnp.int32, (ROWS, tile_cols), 1)
    p = jnp.where(lane < tile_rows, mine - beyond, beyond - mine) * 0.5
    lower = jnp.concatenate([pltpu.roll(beside, tile_rows - 1, 1)[1:], beside[ROWS - 1 :]])
    upper = jnp.concatenate([beside[:1], pltpu.roll(beside, tile_cols - tile_rows + 1, 1)[:-1]])
    place = lane % tile_rows
    following = jnp.where(place == tile_rows - 1, lower, pltpu.roll(beside, tile_cols - 1, 1))
    preceding = jnp.where(place == 0, upper, pltpu.roll(beside, 1, 1))
    finish(slice(pixels, pixels + ROWS), p, (following - preceding) * 0.5, shade)


def make_maps(column, got):
    tile_cols = got.shape[2]
    pixels = ROWS * (got.shape[1] - ROWS) // 2
    return pl.pallas_call(
        maps_kernel,
        out_shape=pltpu.VMEM((4, pixels + ROWS, tile_cols), jnp.float32),
        in_specs=[SMEM, VMEM],
        out_specs=VMEM,
        scratch_shapes=[
            pltpu.VMEM((pixels + 16, tile_cols), jnp.float32),
            pltpu.VMEM((tile_cols, tile_cols), jnp.float32),
        ],
        cost_estimate=pl.CostEstimate(flops=0, bytes_accessed=3 << 20, transcendentals=0),
        compiler_params=pltpu.CompilerParams(vmem_limit_bytes=4 << 20),
        name="maps",
    )(column, *in_vmem(got))


def add_block(maps, totals, values, bright):
    pw, qw, w, albedo = maps
    sum_x, sum_y, sum_z, shade = totals
    sx, sy, sz, vx, vy, vz, mix, gain = values
    mix2 = mix * 2.0
    rest = 1.0 - mix
    bright = bright.astype(jnp.float32)
    ci = sz * w - sx * pw - sy * qw
    ce = vz * w - vx * pw - vy * qw
    square = ci * ci + SMOOTH
    inv_root = lax.rsqrt(square)
    mu = (ci + square * inv_root) * 0.5
    inv = 1.0 / (mu + ce)
    k = mix2 * inv
    u = mu * inv
    c = ce * inv
    shading = mu * (k + rest)
    misfit = (gain * albedo) * shading - bright
    scaled = gain * misfit
    shade = shade + scaled * shading
    gs = scaled * albedo
    gk = gs * k
    gl = gk * c + gs * rest
    gi = gl * (mu * inv_root)
    ge = gk * u
    return (
        sum_x + (gi * sx - ge * vx),
        sum_y + (gi * sy - ge * vy),
        sum_z + (gi * sz - ge * vz),
        shade,
    )


def terms_kernel(scale, with_sums, picks, *refs):
    column_ref, maps_ref, *refs = refs
    sums_ref = None
    if with_sums:
        sums_ref, *refs = refs
    got, refs = refs[: len(picks)], refs[len(picks) :]
    out_ref, lines, params, sem, *refs = refs
    units = [ref.at[pick] for ref, some in zip(got, picks) for pick in some]
    tile_cols = maps_ref.shape[2]
    pixels = maps_ref.shape[1] - ROWS
    tile_rows = pixels // ROWS
    for index, unit in enumerate(units):
        lines[index * ROWS : (index + 1) * ROWS, :] = unit[pixels + ROWS :, :].astype(jnp.float32)
    copy = pltpu.make_async_copy(lines, params, sem)
    copy.start()
    copy.wait()

    def run(part, size, values_of):
        p, q, w, albedo = (maps_ref[k, part, :] for k in range(4))
        if with_sums:
            totals = tuple(sums_ref[k, part, :] for k in range(4))
        else:
            totals = (jnp.zeros((size, tile_cols), jnp.float32),) * 4
        maps = (p * w, q * w, w, albedo)
        for number, unit in enumerate(units):
            totals = add_block(maps, totals, values_of(number), unit[part, :])
        if scale is None:
            for k, total in enumerate(totals):
                out_ref[k, part, :] = total
            return None
        sum_x, sum_y, sum_z, shade = totals
        up = (w * w * w) * (sum_z - p * sum_x - q * sum_y)
        half_x = (-(w * sum_x) - p * up) * (0.5 * scale)
        half_y = (-(w * sum_y) - q * up) * (0.5 * scale)
        return half_x, half_y, shade * scale

    def strip(index, carry):
        first = pl.multiple_of(index * STRIP, STRIP)
        row = index // (tile_rows // STRIP)
        result = run(pl.ds(first, STRIP), STRIP, lambda number: [params[number * ROWS + row, k] for k in range(PARAMS)])
        if result is not None:
            slope_x, slope_y, _ = refs
            slope_x[pl.ds(first, STRIP), :] = result[0]
            slope_y[pl.ds(pl.multiple_of(first + 8, 8), STRIP), :] = result[1]
            for half in range(STRIP // 8):
                out_ref[index * (STRIP // 8) + half, 8:16, :] = result[2][half * 8 : half * 8 + 8]
        return carry

    lax.fori_loop(0, pixels // STRIP, strip, 0)

    west_half = lax.broadcasted_iota(jnp.int32, (ROWS, tile_cols), 1) < tile_rows

    def side_values(number):
        rows = lines[number * ROWS : (number + 1) * ROWS, :]
        values = []
        for k in range(PARAMS):
            west, east = (
                jnp.broadcast_to(rows[:, n * PARAMS + k : n * PARAMS + k + 1], (ROWS, tile_cols)) for n in (1, 2)
            )
            values.append(jnp.where(west_half, west, east))
        return values

    result = run(slice(pixels, pixels + ROWS), ROWS, side_values)
    if result is None:
        return

    slope_x, slope_y, side = refs
    column = column_ref[0]
    side[...] = turned(result[0])
    slope_y[7:8, :] = -slope_y[8:9, :]
    slope_y[8 + pixels : 9 + pixels, :] = -slope_y[7 + pixels : 8 + pixels, :]
    lane = lax.broadcasted_iota(jnp.int32, (tile_rows, tile_cols), 1)
    for row in range(ROWS):
        start = row * tile_rows
        here = slope_x[start : start + tile_rows, :]
        west = pltpu.roll(side[:tile_rows, :], (tile_cols - row) % tile_cols, 1)
        east = pltpu.roll(side[tile_rows:, :], tile_cols - 1 - row, 1)
        before = jnp.where(lane == 0, jnp.where(column == 0, -here, west), pltpu.roll(here, 1, 1))
        after = jnp.where(
            lane == tile_cols - 1,
            jnp.where(column == CLASSES * CORES - 1, -here, east),
            pltpu.roll(here, tile_cols - 1, 1),
        )
        spread = before - after + slope_y[start + 7 : start + 7 + tile_rows, :] - slope_y[start + 9 : start + 9 + tile_rows, :]
        for group in range(tile_rows // 8):
            out_ref[row * (tile_rows // 8) + group, 0:8, :] = spread[group * 8 : group * 8 + 8]


def terms(column, maps, sums, got, scale):
    arrays, picks = zip(*got)
    count = sum(len(some) for some in picks)
    given = [maps] + ([] if sums is None else [sums]) + list(arrays)
    rows, cols = maps.shape[1:]
    scratch = [
        pltpu.VMEM((count * ROWS, cols), jnp.float32),
        pltpu.SMEM((count * ROWS, cols), jnp.float32),
        pltpu.SemaphoreType.DMA,
    ]
    if scale is None:
        out = (4, rows, cols)
    else:
        out = ((rows - ROWS) // 8, 16, cols)
        scratch += [pltpu.VMEM((rows - ROWS, cols), jnp.float32), pltpu.VMEM((rows - ROWS + 16, cols), jnp.float32)]
        scratch += [pltpu.VMEM((cols, cols), jnp.float32)]
    return pl.pallas_call(
        lambda *refs: terms_kernel(scale, sums is not None, picks, *refs),
        out_shape=pltpu.VMEM(out, jnp.float32),
        in_specs=[SMEM] + [VMEM] * len(given),
        out_specs=VMEM,
        scratch_shapes=scratch,
        cost_estimate=pl.CostEstimate(flops=60 * count * rows * cols, bytes_accessed=4 << 20, transcendentals=0),
        compiler_params=pltpu.CompilerParams(vmem_limit_bytes=4 << 20),
    )(column, *in_vmem(*given))


EACH2 = [(0,), (1,)]
EACH4 = EACH2 + [(2,), (3,)]


def body(heights, albedo, blocks, block_params, block_dest):
    column_here = lax.axis_index(("zl", "c"))
    tile_rows, tile_cols = heights.shape[1:]
    block_count = block_dest.shape[2]

    params_wide = jnp.pad(
        block_params.reshape(block_count, PARAMS).astype(jnp.float32), ((0, 0), (0, tile_cols - PARAMS))
    )
    here = jnp.stack([lax.axis_index("zl"), lax.axis_index("c")]).astype(jnp.int32)
    near, own, other = pack(
        here,
        block_dest.reshape(block_count),
        params_wide,
        blocks.reshape(block_count, tile_rows, tile_cols),
    )
    swapped = lax.ppermute(other, "c", [(0, 1), (1, 0)])
    to_right = jnp.concatenate([own[0], swapped[1]])
    to_left = jnp.concatenate([own[2], swapped[3]])
    to_right2 = jnp.stack([own[1, 0], swapped[2, 0]])
    to_left2 = jnp.stack([own[1, 1], swapped[2, 1]])
    right = ring_shift(to_right, 1)
    left = ring_shift(to_left, -1)
    right2 = ring_shift(to_right2, 2)
    left2 = ring_shift(to_left2, -2)

    height, shade = heights[0], albedo[0]
    first, last = jnp.stack([height[:, 0], height[:, 1], shade[:, 0]]), jnp.stack([height[:, -1], height[:, -2], shade[:, -1]])
    from_west = column_shift(last, 1)
    from_east = column_shift(first, -1)
    beside = jnp.concatenate([from_west, from_east], axis=1)
    mine = jnp.concatenate([first[:1], last[:1]], axis=1)
    rows = jnp.concatenate([beside, mine, jnp.zeros((ROWS - 4, tile_cols), jnp.float32)])
    copies = jnp.broadcast_to(jnp.concatenate([height, shade, rows])[None], (ROWS, 2 * tile_rows + ROWS, tile_cols))
    gathered = lax.all_to_all(copies, "y", split_axis=0, concat_axis=0, tiled=True)
    column = column_here.reshape(1).astype(jnp.int32)
    maps = make_maps(column, gathered)

    sums = terms(column, maps, None, [(near, [(0,), (1,)]), (swapped, [(0, 0), (0, 1)])], None)
    sums = terms(column, maps, sums, [(right, EACH4), (left, EACH4)], None)
    parts = terms(column, maps, sums, [(right2, EACH2), (left2, EACH2)], 1.0 / block_count)
    summed = jnp.sum(lax.all_to_all(parts, ("y",) + IMG, split_axis=0, concat_axis=0, tiled=True), axis=0)
    half = tile_rows // (HALVES * DEPTH)
    return (summed[None, :half], summed[None, half:])


def solution(mesh):
    physical = Mesh(mesh.devices.reshape(ROWS, CLASSES, CORES, HALVES, DEPTH), TILE + IMG)
    placed = (
        P(TILE, None, None),
        P(TILE, None, None),
        P(TILE, IMG, None, None, None),
        P(TILE, IMG, None, None),
        P(TILE, IMG, None, None),
    )

    return jax.shard_map(
        body,
        mesh=physical,
        in_specs=placed,
        out_specs=(P(TILE, IMG, None), P(TILE, IMG, None)),
        check_vma=False,
    )
```

```python
import jax
import jax.numpy as jnp
from jax import lax
from jax.experimental import pallas as pl
from jax.experimental.pallas import tpu as pltpu
from jax.sharding import Mesh
from jax.sharding import PartitionSpec as P


SMOOTH = 0.0025
PARAMS = 8
STRIP = 16
ROWS, CLASSES, CORES, HALVES, DEPTH = 8, 4, 2, 2, 4
RING = CLASSES * HALVES
TILE = ("y", "zl", "c")
IMG = ("zh", "x")

SMEM = pl.BlockSpec(memory_space=pltpu.SMEM)
VMEM = pl.BlockSpec(memory_space=pltpu.VMEM)


def ring_shift(value, steps):
    pairs = []
    for low in range(CLASSES):
        for core in range(CORES):
            for high in range(HALVES):
                z = (high * CLASSES + low + steps) % RING
                source = (low * CORES + core) * HALVES + high
                pairs.append((source, ((z % CLASSES) * CORES + core) * HALVES + z // CLASSES))
    return lax.ppermute(value, ("zl", "c", "zh"), pairs)


def column_shift(value, steps):
    count = CLASSES * CORES
    pairs = [(k, k + steps) for k in range(count) if 0 <= k + steps < count]
    return lax.ppermute(value, ("zl", "c"), pairs)


def in_vmem(*arrays):
    return [pltpu.with_memory_space_constraint(a, pltpu.VMEM) for a in arrays]


def fill_table(dest_ref, table):
    def clear(index, carry):
        table[index] = -1
        return carry

    lax.fori_loop(0, table.shape[0], clear, 0, unroll=8)

    def note(index, carry):
        place = dest_ref[index] * 2
        second = (table[place] >= 0).astype(jnp.int32)
        table[place + second] = index
        return carry

    lax.fori_loop(0, dest_ref.shape[0], note, 0, unroll=4)


def pack_kernel(
    here_ref, dest_ref, params_ref, blocks_hbm, near_ref, right_ref, left_ref, right2_ref, left2_ref, other_ref,
    blocks_ref, sem, table, shifted, columns, rim, lines,
):
    number, tile_rows, tile_cols = blocks_ref.shape
    fetch = pltpu.make_async_copy(blocks_hbm, blocks_ref, sem)
    fetch.start()
    fill_table(dest_ref, table)
    upright = params_ref[...].astype(jnp.float32)
    upright = jnp.concatenate([upright, jnp.zeros((PARAMS, tile_cols - number), jnp.float32)], axis=1)
    plain = turned(upright)[:number]
    for k in range(3):
        shifted[k] = plain if k == 0 else pltpu.roll(plain, k * PARAMS, 1)
    fetch.wait()

    lane8 = lax.broadcasted_iota(jnp.int32, (8, tile_cols), 1)
    sub8 = lax.broadcasted_iota(jnp.int32, (8, tile_cols), 0)
    pick = jnp.where(((sub8 == 0) & (lane8 == tile_cols - 1)) | ((sub8 == 1) & (lane8 == 0)), 1.0, 0.0).astype(jnp.bfloat16)
    flat = lax.dot_general(
        pick,
        blocks_ref[...].reshape(number * tile_rows, tile_cols),
        (((1,), (1,)), ((), ())),
        preferred_element_type=jnp.float32,
    )
    pairs = number // 2
    for m in range(pairs):
        part = slice(m * tile_cols, (m + 1) * tile_cols)
        columns[0, m : m + 1, :] = flat[0:1, part]
        columns[1, m : m + 1, :] = flat[1:2, part]
    left_half = lax.broadcasted_iota(jnp.int32, (pairs, tile_cols), 1) < tile_rows
    last, first = columns[0], columns[1]
    rim[0] = jnp.where(left_half, last, pltpu.roll(first, tile_rows, 1))
    rim[1] = jnp.where(left_half, pltpu.roll(last, tile_rows, 1), first)

    low, core = here_ref[0], here_ref[1]
    count = CLASSES * CORES
    west_half = lax.broadcasted_iota(jnp.int32, (1, tile_cols), 1) < tile_rows
    pixels = ROWS * tile_rows
    mine = {
        0: (near_ref.at[0], near_ref.at[1]),
        1: (right_ref.at[0], right_ref.at[1]),
        2: (right2_ref.at[0], left2_ref.at[0]),
        3: (left_ref.at[0], left_ref.at[1]),
    }

    for kind in range(CORES):
        for d in range(CLASSES):
            column = ((low + d) % CLASSES) * CORES + (core + kind) % CORES
            units = (other_ref.at[d, 0], other_ref.at[d, 1]) if kind else mine[d]

            def place(step, carry):
                found = []
                for row in (step * 2, step * 2 + 1):
                    tile = row * count + column
                    for slot in (0, 1):
                        block = table[2 * tile + slot]
                        west = jnp.where(column > 0, table[jnp.maximum(2 * tile - 2, 0) + slot], -1)
                        east = jnp.where(column < count - 1, table[jnp.minimum(2 * tile + 2, 2 * ROWS * count - 2) + slot], -1)
                        values = blocks_ref[jnp.maximum(block, 0)]
                        values = jnp.where(block >= 0, values, jnp.zeros_like(values))
                        sides = []
                        line = jnp.zeros((1, tile_cols), jnp.float32)
                        for k, index in enumerate((block, west, east)):
                            safe = jnp.maximum(index, 0)
                            line = line + jnp.where(index >= 0, shifted[k, pl.ds(safe, 1), :], 0.0)
                            if k:
                                sides.append(jnp.where(index >= 0, rim[safe % 2, pl.ds(safe // 2, 1), :], 0.0))
                        found.append((row, slot, values, jnp.where(west_half, sides[0], sides[1]), line))
                for row, slot, values, side, line in found:
                    start = pl.multiple_of(row * tile_rows, tile_rows)
                    units[slot][pl.ds(start, tile_rows), :] = values
                    lines[0, slot, pl.ds(row, 1), :] = side
                    lines[1, slot, pl.ds(row, 1), :] = line
                return carry

            lax.fori_loop(0, ROWS // 2, place, 0)
            for slot in (0, 1):
                for k in (0, 1):
                    units[slot][pixels + k * ROWS : pixels + (k + 1) * ROWS, :] = lines[k, slot].astype(jnp.bfloat16)


def pack(here, dest, params, blocks):
    number, tile_rows, tile_cols = blocks.shape
    unit = (ROWS * tile_rows + 2 * ROWS, tile_cols)
    return pl.pallas_call(
        pack_kernel,
        out_shape=[pltpu.VMEM(lead + unit, jnp.bfloat16) for lead in ((2,), (2,), (2,), (1,), (1,), (CLASSES, 2))],
        in_specs=[SMEM, SMEM, VMEM, pl.BlockSpec(memory_space=pltpu.HBM)],
        out_specs=[VMEM] * 6,
        scratch_shapes=[
            pltpu.VMEM(blocks.shape, jnp.bfloat16),
            pltpu.SemaphoreType.DMA,
            pltpu.SMEM((2 * ROWS * CLASSES * CORES,), jnp.int32),
            pltpu.VMEM((3, number, tile_cols), jnp.float32),
            pltpu.VMEM((2, number // 2, tile_cols), jnp.float32),
            pltpu.VMEM((2, number // 2, tile_cols), jnp.float32),
            pltpu.VMEM((2, 2, ROWS, tile_cols), jnp.float32),
        ],
        cost_estimate=pl.CostEstimate(flops=0, bytes_accessed=6 << 20, transcendentals=0),
        compiler_params=pltpu.CompilerParams(vmem_limit_bytes=8 << 20),
        name="pack",
    )(here, *[pltpu.with_memory_space_constraint(a, pltpu.HBM) for a in (dest, params, blocks)])


def join_kernel(swapped_ref, *refs):
    own, (right_ref, left_ref, right2_ref, left2_ref) = refs[:4], refs[4:]
    for half, some in zip((right_ref, left_ref, right2_ref, left2_ref), own):
        half[: some.shape[0]] = some[...]
    right_ref[2:4] = swapped_ref[1]
    left_ref[2:4] = swapped_ref[3]
    right2_ref[1] = swapped_ref[2, 0]
    left2_ref[1] = swapped_ref[2, 1]


def join(swapped, *own):
    return pl.pallas_call(
        join_kernel,
        out_shape=[pltpu.VMEM((2 * a.shape[0],) + a.shape[1:], a.dtype) for a in own],
        in_specs=[VMEM] * 5,
        out_specs=[VMEM] * 4,
        cost_estimate=pl.CostEstimate(flops=0, bytes_accessed=2 << 20, transcendentals=0),
        compiler_params=pltpu.CompilerParams(vmem_limit_bytes=4 << 20),
        name="join",
    )(*in_vmem(swapped, *own))


def turned(rows):
    size = rows.shape[1]
    return jnp.transpose(jnp.concatenate([rows, jnp.zeros((size - rows.shape[0], size), rows.dtype)]))


def maps_kernel(column_ref, got_ref, maps_ref, tall, side):
    tile_cols = got_ref.shape[2]
    tile_rows = (got_ref.shape[1] - ROWS) // 2
    pixels = ROWS * tile_rows
    column = column_ref[0]
    lane = lax.broadcasted_iota(jnp.int32, (tile_rows, tile_cols), 1)

    def finish(part, p, q, albedo):
        maps_ref[0, part, :] = p
        maps_ref[1, part, :] = q
        maps_ref[2, part, :] = 1.0 / jnp.sqrt(1.0 + p * p + q * q)
        maps_ref[3, part, :] = albedo

    for row in range(ROWS):
        tall[8 + row * tile_rows : 8 + (row + 1) * tile_rows, :] = got_ref[row, :tile_rows, :]
    tall[7:8, :] = got_ref[0, 0:1, :]
    tall[8 + pixels : 9 + pixels, :] = got_ref[ROWS - 1, tile_rows - 1 : tile_rows, :]
    beside, beyond, shade, mine = [
        jnp.concatenate([got_ref[row, 2 * tile_rows + k : 2 * tile_rows + k + 1, :] for row in range(ROWS)]) for k in range(4)
    ]
    side[...] = turned(beside)
    for row in range(ROWS):
        start = 8 + row * tile_rows
        height = tall[start : start + tile_rows, :]
        west = pltpu.roll(side[:tile_rows, :], (tile_cols - row) % tile_cols, 1)
        east = pltpu.roll(side[tile_rows:, :], tile_cols - 1 - row, 1)
        before = jnp.where(lane == 0, jnp.where(column == 0, height, west), pltpu.roll(height, 1, 1))
        after = jnp.where(
            lane == tile_cols - 1,
            jnp.where(column == CLASSES * CORES - 1, height, east),
            pltpu.roll(height, tile_cols - 1, 1),
        )
        p = (after - before) * 0.5
        q = (tall[start + 1 : start + 1 + tile_rows, :] - tall[start - 1 : start - 1 + tile_rows, :]) * 0.5
        finish(slice(row * tile_rows, (row + 1) * tile_rows), p, q, got_ref[row, tile_rows : 2 * tile_rows, :])

    lane = lax.broadcasted_iota(jnp.int32, (ROWS, tile_cols), 1)
    p = jnp.where(lane < tile_rows, mine - beyond, beyond - mine) * 0.5
    lower = jnp.concatenate([pltpu.roll(beside, tile_rows - 1, 1)[1:], beside[ROWS - 1 :]])
    upper = jnp.concatenate([beside[:1], pltpu.roll(beside, tile_cols - tile_rows + 1, 1)[:-1]])
    place = lane % tile_rows
    following = jnp.where(place == tile_rows - 1, lower, pltpu.roll(beside, tile_cols - 1, 1))
    preceding = jnp.where(place == 0, upper, pltpu.roll(beside, 1, 1))
    finish(slice(pixels, pixels + ROWS), p, (following - preceding) * 0.5, shade)


def make_maps(column, got):
    tile_cols = got.shape[2]
    pixels = ROWS * (got.shape[1] - ROWS) // 2
    return pl.pallas_call(
        maps_kernel,
        out_shape=pltpu.VMEM((4, pixels + ROWS, tile_cols), jnp.float32),
        in_specs=[SMEM, VMEM],
        out_specs=VMEM,
        scratch_shapes=[
            pltpu.VMEM((pixels + 16, tile_cols), jnp.float32),
            pltpu.VMEM((tile_cols, tile_cols), jnp.float32),
        ],
        cost_estimate=pl.CostEstimate(flops=0, bytes_accessed=3 << 20, transcendentals=0),
        compiler_params=pltpu.CompilerParams(vmem_limit_bytes=4 << 20),
        name="maps",
    )(column, *in_vmem(got))


def add_block(maps, totals, values, bright):
    pw, qw, w, albedo = maps
    sum_x, sum_y, sum_z, shade = totals
    sx, sy, sz, vx, vy, vz, mix, gain = values
    mix2, rest = mix * 2.0, (1.0 - mix) * 0.5
    vx, vy, vz = vx * 2.0, vy * 2.0, vz * 2.0
    ci = sz * w - sx * pw - sy * qw
    ce = vz * w - vx * pw - vy * qw
    square = ci * ci + SMOOTH
    inv_root = lax.rsqrt(square)
    mu = ci + square * inv_root
    inv = 1.0 / (mu + ce)
    k = mix2 * inv
    shading = mu * (k + rest)
    weight = gain * albedo
    gs = weight * (weight * shading - bright.astype(jnp.float32))
    shade = shade + gs * shading
    gi = (gs * (k * (ce * inv) + rest)) * (mu * inv_root)
    ge = (gs * k) * (mu * inv)
    return (
        sum_x + (gi * sx - ge * vx),
        sum_y + (gi * sy - ge * vy),
        sum_z + (gi * sz - ge * vz),
        shade,
    )


def terms_kernel(scale, with_sums, picks, *refs):
    column_ref, maps_ref, *refs = refs
    sums_ref = None
    if with_sums:
        sums_ref, *refs = refs
    got, refs = refs[: len(picks)], refs[len(picks) :]
    out_ref, lines, params, sem, *refs = refs
    units = [ref.at[pick] for ref, some in zip(got, picks) for pick in some]
    tile_cols = maps_ref.shape[2]
    pixels = maps_ref.shape[1] - ROWS
    tile_rows = pixels // ROWS
    for index, unit in enumerate(units):
        lines[index * ROWS : (index + 1) * ROWS, :] = unit[pixels + ROWS :, :].astype(jnp.float32)
    copy = pltpu.make_async_copy(lines, params, sem)
    copy.start()
    copy.wait()

    def run(part, size, values_of):
        p, q, w, albedo = (maps_ref[k, part, :] for k in range(4))
        if with_sums:
            totals = tuple(sums_ref[k, part, :] for k in range(4))
        else:
            totals = (jnp.zeros((size, tile_cols), jnp.float32),) * 4
        maps = (p * w, q * w, w, albedo)
        for number, unit in enumerate(units):
            totals = add_block(maps, totals, values_of(number), unit[part, :])
        if scale is None:
            for k, total in enumerate(totals):
                out_ref[k, part, :] = total
            return None
        sum_x, sum_y, sum_z, shade = totals
        up = (w * w * w) * (sum_z - p * sum_x - q * sum_y)
        half_x = (-(w * sum_x) - p * up) * (0.5 * scale)
        half_y = (-(w * sum_y) - q * up) * (0.5 * scale)
        return half_x, half_y, shade * scale / albedo

    def strip(index, carry):
        first = pl.multiple_of(index * STRIP, STRIP)
        row = index // (tile_rows // STRIP)
        result = run(pl.ds(first, STRIP), STRIP, lambda number: [params[number * ROWS + row, k] for k in range(PARAMS)])
        if result is not None:
            slope_x, slope_y, _ = refs
            slope_x[pl.ds(first, STRIP), :] = result[0]
            slope_y[pl.ds(pl.multiple_of(first + 8, 8), STRIP), :] = result[1]
            for half in range(STRIP // 8):
                out_ref[index * (STRIP // 8) + half, 8:16, :] = result[2][half * 8 : half * 8 + 8]
        return carry

    lax.fori_loop(0, pixels // STRIP, strip, 0)

    west_half = lax.broadcasted_iota(jnp.int32, (ROWS, tile_cols), 1) < tile_rows

    def side_values(number):
        rows = lines[number * ROWS : (number + 1) * ROWS, :]
        values = []
        for k in range(PARAMS):
            west, east = (
                jnp.broadcast_to(rows[:, n * PARAMS + k : n * PARAMS + k + 1], (ROWS, tile_cols)) for n in (1, 2)
            )
            values.append(jnp.where(west_half, west, east))
        return values

    result = run(slice(pixels, pixels + ROWS), ROWS, side_values)
    if result is None:
        return

    slope_x, slope_y, side = refs
    column = column_ref[0]
    side[...] = turned(result[0])
    slope_y[7:8, :] = -slope_y[8:9, :]
    slope_y[8 + pixels : 9 + pixels, :] = -slope_y[7 + pixels : 8 + pixels, :]
    lane = lax.broadcasted_iota(jnp.int32, (tile_rows, tile_cols), 1)
    for row in range(ROWS):
        start = row * tile_rows
        here = slope_x[start : start + tile_rows, :]
        west = pltpu.roll(side[:tile_rows, :], (tile_cols - row) % tile_cols, 1)
        east = pltpu.roll(side[tile_rows:, :], tile_cols - 1 - row, 1)
        before = jnp.where(lane == 0, jnp.where(column == 0, -here, west), pltpu.roll(here, 1, 1))
        after = jnp.where(
            lane == tile_cols - 1,
            jnp.where(column == CLASSES * CORES - 1, -here, east),
            pltpu.roll(here, tile_cols - 1, 1),
        )
        spread = before - after + slope_y[start + 7 : start + 7 + tile_rows, :] - slope_y[start + 9 : start + 9 + tile_rows, :]
        for group in range(tile_rows // 8):
            out_ref[row * (tile_rows // 8) + group, 0:8, :] = spread[group * 8 : group * 8 + 8]


def terms(column, maps, sums, got, scale):
    arrays, picks = zip(*got)
    count = sum(len(some) for some in picks)
    given = [maps] + ([] if sums is None else [sums]) + list(arrays)
    rows, cols = maps.shape[1:]
    scratch = [
        pltpu.VMEM((count * ROWS, cols), jnp.float32),
        pltpu.SMEM((count * ROWS, cols), jnp.float32),
        pltpu.SemaphoreType.DMA,
    ]
    if scale is None:
        out = (4, rows, cols)
    else:
        out = ((rows - ROWS) // 8, 16, cols)
        scratch += [pltpu.VMEM((rows - ROWS, cols), jnp.float32), pltpu.VMEM((rows - ROWS + 16, cols), jnp.float32)]
        scratch += [pltpu.VMEM((cols, cols), jnp.float32)]
    return pl.pallas_call(
        lambda *refs: terms_kernel(scale, sums is not None, picks, *refs),
        out_shape=pltpu.VMEM(out, jnp.float32),
        in_specs=[SMEM] + [VMEM] * len(given),
        out_specs=VMEM,
        scratch_shapes=scratch,
        cost_estimate=pl.CostEstimate(flops=60 * count * rows * cols, bytes_accessed=4 << 20, transcendentals=0),
        compiler_params=pltpu.CompilerParams(vmem_limit_bytes=4 << 20),
    )(column, *in_vmem(*given))


EACH2 = [(0,), (1,)]
EACH4 = EACH2 + [(2,), (3,)]


def body(heights, albedo, blocks, block_params, block_dest):
    column_here = lax.axis_index(("zl", "c"))
    tile_rows, tile_cols = heights.shape[1:]
    block_count = block_dest.shape[2]

    here = jnp.stack([lax.axis_index("zl"), lax.axis_index("c")]).astype(jnp.int32)
    near, *own, other = pack(
        here,
        block_dest.reshape(block_count),
        block_params.reshape(block_count, PARAMS).T,
        blocks.reshape(block_count, tile_rows, tile_cols),
    )
    swapped = lax.ppermute(other, "c", [(0, 1), (1, 0)])
    to_right, to_left, to_right2, to_left2 = join(swapped, *own)
    right2 = ring_shift(to_right2, 2)
    left2 = ring_shift(to_left2, -2)
    right = ring_shift(to_right, 1)
    left = ring_shift(to_left, -1)

    height, shade = heights[0], albedo[0]
    first, last = jnp.stack([height[:, 0], height[:, 1], shade[:, 0]]), jnp.stack([height[:, -1], height[:, -2], shade[:, -1]])
    from_west = column_shift(last, 1)
    from_east = column_shift(first, -1)
    beside = jnp.concatenate([from_west, from_east], axis=1)
    mine = jnp.concatenate([first[:1], last[:1]], axis=1)
    rows = jnp.concatenate([beside, mine, jnp.zeros((ROWS - 4, tile_cols), jnp.float32)])
    copies = jnp.broadcast_to(jnp.concatenate([height, shade, rows])[None], (ROWS, 2 * tile_rows + ROWS, tile_cols))
    gathered = lax.all_to_all(copies, "y", split_axis=0, concat_axis=0, tiled=True)
    column = column_here.reshape(1).astype(jnp.int32)
    maps = make_maps(column, gathered)

    sums = terms(column, maps, None, [(near, [(0,), (1,)]), (swapped, [(0, 0), (0, 1)])], None)
    sums = terms(column, maps, sums, [(right2, EACH2), (left2, EACH2)], None)
    parts = terms(column, maps, sums, [(right, EACH4), (left, EACH4)], 1.0 / block_count)
    summed = jnp.sum(lax.all_to_all(parts, ("y",) + IMG, split_axis=0, concat_axis=0, tiled=True), axis=0)
    half = tile_rows // (HALVES * DEPTH)
    return (summed[None, :half], summed[None, half:])


def solution(mesh):
    physical = Mesh(mesh.devices.reshape(ROWS, CLASSES, CORES, HALVES, DEPTH), TILE + IMG)
    placed = (
        P(TILE, None, None),
        P(TILE, None, None),
        P(TILE, IMG, None, None, None),
        P(TILE, IMG, None, None),
        P(TILE, IMG, None, None),
    )

    return jax.shard_map(
        body,
        mesh=physical,
        in_specs=placed,
        out_specs=(P(TILE, IMG, None), P(TILE, IMG, None)),
        check_vma=False,
    )
```

```python
import jax
import jax.numpy as jnp
from jax import lax
from jax.experimental import pallas as pl
from jax.experimental.pallas import tpu as pltpu
from jax.sharding import Mesh
from jax.sharding import PartitionSpec as P


SMOOTH = 0.0025
PARAMS = 8
STRIP = 16
ROWS, CLASSES, CORES, HALVES, DEPTH = 8, 4, 2, 2, 4
RING = CLASSES * HALVES
TILE = ("y", "zl", "c")
IMG = ("zh", "x")

SMEM = pl.BlockSpec(memory_space=pltpu.SMEM)
VMEM = pl.BlockSpec(memory_space=pltpu.VMEM)


def ring_shift(value, steps):
    pairs = []
    for low in range(CLASSES):
        for core in range(CORES):
            for high in range(HALVES):
                z = (high * CLASSES + low + steps) % RING
                source = (low * CORES + core) * HALVES + high
                pairs.append((source, ((z % CLASSES) * CORES + core) * HALVES + z // CLASSES))
    return lax.ppermute(value, ("zl", "c", "zh"), pairs)


def column_shift(value, steps):
    count = CLASSES * CORES
    pairs = [(k, k + steps) for k in range(count) if 0 <= k + steps < count]
    return lax.ppermute(value, ("zl", "c"), pairs)


def in_vmem(*arrays):
    return [pltpu.with_memory_space_constraint(a, pltpu.VMEM) for a in arrays]


def fill_table(dest_ref, table):
    def clear(index, carry):
        table[index] = -1
        return carry

    lax.fori_loop(0, table.shape[0], clear, 0, unroll=8)

    def note(index, carry):
        place = dest_ref[index] * 2
        second = (table[place] >= 0).astype(jnp.int32)
        table[place + second] = index
        return carry

    lax.fori_loop(0, dest_ref.shape[0], note, 0, unroll=4)


def pack_kernel(
    here_ref, dest_ref, params_ref, height_ref, albedo_ref, blocks_hbm, near_ref, right_ref, left_ref, right2_ref, left2_ref, other_ref, copies_ref,
    blocks_ref, sem, table, shifted, columns, rim, lines,
):
    number, tile_rows, tile_cols = blocks_ref.shape
    fetch = pltpu.make_async_copy(blocks_hbm, blocks_ref, sem)
    fetch.start()
    fill_table(dest_ref, table)
    upright = params_ref[...].astype(jnp.float32)
    upright = jnp.concatenate([upright, jnp.zeros((PARAMS, tile_cols - number), jnp.float32)], axis=1)
    plain = turned(upright)[:number]
    for k in range(3):
        shifted[k] = plain if k == 0 else pltpu.roll(plain, k * PARAMS, 1)

    height, albedo = height_ref[...], albedo_ref[...]
    blank = jnp.zeros((tile_cols - tile_rows, tile_cols), jnp.float32)
    tall, shade = (jnp.transpose(jnp.concatenate([m, blank])) for m in (height, albedo))
    west_half = lax.broadcasted_iota(jnp.int32, (1, tile_cols), 1) < tile_rows
    ends = [
        jnp.where(west_half, m[a : a + 1], pltpu.roll(m[b : b + 1], tile_rows, 1))
        for m, a, b in ((tall, 0, tile_cols - 1), (tall, 1, tile_cols - 2), (shade, 0, tile_cols - 1))
    ]
    ends = jnp.concatenate(ends + [jnp.zeros((ROWS - 3, tile_cols), jnp.float32)])
    for row in range(ROWS):
        copies_ref[row, :tile_rows, :] = height
        copies_ref[row, tile_rows : 2 * tile_rows, :] = albedo
        copies_ref[row, 2 * tile_rows :, :] = ends
    fetch.wait()

    lane8 = lax.broadcasted_iota(jnp.int32, (8, tile_cols), 1)
    sub8 = lax.broadcasted_iota(jnp.int32, (8, tile_cols), 0)
    pick = jnp.where(((sub8 == 0) & (lane8 == tile_cols - 1)) | ((sub8 == 1) & (lane8 == 0)), 1.0, 0.0).astype(jnp.bfloat16)
    flat = lax.dot_general(
        pick,
        blocks_ref[...].reshape(number * tile_rows, tile_cols),
        (((1,), (1,)), ((), ())),
        preferred_element_type=jnp.float32,
    )
    pairs = number // 2
    for m in range(pairs):
        part = slice(m * tile_cols, (m + 1) * tile_cols)
        columns[0, m : m + 1, :] = flat[0:1, part]
        columns[1, m : m + 1, :] = flat[1:2, part]
    left_half = lax.broadcasted_iota(jnp.int32, (pairs, tile_cols), 1) < tile_rows
    last, first = columns[0], columns[1]
    rim[0] = jnp.where(left_half, last, pltpu.roll(first, tile_rows, 1))
    rim[1] = jnp.where(left_half, pltpu.roll(last, tile_rows, 1), first)

    low, core = here_ref[0], here_ref[1]
    count = CLASSES * CORES
    pixels = ROWS * tile_rows
    mine = {
        0: (near_ref.at[0], near_ref.at[1]),
        1: (right_ref.at[0], right_ref.at[1]),
        2: (right2_ref.at[0], left2_ref.at[0]),
        3: (left_ref.at[0], left_ref.at[1]),
    }

    for kind in range(CORES):
        for d in range(CLASSES):
            column = ((low + d) % CLASSES) * CORES + (core + kind) % CORES
            units = (other_ref.at[d, 0], other_ref.at[d, 1]) if kind else mine[d]

            def place(step, carry):
                found = []
                for row in (step * 2, step * 2 + 1):
                    tile = row * count + column
                    for slot in (0, 1):
                        block = table[2 * tile + slot]
                        west = jnp.where(column > 0, table[jnp.maximum(2 * tile - 2, 0) + slot], -1)
                        east = jnp.where(column < count - 1, table[jnp.minimum(2 * tile + 2, 2 * ROWS * count - 2) + slot], -1)
                        values = blocks_ref[jnp.maximum(block, 0)]
                        values = jnp.where(block >= 0, values, jnp.zeros_like(values))
                        sides = []
                        line = jnp.zeros((1, tile_cols), jnp.float32)
                        for k, index in enumerate((block, west, east)):
                            safe = jnp.maximum(index, 0)
                            line = line + jnp.where(index >= 0, shifted[k, pl.ds(safe, 1), :], 0.0)
                            if k:
                                sides.append(jnp.where(index >= 0, rim[safe % 2, pl.ds(safe // 2, 1), :], 0.0))
                        found.append((row, slot, values, jnp.where(west_half, sides[0], sides[1]), line))
                for row, slot, values, side, line in found:
                    start = pl.multiple_of(row * tile_rows, tile_rows)
                    units[slot][pl.ds(start, tile_rows), :] = values
                    lines[0, slot, pl.ds(row, 1), :] = side
                    lines[1, slot, pl.ds(row, 1), :] = line
                return carry

            lax.fori_loop(0, ROWS // 2, place, 0)
            for slot in (0, 1):
                for k in (0, 1):
                    units[slot][pixels + k * ROWS : pixels + (k + 1) * ROWS, :] = lines[k, slot].astype(jnp.bfloat16)


def pack(here, dest, params, height, albedo, blocks):
    number, tile_rows, tile_cols = blocks.shape
    unit = (ROWS * tile_rows + 2 * ROWS, tile_cols)
    return pl.pallas_call(
        pack_kernel,
        out_shape=[pltpu.VMEM(lead + unit, jnp.bfloat16) for lead in ((2,), (2,), (2,), (1,), (1,), (CLASSES, 2))]
        + [pltpu.VMEM((ROWS, 2 * tile_rows + ROWS, tile_cols), jnp.float32)],
        in_specs=[SMEM, SMEM, VMEM, VMEM, VMEM, pl.BlockSpec(memory_space=pltpu.HBM)],
        out_specs=[VMEM] * 7,
        scratch_shapes=[
            pltpu.VMEM(blocks.shape, jnp.bfloat16),
            pltpu.SemaphoreType.DMA,
            pltpu.SMEM((2 * ROWS * CLASSES * CORES,), jnp.int32),
            pltpu.VMEM((3, number, tile_cols), jnp.float32),
            pltpu.VMEM((2, number // 2, tile_cols), jnp.float32),
            pltpu.VMEM((2, number // 2, tile_cols), jnp.float32),
            pltpu.VMEM((2, 2, ROWS, tile_cols), jnp.float32),
        ],
        cost_estimate=pl.CostEstimate(flops=0, bytes_accessed=6 << 20, transcendentals=0),
        compiler_params=pltpu.CompilerParams(vmem_limit_bytes=8 << 20),
        name="pack",
    )(here, *[pltpu.with_memory_space_constraint(a, pltpu.HBM) for a in (dest, params, height, albedo, blocks)])


def join_kernel(swapped_ref, *refs):
    own, (right_ref, left_ref, right2_ref, left2_ref) = refs[:4], refs[4:]
    for half, some in zip((right_ref, left_ref, right2_ref, left2_ref), own):
        half[: some.shape[0]] = some[...]
    right_ref[2:4] = swapped_ref[1]
    left_ref[2:4] = swapped_ref[3]
    right2_ref[1] = swapped_ref[2, 0]
    left2_ref[1] = swapped_ref[2, 1]


def join(swapped, *own):
    return pl.pallas_call(
        join_kernel,
        out_shape=[pltpu.VMEM((2 * a.shape[0],) + a.shape[1:], a.dtype) for a in own],
        in_specs=[VMEM] * 5,
        out_specs=[VMEM] * 4,
        cost_estimate=pl.CostEstimate(flops=0, bytes_accessed=2 << 20, transcendentals=0),
        compiler_params=pltpu.CompilerParams(vmem_limit_bytes=4 << 20),
        name="join",
    )(*in_vmem(swapped, *own))


def turned(rows):
    size = rows.shape[1]
    return jnp.transpose(jnp.concatenate([rows, jnp.zeros((size - rows.shape[0], size), rows.dtype)]))


def maps_kernel(column_ref, got_ref, west_ref, east_ref, maps_ref, tall, side):
    tile_cols = got_ref.shape[2]
    tile_rows = (got_ref.shape[1] - ROWS) // 2
    pixels = ROWS * tile_rows
    column = column_ref[0]
    lane = lax.broadcasted_iota(jnp.int32, (tile_rows, tile_cols), 1)

    def finish(part, p, q, albedo):
        maps_ref[0, part, :] = p
        maps_ref[1, part, :] = q
        maps_ref[2, part, :] = 1.0 / jnp.sqrt(1.0 + p * p + q * q)
        maps_ref[3, part, :] = albedo

    for row in range(ROWS):
        tall[8 + row * tile_rows : 8 + (row + 1) * tile_rows, :] = got_ref[row, :tile_rows, :]
    tall[7:8, :] = got_ref[0, 0:1, :]
    tall[8 + pixels : 9 + pixels, :] = got_ref[ROWS - 1, tile_rows - 1 : tile_rows, :]
    left_half = lax.broadcasted_iota(jnp.int32, (ROWS, tile_cols), 1) < tile_rows
    beside, beyond, shade = [
        pltpu.roll(jnp.where(left_half, east_ref[k], west_ref[k]), tile_rows, 1) for k in range(3)
    ]
    mine = jnp.concatenate([got_ref[row, 2 * tile_rows : 2 * tile_rows + 1, :] for row in range(ROWS)])
    side[...] = turned(beside)
    for row in range(ROWS):
        start = 8 + row * tile_rows
        height = tall[start : start + tile_rows, :]
        west = pltpu.roll(side[:tile_rows, :], (tile_cols - row) % tile_cols, 1)
        east = pltpu.roll(side[tile_rows:, :], tile_cols - 1 - row, 1)
        before = jnp.where(lane == 0, jnp.where(column == 0, height, west), pltpu.roll(height, 1, 1))
        after = jnp.where(
            lane == tile_cols - 1,
            jnp.where(column == CLASSES * CORES - 1, height, east),
            pltpu.roll(height, tile_cols - 1, 1),
        )
        p = (after - before) * 0.5
        q = (tall[start + 1 : start + 1 + tile_rows, :] - tall[start - 1 : start - 1 + tile_rows, :]) * 0.5
        finish(slice(row * tile_rows, (row + 1) * tile_rows), p, q, got_ref[row, tile_rows : 2 * tile_rows, :])

    lane = lax.broadcasted_iota(jnp.int32, (ROWS, tile_cols), 1)
    p = jnp.where(lane < tile_rows, mine - beyond, beyond - mine) * 0.5
    lower = jnp.concatenate([pltpu.roll(beside, tile_rows - 1, 1)[1:], beside[ROWS - 1 :]])
    upper = jnp.concatenate([beside[:1], pltpu.roll(beside, tile_cols - tile_rows + 1, 1)[:-1]])
    place = lane % tile_rows
    following = jnp.where(place == tile_rows - 1, lower, pltpu.roll(beside, tile_cols - 1, 1))
    preceding = jnp.where(place == 0, upper, pltpu.roll(beside, 1, 1))
    finish(slice(pixels, pixels + ROWS), p, (following - preceding) * 0.5, shade)


def make_maps(column, got, from_west, from_east):
    tile_cols = got.shape[2]
    pixels = ROWS * (got.shape[1] - ROWS) // 2
    return pl.pallas_call(
        maps_kernel,
        out_shape=pltpu.VMEM((4, pixels + ROWS, tile_cols), jnp.float32),
        in_specs=[SMEM, VMEM, VMEM, VMEM],
        out_specs=VMEM,
        scratch_shapes=[
            pltpu.VMEM((pixels + 16, tile_cols), jnp.float32),
            pltpu.VMEM((tile_cols, tile_cols), jnp.float32),
        ],
        cost_estimate=pl.CostEstimate(flops=0, bytes_accessed=3 << 20, transcendentals=0),
        compiler_params=pltpu.CompilerParams(vmem_limit_bytes=4 << 20),
        name="maps",
    )(column, *in_vmem(got, from_west, from_east))


def add_block(maps, totals, values, bright):
    pw, qw, w, albedo = maps
    sum_x, sum_y, sum_z, shade = totals
    sx, sy, sz, vx, vy, vz, mix, gain = values
    mix2, rest = mix * 2.0, (1.0 - mix) * 0.5
    vx, vy, vz = vx * 2.0, vy * 2.0, vz * 2.0
    ci = sz * w - sx * pw - sy * qw
    ce = vz * w - vx * pw - vy * qw
    square = ci * ci + SMOOTH
    inv_root = lax.rsqrt(square)
    mu = ci + square * inv_root
    inv = 1.0 / (mu + ce)
    k = mix2 * inv
    shading = mu * (k + rest)
    weight = gain * albedo
    gs = weight * (weight * shading - bright.astype(jnp.float32))
    shade = shade + gs * shading
    gi = (gs * (k * (ce * inv) + rest)) * (mu * inv_root)
    ge = (gs * k) * (mu * inv)
    return (
        sum_x + (gi * sx - ge * vx),
        sum_y + (gi * sy - ge * vy),
        sum_z + (gi * sz - ge * vz),
        shade,
    )


def terms_kernel(scale, with_sums, picks, *refs):
    column_ref, maps_ref, *refs = refs
    sums_ref = None
    if with_sums:
        sums_ref, *refs = refs
    got, refs = refs[: len(picks)], refs[len(picks) :]
    out_ref, lines, params, sem, *refs = refs
    units = [ref.at[pick] for ref, some in zip(got, picks) for pick in some]
    tile_cols = maps_ref.shape[2]
    pixels = maps_ref.shape[1] - ROWS
    tile_rows = pixels // ROWS
    for index, unit in enumerate(units):
        lines[index * ROWS : (index + 1) * ROWS, :] = unit[pixels + ROWS :, :].astype(jnp.float32)
    copy = pltpu.make_async_copy(lines, params, sem)
    copy.start()
    copy.wait()

    def run(part, size, values_of):
        p, q, w, albedo = (maps_ref[k, part, :] for k in range(4))
        if with_sums:
            totals = tuple(sums_ref[k, part, :] for k in range(4))
        else:
            totals = (jnp.zeros((size, tile_cols), jnp.float32),) * 4
        maps = (p * w, q * w, w, albedo)
        for number, unit in enumerate(units):
            totals = add_block(maps, totals, values_of(number), unit[part, :])
        if scale is None:
            for k, total in enumerate(totals):
                out_ref[k, part, :] = total
            return None
        sum_x, sum_y, sum_z, shade = totals
        up = (w * w * w) * (sum_z - p * sum_x - q * sum_y)
        half_x = (-(w * sum_x) - p * up) * (0.5 * scale)
        half_y = (-(w * sum_y) - q * up) * (0.5 * scale)
        return half_x, half_y, shade * scale / albedo

    def strip(index, carry):
        first = pl.multiple_of(index * STRIP, STRIP)
        row = index // (tile_rows // STRIP)
        result = run(pl.ds(first, STRIP), STRIP, lambda number: [params[number * ROWS + row, k] for k in range(PARAMS)])
        if result is not None:
            slope_x, slope_y, _ = refs
            slope_x[pl.ds(first, STRIP), :] = result[0]
            slope_y[pl.ds(pl.multiple_of(first + 8, 8), STRIP), :] = result[1]
            for half in range(STRIP // 8):
                out_ref[index * (STRIP // 8) + half, 8:16, :] = result[2][half * 8 : half * 8 + 8]
        return carry

    lax.fori_loop(0, pixels // STRIP, strip, 0)

    west_half = lax.broadcasted_iota(jnp.int32, (ROWS, tile_cols), 1) < tile_rows

    def side_values(number):
        rows = lines[number * ROWS : (number + 1) * ROWS, :]
        values = []
        for k in range(PARAMS):
            west, east = (
                jnp.broadcast_to(rows[:, n * PARAMS + k : n * PARAMS + k + 1], (ROWS, tile_cols)) for n in (1, 2)
            )
            values.append(jnp.where(west_half, west, east))
        return values

    result = run(slice(pixels, pixels + ROWS), ROWS, side_values)
    if result is None:
        return

    slope_x, slope_y, side = refs
    column = column_ref[0]
    side[...] = turned(result[0])
    slope_y[7:8, :] = -slope_y[8:9, :]
    slope_y[8 + pixels : 9 + pixels, :] = -slope_y[7 + pixels : 8 + pixels, :]
    lane = lax.broadcasted_iota(jnp.int32, (tile_rows, tile_cols), 1)
    for row in range(ROWS):
        start = row * tile_rows
        here = slope_x[start : start + tile_rows, :]
        west = pltpu.roll(side[:tile_rows, :], (tile_cols - row) % tile_cols, 1)
        east = pltpu.roll(side[tile_rows:, :], tile_cols - 1 - row, 1)
        before = jnp.where(lane == 0, jnp.where(column == 0, -here, west), pltpu.roll(here, 1, 1))
        after = jnp.where(
            lane == tile_cols - 1,
            jnp.where(column == CLASSES * CORES - 1, -here, east),
            pltpu.roll(here, tile_cols - 1, 1),
        )
        spread = before - after + slope_y[start + 7 : start + 7 + tile_rows, :] - slope_y[start + 9 : start + 9 + tile_rows, :]
        for group in range(tile_rows // 8):
            out_ref[row * (tile_rows // 8) + group, 0:8, :] = spread[group * 8 : group * 8 + 8]


def terms(column, maps, sums, got, scale):
    arrays, picks = zip(*got)
    count = sum(len(some) for some in picks)
    given = [maps] + ([] if sums is None else [sums]) + list(arrays)
    rows, cols = maps.shape[1:]
    scratch = [
        pltpu.VMEM((count * ROWS, cols), jnp.float32),
        pltpu.SMEM((count * ROWS, cols), jnp.float32),
        pltpu.SemaphoreType.DMA,
    ]
    if scale is None:
        out = (4, rows, cols)
    else:
        out = ((rows - ROWS) // 8, 16, cols)
        scratch += [pltpu.VMEM((rows - ROWS, cols), jnp.float32), pltpu.VMEM((rows - ROWS + 16, cols), jnp.float32)]
        scratch += [pltpu.VMEM((cols, cols), jnp.float32)]
    return pl.pallas_call(
        lambda *refs: terms_kernel(scale, sums is not None, picks, *refs),
        out_shape=pltpu.VMEM(out, jnp.float32),
        in_specs=[SMEM] + [VMEM] * len(given),
        out_specs=VMEM,
        scratch_shapes=scratch,
        cost_estimate=pl.CostEstimate(flops=60 * count * rows * cols, bytes_accessed=4 << 20, transcendentals=0),
        compiler_params=pltpu.CompilerParams(vmem_limit_bytes=4 << 20),
    )(column, *in_vmem(*given))


EACH2 = [(0,), (1,)]
EACH4 = EACH2 + [(2,), (3,)]


def body(heights, albedo, blocks, block_params, block_dest):
    column_here = lax.axis_index(("zl", "c"))
    tile_rows, tile_cols = heights.shape[1:]
    block_count = block_dest.shape[2]

    here = jnp.stack([lax.axis_index("zl"), lax.axis_index("c")]).astype(jnp.int32)
    near, *own, other, copies = pack(
        here,
        block_dest.reshape(block_count),
        block_params.reshape(block_count, PARAMS).T,
        heights[0],
        albedo[0],
        blocks.reshape(block_count, tile_rows, tile_cols),
    )
    swapped = lax.ppermute(other, "c", [(0, 1), (1, 0)])
    to_right, to_left, to_right2, to_left2 = join(swapped, *own)
    right2 = ring_shift(to_right2, 2)
    left2 = ring_shift(to_left2, -2)
    right = ring_shift(to_right, 1)
    left = ring_shift(to_left, -1)

    gathered = lax.all_to_all(copies, "y", split_axis=0, concat_axis=0, tiled=True)
    ends = gathered[:, 2 * tile_rows : 2 * tile_rows + 3].swapaxes(0, 1)
    from_west = column_shift(ends, 1)
    from_east = column_shift(ends, -1)
    column = column_here.reshape(1).astype(jnp.int32)
    maps = make_maps(column, gathered, from_west, from_east)

    sums = terms(column, maps, None, [(near, [(0,), (1,)]), (swapped, [(0, 0), (0, 1)])], None)
    sums = terms(column, maps, sums, [(right2, EACH2), (left2, EACH2)], None)
    sums = terms(column, maps, sums, [(right, EACH4)], None)
    parts = terms(column, maps, sums, [(left, EACH4)], 1.0 / block_count)
    summed = jnp.sum(lax.all_to_all(parts, ("y",) + IMG, split_axis=0, concat_axis=0, tiled=True), axis=0)
    half = tile_rows // (HALVES * DEPTH)
    return (summed[None, :half], summed[None, half:])


def solution(mesh):
    physical = Mesh(mesh.devices.reshape(ROWS, CLASSES, CORES, HALVES, DEPTH), TILE + IMG)
    placed = (
        P(TILE, None, None),
        P(TILE, None, None),
        P(TILE, IMG, None, None, None),
        P(TILE, IMG, None, None),
        P(TILE, IMG, None, None),
    )

    return jax.shard_map(
        body,
        mesh=physical,
        in_specs=placed,
        out_specs=(P(TILE, IMG, None), P(TILE, IMG, None)),
        check_vma=False,
    )
```

```python
import jax
import jax.numpy as jnp
from jax import lax
from jax.experimental import pallas as pl
from jax.experimental.pallas import tpu as pltpu
from jax.sharding import Mesh
from jax.sharding import PartitionSpec as P


SMOOTH = 0.0025
PARAMS = 8
STRIP = 16
ROWS, CLASSES, CORES, HALVES, DEPTH = 8, 4, 2, 2, 4
RING = CLASSES * HALVES
TILE = ("y", "zl", "c")
IMG = ("zh", "x")

SMEM = pl.BlockSpec(memory_space=pltpu.SMEM)
VMEM = pl.BlockSpec(memory_space=pltpu.VMEM)


def ring_shift(value, steps):
    pairs = []
    for low in range(CLASSES):
        for core in range(CORES):
            for high in range(HALVES):
                z = (high * CLASSES + low + steps * (1 - 2 * core)) % RING
                source = (low * CORES + core) * HALVES + high
                pairs.append((source, ((z % CLASSES) * CORES + core) * HALVES + z // CLASSES))
    return lax.ppermute(value, ("zl", "c", "zh"), pairs)


def column_shift(value, steps):
    count = CLASSES * CORES
    pairs = [(k, k + steps) for k in range(count) if 0 <= k + steps < count]
    return lax.ppermute(value, ("zl", "c"), pairs)


def in_vmem(*arrays):
    return [pltpu.with_memory_space_constraint(a, pltpu.VMEM) for a in arrays]


def fill_table(dest_ref, table):
    def clear(index, carry):
        table[index] = -1
        return carry

    lax.fori_loop(0, table.shape[0], clear, 0, unroll=8)

    def note(index, carry):
        place = dest_ref[index] * 2
        second = (table[place] >= 0).astype(jnp.int32)
        table[place + second] = index
        return carry

    lax.fori_loop(0, dest_ref.shape[0], note, 0, unroll=4)


def first_turn(core):
    return 1 + core * (CLASSES - 2)


def pack_kernel(
    here_ref, dest_ref, params_ref, blocks_hbm, near_ref, first_ref, second_ref, far_ref, other_ref,
    blocks_ref, sem, table, shifted, columns, rim, lines,
):
    number, tile_rows, tile_cols = blocks_ref.shape
    fetch = pltpu.make_async_copy(blocks_hbm, blocks_ref, sem)
    fetch.start()
    fill_table(dest_ref, table)
    upright = params_ref[...].astype(jnp.float32)
    upright = jnp.concatenate([upright, jnp.zeros((PARAMS, tile_cols - number), jnp.float32)], axis=1)
    plain = turned(upright)[:number]
    for k in range(3):
        shifted[k] = plain if k == 0 else pltpu.roll(plain, k * PARAMS, 1)

    fetch.wait()

    lane8 = lax.broadcasted_iota(jnp.int32, (8, tile_cols), 1)
    sub8 = lax.broadcasted_iota(jnp.int32, (8, tile_cols), 0)
    pick = jnp.where(((sub8 == 0) & (lane8 == tile_cols - 1)) | ((sub8 == 1) & (lane8 == 0)), 1.0, 0.0).astype(jnp.bfloat16)
    flat = lax.dot_general(
        pick,
        blocks_ref[...].reshape(number * tile_rows, tile_cols),
        (((1,), (1,)), ((), ())),
        preferred_element_type=jnp.float32,
    )
    pairs = number // 2
    for m in range(pairs):
        part = slice(m * tile_cols, (m + 1) * tile_cols)
        columns[0, m : m + 1, :] = flat[0:1, part]
        columns[1, m : m + 1, :] = flat[1:2, part]
    left_half = lax.broadcasted_iota(jnp.int32, (pairs, tile_cols), 1) < tile_rows
    last, first = columns[0], columns[1]
    rim[0] = jnp.where(left_half, last, pltpu.roll(first, tile_rows, 1))
    rim[1] = jnp.where(left_half, pltpu.roll(last, tile_rows, 1), first)

    low, core = here_ref[0], here_ref[1]
    count = CLASSES * CORES
    west_half = lax.broadcasted_iota(jnp.int32, (1, tile_cols), 1) < tile_rows
    pixels = ROWS * tile_rows
    turn = first_turn(core)
    mine = [
        (0, near_ref.at[0], near_ref.at[1]),
        (turn, first_ref.at[0], first_ref.at[1]),
        (CLASSES // 2, far_ref.at[core], far_ref.at[1 - core]),
        (CLASSES - turn, second_ref.at[0], second_ref.at[1]),
    ]

    for kind in range(CORES):
        for d in range(CLASSES):
            step, *units = (d, other_ref.at[d, 0], other_ref.at[d, 1]) if kind else mine[d]
            column = ((low + step) % CLASSES) * CORES + (core + kind) % CORES

            def place(step, carry):
                found = []
                for row in (step * 2, step * 2 + 1):
                    tile = row * count + column
                    for slot in (0, 1):
                        block = table[2 * tile + slot]
                        west = jnp.where(column > 0, table[jnp.maximum(2 * tile - 2, 0) + slot], -1)
                        east = jnp.where(column < count - 1, table[jnp.minimum(2 * tile + 2, 2 * ROWS * count - 2) + slot], -1)
                        values = blocks_ref[jnp.maximum(block, 0)]
                        values = jnp.where(block >= 0, values, jnp.zeros_like(values))
                        sides = []
                        line = jnp.zeros((1, tile_cols), jnp.float32)
                        for k, index in enumerate((block, west, east)):
                            safe = jnp.maximum(index, 0)
                            line = line + jnp.where(index >= 0, shifted[k, pl.ds(safe, 1), :], 0.0)
                            if k:
                                sides.append(jnp.where(index >= 0, rim[safe % 2, pl.ds(safe // 2, 1), :], 0.0))
                        found.append((row, slot, values, jnp.where(west_half, sides[0], sides[1]), line))
                for row, slot, values, side, line in found:
                    start = pl.multiple_of(row * tile_rows, tile_rows)
                    units[slot][pl.ds(start, tile_rows), :] = values
                    lines[0, slot, pl.ds(row, 1), :] = side
                    lines[1, slot, pl.ds(row, 1), :] = line
                return carry

            lax.fori_loop(0, ROWS // 2, place, 0)
            for slot in (0, 1):
                for k in (0, 1):
                    units[slot][pixels + k * ROWS : pixels + (k + 1) * ROWS, :] = lines[k, slot].astype(jnp.bfloat16)


def pack(here, dest, params, blocks):
    number, tile_rows, tile_cols = blocks.shape
    unit = (ROWS * tile_rows + 2 * ROWS, tile_cols)
    return pl.pallas_call(
        pack_kernel,
        out_shape=[pltpu.VMEM(lead + unit, jnp.bfloat16) for lead in ((2,), (2,), (2,), (2,), (CLASSES, 2))],
        in_specs=[SMEM, SMEM, VMEM, pl.BlockSpec(memory_space=pltpu.HBM)],
        out_specs=[VMEM] * 5,
        scratch_shapes=[
            pltpu.VMEM(blocks.shape, jnp.bfloat16),
            pltpu.SemaphoreType.DMA,
            pltpu.SMEM((2 * ROWS * CLASSES * CORES,), jnp.int32),
            pltpu.VMEM((3, number, tile_cols), jnp.float32),
            pltpu.VMEM((2, number // 2, tile_cols), jnp.float32),
            pltpu.VMEM((2, number // 2, tile_cols), jnp.float32),
            pltpu.VMEM((2, 2, ROWS, tile_cols), jnp.float32),
        ],
        cost_estimate=pl.CostEstimate(flops=0, bytes_accessed=6 << 20, transcendentals=0),
        compiler_params=pltpu.CompilerParams(vmem_limit_bytes=8 << 20),
        name="pack",
    )(here, *[pltpu.with_memory_space_constraint(a, pltpu.HBM) for a in (dest, params, blocks)])


def join_kernel(here_ref, swapped_ref, first_own, second_own, far_own, first_ref, second_ref, far0_ref, far1_ref):
    core = here_ref[1]
    turn = first_turn(core)
    first_ref[0:2] = first_own[...]
    first_ref[2:4] = swapped_ref[turn]
    second_ref[0:2] = second_own[...]
    second_ref[2:4] = swapped_ref[CLASSES - turn]
    far0_ref[0] = far_own[0]
    far0_ref[1] = swapped_ref[CLASSES // 2, core]
    far1_ref[0] = far_own[1]
    far1_ref[1] = swapped_ref[CLASSES // 2, 1 - core]


def join(here, swapped, *own):
    unit = swapped.shape[2:]
    return pl.pallas_call(
        join_kernel,
        out_shape=[pltpu.VMEM((n,) + unit, swapped.dtype) for n in (4, 4, 2, 2)],
        in_specs=[SMEM] + [VMEM] * 4,
        out_specs=[VMEM] * 4,
        cost_estimate=pl.CostEstimate(flops=0, bytes_accessed=2 << 20, transcendentals=0),
        compiler_params=pltpu.CompilerParams(vmem_limit_bytes=4 << 20),
        name="join",
    )(here, *in_vmem(swapped, *own))


def copies_kernel(height_ref, albedo_ref, rows_ref, out_ref):
    tile_rows = height_ref.shape[0]
    for row in range(ROWS):
        out_ref[row, :tile_rows, :] = height_ref[...]
        out_ref[row, tile_rows : 2 * tile_rows, :] = albedo_ref[...]
        out_ref[row, 2 * tile_rows :, :] = rows_ref[...]


def make_copies(height, albedo, rows):
    return pl.pallas_call(
        copies_kernel,
        out_shape=pltpu.VMEM((ROWS, 2 * height.shape[0] + ROWS, height.shape[1]), jnp.float32),
        in_specs=[VMEM] * 3,
        out_specs=VMEM,
        cost_estimate=pl.CostEstimate(flops=0, bytes_accessed=1 << 20, transcendentals=0),
        compiler_params=pltpu.CompilerParams(vmem_limit_bytes=4 << 20),
        name="copies",
    )(*in_vmem(height, albedo, rows))


def turned(rows):
    size = rows.shape[1]
    return jnp.transpose(jnp.concatenate([rows, jnp.zeros((size - rows.shape[0], size), rows.dtype)]))


def maps_kernel(column_ref, got_ref, maps_ref, tall, side):
    tile_cols = got_ref.shape[2]
    tile_rows = (got_ref.shape[1] - ROWS) // 2
    pixels = ROWS * tile_rows
    column = column_ref[0]
    lane = lax.broadcasted_iota(jnp.int32, (tile_rows, tile_cols), 1)

    def finish(part, p, q, albedo):
        maps_ref[0, part, :] = p
        maps_ref[1, part, :] = q
        maps_ref[2, part, :] = 1.0 / jnp.sqrt(1.0 + p * p + q * q)
        maps_ref[3, part, :] = albedo

    for row in range(ROWS):
        tall[8 + row * tile_rows : 8 + (row + 1) * tile_rows, :] = got_ref[row, :tile_rows, :]
    tall[7:8, :] = got_ref[0, 0:1, :]
    tall[8 + pixels : 9 + pixels, :] = got_ref[ROWS - 1, tile_rows - 1 : tile_rows, :]
    beside, beyond, shade, mine = [
        jnp.concatenate([got_ref[row, 2 * tile_rows + k : 2 * tile_rows + k + 1, :] for row in range(ROWS)]) for k in range(4)
    ]
    side[...] = turned(beside)
    for row in range(ROWS):
        start = 8 + row * tile_rows
        height = tall[start : start + tile_rows, :]
        west = pltpu.roll(side[:tile_rows, :], (tile_cols - row) % tile_cols, 1)
        east = pltpu.roll(side[tile_rows:, :], tile_cols - 1 - row, 1)
        before = jnp.where(lane == 0, jnp.where(column == 0, height, west), pltpu.roll(height, 1, 1))
        after = jnp.where(
            lane == tile_cols - 1,
            jnp.where(column == CLASSES * CORES - 1, height, east),
            pltpu.roll(height, tile_cols - 1, 1),
        )
        p = (after - before) * 0.5
        q = (tall[start + 1 : start + 1 + tile_rows, :] - tall[start - 1 : start - 1 + tile_rows, :]) * 0.5
        finish(slice(row * tile_rows, (row + 1) * tile_rows), p, q, got_ref[row, tile_rows : 2 * tile_rows, :])

    lane = lax.broadcasted_iota(jnp.int32, (ROWS, tile_cols), 1)
    p = jnp.where(lane < tile_rows, mine - beyond, beyond - mine) * 0.5
    lower = jnp.concatenate([pltpu.roll(beside, tile_rows - 1, 1)[1:], beside[ROWS - 1 :]])
    upper = jnp.concatenate([beside[:1], pltpu.roll(beside, tile_cols - tile_rows + 1, 1)[:-1]])
    place = lane % tile_rows
    following = jnp.where(place == tile_rows - 1, lower, pltpu.roll(beside, tile_cols - 1, 1))
    preceding = jnp.where(place == 0, upper, pltpu.roll(beside, 1, 1))
    finish(slice(pixels, pixels + ROWS), p, (following - preceding) * 0.5, shade)


def make_maps(column, got):
    tile_cols = got.shape[2]
    pixels = ROWS * (got.shape[1] - ROWS) // 2
    return pl.pallas_call(
        maps_kernel,
        out_shape=pltpu.VMEM((4, pixels + ROWS, tile_cols), jnp.float32),
        in_specs=[SMEM, VMEM],
        out_specs=VMEM,
        scratch_shapes=[
            pltpu.VMEM((pixels + 16, tile_cols), jnp.float32),
            pltpu.VMEM((tile_cols, tile_cols), jnp.float32),
        ],
        cost_estimate=pl.CostEstimate(flops=0, bytes_accessed=3 << 20, transcendentals=0),
        compiler_params=pltpu.CompilerParams(vmem_limit_bytes=4 << 20),
        name="maps",
    )(column, *in_vmem(got))


def add_block(maps, totals, values, bright):
    pw, qw, w, albedo = maps
    sum_x, sum_y, sum_z, shade = totals
    sx, sy, sz, vx, vy, vz, mix, gain = values
    mix2, rest = mix * 2.0, (1.0 - mix) * 0.5
    vx, vy, vz = vx * 2.0, vy * 2.0, vz * 2.0
    ci = sz * w - sx * pw - sy * qw
    ce = vz * w - vx * pw - vy * qw
    square = ci * ci + SMOOTH
    inv_root = lax.rsqrt(square)
    mu = ci + square * inv_root
    inv = 1.0 / (mu + ce)
    k = mix2 * inv
    shading = mu * (k + rest)
    weight = gain * albedo
    gs = weight * (weight * shading - bright.astype(jnp.float32))
    shade = shade + gs * shading
    gi = (gs * (k * (ce * inv) + rest)) * (mu * inv_root)
    ge = (gs * k) * (mu * inv)
    return (
        sum_x + (gi * sx - ge * vx),
        sum_y + (gi * sy - ge * vy),
        sum_z + (gi * sz - ge * vz),
        shade,
    )


def terms_kernel(scale, with_sums, picks, *refs):
    column_ref, maps_ref, *refs = refs
    sums_ref = None
    if with_sums:
        sums_ref, *refs = refs
    got, refs = refs[: len(picks)], refs[len(picks) :]
    out_ref, lines, params, sem, *refs = refs
    units = [ref.at[pick] for ref, some in zip(got, picks) for pick in some]
    tile_cols = maps_ref.shape[2]
    pixels = maps_ref.shape[1] - ROWS
    tile_rows = pixels // ROWS
    for index, unit in enumerate(units):
        lines[index * ROWS : (index + 1) * ROWS, :] = unit[pixels + ROWS :, :].astype(jnp.float32)
    copy = pltpu.make_async_copy(lines, params, sem)
    copy.start()
    copy.wait()

    def run(part, size, values_of):
        p, q, w, albedo = (maps_ref[k, part, :] for k in range(4))
        if with_sums:
            totals = tuple(sums_ref[k, part, :] for k in range(4))
        else:
            totals = (jnp.zeros((size, tile_cols), jnp.float32),) * 4
        maps = (p * w, q * w, w, albedo)
        for number, unit in enumerate(units):
            totals = add_block(maps, totals, values_of(number), unit[part, :])
        if scale is None:
            for k, total in enumerate(totals):
                out_ref[k, part, :] = total
            return None
        sum_x, sum_y, sum_z, shade = totals
        up = (w * w * w) * (sum_z - p * sum_x - q * sum_y)
        half_x = (-(w * sum_x) - p * up) * (0.5 * scale)
        half_y = (-(w * sum_y) - q * up) * (0.5 * scale)
        return half_x, half_y, shade * scale / albedo

    def strip(index, carry):
        first = pl.multiple_of(index * STRIP, STRIP)
        row = index // (tile_rows // STRIP)
        result = run(pl.ds(first, STRIP), STRIP, lambda number: [params[number * ROWS + row, k] for k in range(PARAMS)])
        if result is not None:
            slope_x, slope_y, _ = refs
            slope_x[pl.ds(first, STRIP), :] = result[0]
            slope_y[pl.ds(pl.multiple_of(first + 8, 8), STRIP), :] = result[1]
            for half in range(STRIP // 8):
                out_ref[index * (STRIP // 8) + half, 8:16, :] = result[2][half * 8 : half * 8 + 8]
        return carry

    lax.fori_loop(0, pixels // STRIP, strip, 0)

    west_half = lax.broadcasted_iota(jnp.int32, (ROWS, tile_cols), 1) < tile_rows

    def side_values(number):
        rows = lines[number * ROWS : (number + 1) * ROWS, :]
        values = []
        for k in range(PARAMS):
            west, east = (
                jnp.broadcast_to(rows[:, n * PARAMS + k : n * PARAMS + k + 1], (ROWS, tile_cols)) for n in (1, 2)
            )
            values.append(jnp.where(west_half, west, east))
        return values

    result = run(slice(pixels, pixels + ROWS), ROWS, side_values)
    if result is None:
        return

    slope_x, slope_y, side = refs
    column = column_ref[0]
    side[...] = turned(result[0])
    slope_y[7:8, :] = -slope_y[8:9, :]
    slope_y[8 + pixels : 9 + pixels, :] = -slope_y[7 + pixels : 8 + pixels, :]
    lane = lax.broadcasted_iota(jnp.int32, (tile_rows, tile_cols), 1)
    for row in range(ROWS):
        start = row * tile_rows
        here = slope_x[start : start + tile_rows, :]
        west = pltpu.roll(side[:tile_rows, :], (tile_cols - row) % tile_cols, 1)
        east = pltpu.roll(side[tile_rows:, :], tile_cols - 1 - row, 1)
        before = jnp.where(lane == 0, jnp.where(column == 0, -here, west), pltpu.roll(here, 1, 1))
        after = jnp.where(
            lane == tile_cols - 1,
            jnp.where(column == CLASSES * CORES - 1, -here, east),
            pltpu.roll(here, tile_cols - 1, 1),
        )
        spread = before - after + slope_y[start + 7 : start + 7 + tile_rows, :] - slope_y[start + 9 : start + 9 + tile_rows, :]
        for group in range(tile_rows // 8):
            out_ref[row * (tile_rows // 8) + group, 0:8, :] = spread[group * 8 : group * 8 + 8]


def terms(column, maps, sums, got, scale):
    arrays, picks = zip(*got)
    count = sum(len(some) for some in picks)
    given = [maps] + ([] if sums is None else [sums]) + list(arrays)
    rows, cols = maps.shape[1:]
    scratch = [
        pltpu.VMEM((count * ROWS, cols), jnp.float32),
        pltpu.SMEM((count * ROWS, cols), jnp.float32),
        pltpu.SemaphoreType.DMA,
    ]
    if scale is None:
        out = (4, rows, cols)
    else:
        out = ((rows - ROWS) // 8, 16, cols)
        scratch += [pltpu.VMEM((rows - ROWS, cols), jnp.float32), pltpu.VMEM((rows - ROWS + 16, cols), jnp.float32)]
        scratch += [pltpu.VMEM((cols, cols), jnp.float32)]
    return pl.pallas_call(
        lambda *refs: terms_kernel(scale, sums is not None, picks, *refs),
        out_shape=pltpu.VMEM(out, jnp.float32),
        in_specs=[SMEM] + [VMEM] * len(given),
        out_specs=VMEM,
        scratch_shapes=scratch,
        cost_estimate=pl.CostEstimate(flops=60 * count * rows * cols, bytes_accessed=4 << 20, transcendentals=0),
        compiler_params=pltpu.CompilerParams(vmem_limit_bytes=4 << 20),
    )(column, *in_vmem(*given))


EACH2 = [(0,), (1,)]
EACH4 = EACH2 + [(2,), (3,)]


def body(heights, albedo, blocks, block_params, block_dest):
    column_here = lax.axis_index(("zl", "c"))
    tile_rows, tile_cols = heights.shape[1:]
    block_count = block_dest.shape[2]

    height, shade = heights[0], albedo[0]
    first, last = jnp.stack([height[:, 0], height[:, 1], shade[:, 0]]), jnp.stack([height[:, -1], height[:, -2], shade[:, -1]])
    from_west = column_shift(last, 1)
    from_east = column_shift(first, -1)

    here = jnp.stack([lax.axis_index("zl"), lax.axis_index("c")]).astype(jnp.int32)
    near, *own, other = pack(
        here,
        block_dest.reshape(block_count),
        block_params.reshape(block_count, PARAMS).T,
        blocks.reshape(block_count, tile_rows, tile_cols),
    )
    swapped = lax.ppermute(other, "c", [(0, 1), (1, 0)])
    to_first, to_second, to_far0, to_far1 = join(here, swapped, *own)
    far0 = ring_shift(to_far0, 2)
    far1 = ring_shift(to_far1, -2)
    next0 = ring_shift(to_first, 1)
    next1 = ring_shift(to_second, -1)

    beside = jnp.concatenate([from_west, from_east], axis=1)
    mine = jnp.concatenate([first[:1], last[:1]], axis=1)
    rows = jnp.concatenate([beside, mine, jnp.zeros((ROWS - 4, tile_cols), jnp.float32)])
    copies = make_copies(height, shade, rows)
    gathered = lax.all_to_all(copies, "y", split_axis=0, concat_axis=0, tiled=True)
    column = column_here.reshape(1).astype(jnp.int32)
    maps = make_maps(column, gathered)

    sums = terms(column, maps, None, [(near, [(0,), (1,)]), (swapped, [(0, 0), (0, 1)])], None)
    sums = terms(column, maps, sums, [(far0, EACH2), (far1, EACH2)], None)
    sums = terms(column, maps, sums, [(next0, EACH4)], None)
    parts = terms(column, maps, sums, [(next1, EACH4)], 1.0 / block_count)
    summed = jnp.sum(lax.all_to_all(parts, ("y",) + IMG, split_axis=0, concat_axis=0, tiled=True), axis=0)
    half = tile_rows // (HALVES * DEPTH)
    return (summed[None, :half], summed[None, half:])


def solution(mesh):
    physical = Mesh(mesh.devices.reshape(ROWS, CLASSES, CORES, HALVES, DEPTH), TILE + IMG)
    placed = (
        P(TILE, None, None),
        P(TILE, None, None),
        P(TILE, IMG, None, None, None),
        P(TILE, IMG, None, None),
        P(TILE, IMG, None, None),
    )

    return jax.shard_map(
        body,
        mesh=physical,
        in_specs=placed,
        out_specs=(P(TILE, IMG, None), P(TILE, IMG, None)),
        check_vma=False,
    )
```

```python
import jax
import jax.numpy as jnp
from jax import lax
from jax.experimental import pallas as pl
from jax.experimental.pallas import tpu as pltpu
from jax.sharding import Mesh
from jax.sharding import PartitionSpec as P


SMOOTH = 0.0025
PARAMS = 8
STRIP = 16
ROWS, CLASSES, CORES, HALVES, DEPTH = 8, 4, 2, 2, 4
RING = CLASSES * HALVES
TILE = ("y", "zl", "c")
IMG = ("zh", "x")

SMEM = pl.BlockSpec(memory_space=pltpu.SMEM)
VMEM = pl.BlockSpec(memory_space=pltpu.VMEM)


def ring_shift(value, steps):
    pairs = []
    for low in range(CLASSES):
        for core in range(CORES):
            for high in range(HALVES):
                z = (high * CLASSES + low + steps * (1 - 2 * core)) % RING
                source = (low * CORES + core) * HALVES + high
                pairs.append((source, ((z % CLASSES) * CORES + core) * HALVES + z // CLASSES))
    return lax.ppermute(value, ("zl", "c", "zh"), pairs)


def column_shift(value, steps):
    count = CLASSES * CORES
    pairs = [(k, k + steps) for k in range(count) if 0 <= k + steps < count]
    return lax.ppermute(value, ("zl", "c"), pairs)


def in_vmem(*arrays):
    return [pltpu.with_memory_space_constraint(a, pltpu.VMEM) for a in arrays]


def fill_table(dest_ref, table):
    number = dest_ref.shape[0]

    def clear(index, carry):
        table[index] = number
        return carry

    lax.fori_loop(0, table.shape[0], clear, 0, unroll=8)

    def note(index, carry):
        place = dest_ref[index] * 2
        second = (table[place] < number).astype(jnp.int32)
        table[place + second] = index
        return carry

    lax.fori_loop(0, number, note, 0, unroll=4)


def first_turn(core):
    return 1 + core * (CLASSES - 2)


def pack_kernel(
    here_ref, dest_ref, params_ref, blocks_hbm, near_ref, first_ref, second_ref, far_ref, other_ref,
    blocks_ref, sem, table, shifted, columns, rim, lines,
):
    number, tile_rows, tile_cols = blocks_hbm.shape
    fetch = pltpu.make_async_copy(blocks_hbm, blocks_ref.at[:number], sem)
    fetch.start()
    blocks_ref[number] = jnp.zeros((tile_rows, tile_cols), jnp.bfloat16)
    for part in range(3):
        shifted[part, number:, :] = jnp.zeros((8, tile_cols), jnp.float32)
    for part in range(2):
        rim[part, number // 2 :, :] = jnp.zeros((8, tile_cols), jnp.float32)
    fill_table(dest_ref, table)
    upright = params_ref[...].astype(jnp.float32)
    upright = jnp.concatenate([upright, jnp.zeros((PARAMS, tile_cols - number), jnp.float32)], axis=1)
    plain = turned(upright)[:number]
    for k in range(3):
        shifted[k, :number, :] = plain if k == 0 else pltpu.roll(plain, k * PARAMS, 1)

    fetch.wait()

    lane8 = lax.broadcasted_iota(jnp.int32, (8, tile_cols), 1)
    sub8 = lax.broadcasted_iota(jnp.int32, (8, tile_cols), 0)
    pick = jnp.where(((sub8 == 0) & (lane8 == tile_cols - 1)) | ((sub8 == 1) & (lane8 == 0)), 1.0, 0.0).astype(jnp.bfloat16)
    flat = lax.dot_general(
        pick,
        blocks_ref[:number].reshape(number * tile_rows, tile_cols),
        (((1,), (1,)), ((), ())),
        preferred_element_type=jnp.float32,
    )
    pairs = number // 2
    for m in range(pairs):
        part = slice(m * tile_cols, (m + 1) * tile_cols)
        columns[0, m : m + 1, :] = flat[0:1, part]
        columns[1, m : m + 1, :] = flat[1:2, part]
    left_half = lax.broadcasted_iota(jnp.int32, (pairs, tile_cols), 1) < tile_rows
    last, first = columns[0], columns[1]
    rim[0, :pairs, :] = jnp.where(left_half, last, pltpu.roll(first, tile_rows, 1))
    rim[1, :pairs, :] = jnp.where(left_half, pltpu.roll(last, tile_rows, 1), first)

    low, core = here_ref[0], here_ref[1]
    count = CLASSES * CORES
    west_half = lax.broadcasted_iota(jnp.int32, (1, tile_cols), 1) < tile_rows
    pixels = ROWS * tile_rows
    turn = first_turn(core)
    mine = [
        (0, near_ref.at[0], near_ref.at[1]),
        (turn, first_ref.at[0], first_ref.at[1]),
        (CLASSES // 2, far_ref.at[0], far_ref.at[1]),
        (CLASSES - turn, second_ref.at[0], second_ref.at[1]),
    ]

    for kind in range(CORES):
        for d in range(CLASSES):
            step, *units = (d, other_ref.at[d, 0], other_ref.at[d, 1]) if kind else mine[d]
            column = ((low + step) % CLASSES) * CORES + (core + kind) % CORES

            def place(step, carry):
                found = []
                for row in (step * 2, step * 2 + 1):
                    tile = row * count + column
                    for slot in (0, 1):
                        block = table[2 * tile + slot]
                        west = jnp.where(column > 0, table[jnp.maximum(2 * tile - 2, 0) + slot], number)
                        east = jnp.where(
                            column < count - 1, table[jnp.minimum(2 * tile + 2, 2 * ROWS * count - 2) + slot], number
                        )
                        line = shifted[0, pl.ds(block, 1), :] + shifted[1, pl.ds(west, 1), :] + shifted[2, pl.ds(east, 1), :]
                        sides = [rim[index % 2, pl.ds(index // 2, 1), :] for index in (west, east)]
                        found.append((row, slot, blocks_ref[block], jnp.where(west_half, sides[0], sides[1]), line))
                for row, slot, values, side, line in found:
                    start = pl.multiple_of(row * tile_rows, tile_rows)
                    units[slot][pl.ds(start, tile_rows), :] = values
                    lines[0, slot, pl.ds(row, 1), :] = side
                    lines[1, slot, pl.ds(row, 1), :] = line
                return carry

            lax.fori_loop(0, ROWS // 2, place, 0)
            for slot in (0, 1):
                for k in (0, 1):
                    units[slot][pixels + k * ROWS : pixels + (k + 1) * ROWS, :] = lines[k, slot].astype(jnp.bfloat16)


def pack(here, dest, params, blocks):
    number, tile_rows, tile_cols = blocks.shape
    unit = (ROWS * tile_rows + 2 * ROWS, tile_cols)
    return pl.pallas_call(
        pack_kernel,
        out_shape=[pltpu.VMEM(lead + unit, jnp.bfloat16) for lead in ((2,), (2,), (2,), (2,), (CLASSES, 2))],
        in_specs=[SMEM, SMEM, VMEM, pl.BlockSpec(memory_space=pltpu.HBM)],
        out_specs=[VMEM] * 5,
        scratch_shapes=[
            pltpu.VMEM((number + 1, tile_rows, tile_cols), jnp.bfloat16),
            pltpu.SemaphoreType.DMA,
            pltpu.SMEM((2 * ROWS * CLASSES * CORES,), jnp.int32),
            pltpu.VMEM((3, number + 8, tile_cols), jnp.float32),
            pltpu.VMEM((2, number // 2, tile_cols), jnp.float32),
            pltpu.VMEM((2, number // 2 + 8, tile_cols), jnp.float32),
            pltpu.VMEM((2, 2, ROWS, tile_cols), jnp.float32),
        ],
        cost_estimate=pl.CostEstimate(flops=0, bytes_accessed=6 << 20, transcendentals=0),
        compiler_params=pltpu.CompilerParams(vmem_limit_bytes=8 << 20),
        name="pack",
    )(here, *[pltpu.with_memory_space_constraint(a, pltpu.HBM) for a in (dest, params, blocks)])


def join_kernel(here_ref, swapped_ref, first_own, second_own, far_own, first_ref, second_ref, far_ref):
    core = here_ref[1]
    turn = first_turn(core)
    first_ref[0:2] = first_own[...]
    first_ref[2:4] = swapped_ref[turn]
    second_ref[0:2] = second_own[...]
    second_ref[2:4] = swapped_ref[CLASSES - turn]
    far_ref[0:2] = far_own[...]
    far_ref[2:4] = swapped_ref[CLASSES // 2]


def join(here, swapped, *own):
    unit = swapped.shape[2:]
    return pl.pallas_call(
        join_kernel,
        out_shape=[pltpu.VMEM((n,) + unit, swapped.dtype) for n in (4, 4, 4)],
        in_specs=[SMEM] + [VMEM] * 4,
        out_specs=[VMEM] * 3,
        cost_estimate=pl.CostEstimate(flops=0, bytes_accessed=2 << 20, transcendentals=0),
        compiler_params=pltpu.CompilerParams(vmem_limit_bytes=4 << 20),
        name="join",
    )(here, *in_vmem(swapped, *own))


def copies_kernel(height_ref, albedo_ref, rows_ref, out_ref):
    tile_rows = height_ref.shape[0]
    for row in range(ROWS):
        out_ref[row, :tile_rows, :] = height_ref[...]
        out_ref[row, tile_rows : 2 * tile_rows, :] = albedo_ref[...]
        out_ref[row, 2 * tile_rows :, :] = rows_ref[...]


def make_copies(height, albedo, rows):
    return pl.pallas_call(
        copies_kernel,
        out_shape=pltpu.VMEM((ROWS, 2 * height.shape[0] + ROWS, height.shape[1]), jnp.float32),
        in_specs=[VMEM] * 3,
        out_specs=VMEM,
        cost_estimate=pl.CostEstimate(flops=0, bytes_accessed=1 << 20, transcendentals=0),
        compiler_params=pltpu.CompilerParams(vmem_limit_bytes=4 << 20),
        name="copies",
    )(*in_vmem(height, albedo, rows))


def turned(rows):
    size = rows.shape[1]
    return jnp.transpose(jnp.concatenate([rows, jnp.zeros((size - rows.shape[0], size), rows.dtype)]))


def maps_kernel(column_ref, got_ref, maps_ref, tall, side):
    tile_cols = got_ref.shape[2]
    tile_rows = (got_ref.shape[1] - ROWS) // 2
    pixels = ROWS * tile_rows
    column = column_ref[0]
    lane = lax.broadcasted_iota(jnp.int32, (tile_rows, tile_cols), 1)

    def finish(part, p, q, albedo):
        maps_ref[0, part, :] = p
        maps_ref[1, part, :] = q
        maps_ref[2, part, :] = 1.0 / jnp.sqrt(1.0 + p * p + q * q)
        maps_ref[3, part, :] = albedo

    for row in range(ROWS):
        tall[8 + row * tile_rows : 8 + (row + 1) * tile_rows, :] = got_ref[row, :tile_rows, :]
    tall[7:8, :] = got_ref[0, 0:1, :]
    tall[8 + pixels : 9 + pixels, :] = got_ref[ROWS - 1, tile_rows - 1 : tile_rows, :]
    beside, beyond, shade, mine = [
        jnp.concatenate([got_ref[row, 2 * tile_rows + k : 2 * tile_rows + k + 1, :] for row in range(ROWS)]) for k in range(4)
    ]
    side[...] = turned(beside)
    for row in range(ROWS):
        start = 8 + row * tile_rows
        height = tall[start : start + tile_rows, :]
        west = pltpu.roll(side[:tile_rows, :], (tile_cols - row) % tile_cols, 1)
        east = pltpu.roll(side[tile_rows:, :], tile_cols - 1 - row, 1)
        before = jnp.where(lane == 0, jnp.where(column == 0, height, west), pltpu.roll(height, 1, 1))
        after = jnp.where(
            lane == tile_cols - 1,
            jnp.where(column == CLASSES * CORES - 1, height, east),
            pltpu.roll(height, tile_cols - 1, 1),
        )
        p = (after - before) * 0.5
        q = (tall[start + 1 : start + 1 + tile_rows, :] - tall[start - 1 : start - 1 + tile_rows, :]) * 0.5
        finish(slice(row * tile_rows, (row + 1) * tile_rows), p, q, got_ref[row, tile_rows : 2 * tile_rows, :])

    lane = lax.broadcasted_iota(jnp.int32, (ROWS, tile_cols), 1)
    p = jnp.where(lane < tile_rows, mine - beyond, beyond - mine) * 0.5
    lower = jnp.concatenate([pltpu.roll(beside, tile_rows - 1, 1)[1:], beside[ROWS - 1 :]])
    upper = jnp.concatenate([beside[:1], pltpu.roll(beside, tile_cols - tile_rows + 1, 1)[:-1]])
    place = lane % tile_rows
    following = jnp.where(place == tile_rows - 1, lower, pltpu.roll(beside, tile_cols - 1, 1))
    preceding = jnp.where(place == 0, upper, pltpu.roll(beside, 1, 1))
    finish(slice(pixels, pixels + ROWS), p, (following - preceding) * 0.5, shade)


def make_maps(column, got):
    tile_cols = got.shape[2]
    pixels = ROWS * (got.shape[1] - ROWS) // 2
    return pl.pallas_call(
        maps_kernel,
        out_shape=pltpu.VMEM((4, pixels + ROWS, tile_cols), jnp.float32),
        in_specs=[SMEM, VMEM],
        out_specs=VMEM,
        scratch_shapes=[
            pltpu.VMEM((pixels + 16, tile_cols), jnp.float32),
            pltpu.VMEM((tile_cols, tile_cols), jnp.float32),
        ],
        cost_estimate=pl.CostEstimate(flops=0, bytes_accessed=3 << 20, transcendentals=0),
        compiler_params=pltpu.CompilerParams(vmem_limit_bytes=4 << 20),
        name="maps",
    )(column, *in_vmem(got))


def add_block(maps, totals, values, bright):
    pw, qw, w, albedo = maps
    sum_x, sum_y, sum_z, shade = totals
    sx, sy, sz, vx, vy, vz, mix, gain = values
    mix2, rest = mix * 2.0, (1.0 - mix) * 0.5
    vx, vy, vz = vx * 2.0, vy * 2.0, vz * 2.0
    ci = sz * w - sx * pw - sy * qw
    ce = vz * w - vx * pw - vy * qw
    square = ci * ci + SMOOTH
    inv_root = lax.rsqrt(square)
    mu = ci + square * inv_root
    inv = 1.0 / (mu + ce)
    k = mix2 * inv
    shading = mu * (k + rest)
    weight = gain * albedo
    gs = weight * (weight * shading - bright.astype(jnp.float32))
    shade = shade + gs * shading
    gi = (gs * (k * (ce * inv) + rest)) * (mu * inv_root)
    ge = (gs * k) * (mu * inv)
    return (
        sum_x + (gi * sx - ge * vx),
        sum_y + (gi * sy - ge * vy),
        sum_z + (gi * sz - ge * vz),
        shade,
    )


def terms_kernel(scale, with_sums, picks, *refs):
    column_ref, maps_ref, *refs = refs
    sums_ref = None
    if with_sums:
        sums_ref, *refs = refs
    got, refs = refs[: len(picks)], refs[len(picks) :]
    out_ref, lines, params, sem, *refs = refs
    units = [ref.at[pick] for ref, some in zip(got, picks) for pick in some]
    tile_cols = maps_ref.shape[2]
    pixels = maps_ref.shape[1] - ROWS
    tile_rows = pixels // ROWS
    for index, unit in enumerate(units):
        lines[index * ROWS : (index + 1) * ROWS, :] = unit[pixels + ROWS :, :].astype(jnp.float32)
    copy = pltpu.make_async_copy(lines, params, sem)
    copy.start()
    copy.wait()

    def run(part, size, values_of):
        p, q, w, albedo = (maps_ref[k, part, :] for k in range(4))
        if with_sums:
            totals = tuple(sums_ref[k, part, :] for k in range(4))
        else:
            totals = (jnp.zeros((size, tile_cols), jnp.float32),) * 4
        maps = (p * w, q * w, w, albedo)
        for number, unit in enumerate(units):
            totals = add_block(maps, totals, values_of(number), unit[part, :])
        if scale is None:
            for k, total in enumerate(totals):
                out_ref[k, part, :] = total
            return None
        sum_x, sum_y, sum_z, shade = totals
        up = (w * w * w) * (sum_z - p * sum_x - q * sum_y)
        half_x = (-(w * sum_x) - p * up) * (0.5 * scale)
        half_y = (-(w * sum_y) - q * up) * (0.5 * scale)
        return half_x, half_y, shade * scale / albedo

    def strip(index, carry):
        first = pl.multiple_of(index * STRIP, STRIP)
        row = index // (tile_rows // STRIP)
        result = run(pl.ds(first, STRIP), STRIP, lambda number: [params[number * ROWS + row, k] for k in range(PARAMS)])
        if result is not None:
            slope_x, slope_y, _ = refs
            slope_x[pl.ds(first, STRIP), :] = result[0]
            slope_y[pl.ds(pl.multiple_of(first + 8, 8), STRIP), :] = result[1]
            for half in range(STRIP // 8):
                out_ref[index * (STRIP // 8) + half, 8:16, :] = result[2][half * 8 : half * 8 + 8]
        return carry

    lax.fori_loop(0, pixels // STRIP, strip, 0)

    west_half = lax.broadcasted_iota(jnp.int32, (ROWS, tile_cols), 1) < tile_rows

    def side_values(number):
        rows = lines[number * ROWS : (number + 1) * ROWS, :]
        values = []
        for k in range(PARAMS):
            west, east = (
                jnp.broadcast_to(rows[:, n * PARAMS + k : n * PARAMS + k + 1], (ROWS, tile_cols)) for n in (1, 2)
            )
            values.append(jnp.where(west_half, west, east))
        return values

    result = run(slice(pixels, pixels + ROWS), ROWS, side_values)
    if result is None:
        return

    slope_x, slope_y, side = refs
    column = column_ref[0]
    side[...] = turned(result[0])
    slope_y[7:8, :] = -slope_y[8:9, :]
    slope_y[8 + pixels : 9 + pixels, :] = -slope_y[7 + pixels : 8 + pixels, :]
    lane = lax.broadcasted_iota(jnp.int32, (tile_rows, tile_cols), 1)
    for row in range(ROWS):
        start = row * tile_rows
        here = slope_x[start : start + tile_rows, :]
        west = pltpu.roll(side[:tile_rows, :], (tile_cols - row) % tile_cols, 1)
        east = pltpu.roll(side[tile_rows:, :], tile_cols - 1 - row, 1)
        before = jnp.where(lane == 0, jnp.where(column == 0, -here, west), pltpu.roll(here, 1, 1))
        after = jnp.where(
            lane == tile_cols - 1,
            jnp.where(column == CLASSES * CORES - 1, -here, east),
            pltpu.roll(here, tile_cols - 1, 1),
        )
        spread = before - after + slope_y[start + 7 : start + 7 + tile_rows, :] - slope_y[start + 9 : start + 9 + tile_rows, :]
        for group in range(tile_rows // 8):
            out_ref[row * (tile_rows // 8) + group, 0:8, :] = spread[group * 8 : group * 8 + 8]


def terms(column, maps, sums, got, scale):
    arrays, picks = zip(*got)
    count = sum(len(some) for some in picks)
    given = [maps] + ([] if sums is None else [sums]) + list(arrays)
    rows, cols = maps.shape[1:]
    scratch = [
        pltpu.VMEM((count * ROWS, cols), jnp.float32),
        pltpu.SMEM((count * ROWS, cols), jnp.float32),
        pltpu.SemaphoreType.DMA,
    ]
    if scale is None:
        out = (4, rows, cols)
    else:
        out = ((rows - ROWS) // 8, 16, cols)
        scratch += [pltpu.VMEM((rows - ROWS, cols), jnp.float32), pltpu.VMEM((rows - ROWS + 16, cols), jnp.float32)]
        scratch += [pltpu.VMEM((cols, cols), jnp.float32)]
    return pl.pallas_call(
        lambda *refs: terms_kernel(scale, sums is not None, picks, *refs),
        out_shape=pltpu.VMEM(out, jnp.float32),
        in_specs=[SMEM] + [VMEM] * len(given),
        out_specs=VMEM,
        scratch_shapes=scratch,
        cost_estimate=pl.CostEstimate(flops=60 * count * rows * cols, bytes_accessed=4 << 20, transcendentals=0),
        compiler_params=pltpu.CompilerParams(vmem_limit_bytes=4 << 20),
    )(column, *in_vmem(*given))


EACH2 = [(0,), (1,)]
EACH4 = EACH2 + [(2,), (3,)]


def body(heights, albedo, blocks, block_params, block_dest):
    column_here = lax.axis_index(("zl", "c"))
    tile_rows, tile_cols = heights.shape[1:]
    block_count = block_dest.shape[2]

    height, shade = heights[0], albedo[0]
    first, last = jnp.stack([height[:, 0], height[:, 1], shade[:, 0]]), jnp.stack([height[:, -1], height[:, -2], shade[:, -1]])
    from_west = column_shift(last, 1)
    from_east = column_shift(first, -1)

    here = jnp.stack([lax.axis_index("zl"), lax.axis_index("c")]).astype(jnp.int32)
    near, *own, other = pack(
        here,
        block_dest.reshape(block_count),
        block_params.reshape(block_count, PARAMS).T,
        blocks.reshape(block_count, tile_rows, tile_cols),
    )
    swapped = lax.ppermute(other, "c", [(0, 1), (1, 0)])
    to_first, to_second, to_far = join(here, swapped, *own)
    far = ring_shift(to_far, 2)
    next0 = ring_shift(to_first, 1)
    next1 = ring_shift(to_second, -1)

    beside = jnp.concatenate([from_west, from_east], axis=1)
    mine = jnp.concatenate([first[:1], last[:1]], axis=1)
    rows = jnp.concatenate([beside, mine, jnp.zeros((ROWS - 4, tile_cols), jnp.float32)])
    copies = make_copies(height, shade, rows)
    gathered = lax.all_to_all(copies, "y", split_axis=0, concat_axis=0, tiled=True)
    column = column_here.reshape(1).astype(jnp.int32)
    maps = make_maps(column, gathered)

    sums = terms(column, maps, None, [(near, [(0,), (1,)]), (swapped, [(0, 0), (0, 1)])], None)
    sums = terms(column, maps, sums, [(far, EACH4)], None)
    sums = terms(column, maps, sums, [(next0, EACH4)], None)
    parts = terms(column, maps, sums, [(next1, EACH4)], 1.0 / block_count)
    summed = jnp.sum(lax.all_to_all(parts, ("y",) + IMG, split_axis=0, concat_axis=0, tiled=True), axis=0)
    half = tile_rows // (HALVES * DEPTH)
    return (summed[None, :half], summed[None, half:])


def solution(mesh):
    physical = Mesh(mesh.devices.reshape(ROWS, CLASSES, CORES, HALVES, DEPTH), TILE + IMG)
    placed = (
        P(TILE, None, None),
        P(TILE, None, None),
        P(TILE, IMG, None, None, None),
        P(TILE, IMG, None, None),
        P(TILE, IMG, None, None),
    )

    return jax.shard_map(
        body,
        mesh=physical,
        in_specs=placed,
        out_specs=(P(TILE, IMG, None), P(TILE, IMG, None)),
        check_vma=False,
    )
```

```python
import jax
import jax.numpy as jnp
from jax import lax
from jax.experimental import pallas as pl
from jax.experimental.pallas import tpu as pltpu
from jax.sharding import Mesh
from jax.sharding import PartitionSpec as P


SMOOTH = 0.0025
PARAMS = 8
STRIP = 16
PLACED = 2
ROWS, CLASSES, CORES, HALVES, DEPTH = 8, 4, 2, 2, 4
RING = CLASSES * HALVES
TILE = ("y", "zl", "c")
IMG = ("zh", "x")

SMEM = pl.BlockSpec(memory_space=pltpu.SMEM)
VMEM = pl.BlockSpec(memory_space=pltpu.VMEM)


def ring_shift(value, steps):
    pairs = []
    for low in range(CLASSES):
        for core in range(CORES):
            for high in range(HALVES):
                z = (high * CLASSES + low + steps * (1 - 2 * core)) % RING
                source = (low * CORES + core) * HALVES + high
                pairs.append((source, ((z % CLASSES) * CORES + core) * HALVES + z // CLASSES))
    return lax.ppermute(value, ("zl", "c", "zh"), pairs)


def column_shift(value, steps):
    count = CLASSES * CORES
    pairs = [(k, k + steps) for k in range(count) if 0 <= k + steps < count]
    return lax.ppermute(value, ("zl", "c"), pairs)


def in_vmem(*arrays):
    return [pltpu.with_memory_space_constraint(a, pltpu.VMEM) for a in arrays]


def fill_table(dest_ref, table):
    number = dest_ref.shape[0]

    def clear(index, carry):
        table[index] = number
        return carry

    lax.fori_loop(0, table.shape[0], clear, 0, unroll=8)

    def note(index, carry):
        place = dest_ref[index] * 2
        second = (table[place] < number).astype(jnp.int32)
        table[place + second] = index
        return carry

    lax.fori_loop(0, number, note, 0, unroll=4)


def first_turn(core):
    return 1 + core * (CLASSES - 2)


def pack_kernel(
    here_ref, dest_ref, params_ref, blocks_hbm, near_ref, first_ref, second_ref, far_ref, other_ref,
    blocks_ref, sem, table, shifted, columns, rim, lines,
):
    number, tile_rows, tile_cols = blocks_hbm.shape
    fetch = pltpu.make_async_copy(blocks_hbm, blocks_ref.at[:number], sem)
    fetch.start()
    blocks_ref[number] = jnp.zeros((tile_rows, tile_cols), jnp.bfloat16)
    for part in range(3):
        shifted[part, number:, :] = jnp.zeros((8, tile_cols), jnp.float32)
    for part in range(2):
        rim[part, number // 2 :, :] = jnp.zeros((8, tile_cols), jnp.float32)
    fill_table(dest_ref, table)
    upright = params_ref[...].astype(jnp.float32)
    upright = jnp.concatenate([upright, jnp.zeros((PARAMS, tile_cols - number), jnp.float32)], axis=1)
    plain = turned(upright)[:number]
    for k in range(3):
        shifted[k, :number, :] = plain if k == 0 else pltpu.roll(plain, k * PARAMS, 1)

    fetch.wait()

    lane8 = lax.broadcasted_iota(jnp.int32, (8, tile_cols), 1)
    sub8 = lax.broadcasted_iota(jnp.int32, (8, tile_cols), 0)
    pick = jnp.where(((sub8 == 0) & (lane8 == tile_cols - 1)) | ((sub8 == 1) & (lane8 == 0)), 1.0, 0.0).astype(jnp.bfloat16)
    flat = lax.dot_general(
        pick,
        blocks_ref[:number].reshape(number * tile_rows, tile_cols),
        (((1,), (1,)), ((), ())),
        preferred_element_type=jnp.float32,
    )
    pairs = number // 2
    for m in range(pairs):
        part = slice(m * tile_cols, (m + 1) * tile_cols)
        columns[0, m : m + 1, :] = flat[0:1, part]
        columns[1, m : m + 1, :] = flat[1:2, part]
    left_half = lax.broadcasted_iota(jnp.int32, (pairs, tile_cols), 1) < tile_rows
    last, first = columns[0], columns[1]
    rim[0, :pairs, :] = jnp.where(left_half, last, pltpu.roll(first, tile_rows, 1))
    rim[1, :pairs, :] = jnp.where(left_half, pltpu.roll(last, tile_rows, 1), first)

    low, core = here_ref[0], here_ref[1]
    count = CLASSES * CORES
    west_half = lax.broadcasted_iota(jnp.int32, (1, tile_cols), 1) < tile_rows
    pixels = ROWS * tile_rows
    turn = first_turn(core)
    mine = [
        (0, near_ref.at[0], near_ref.at[1]),
        (turn, first_ref.at[0], first_ref.at[1]),
        (CLASSES // 2, far_ref.at[0], far_ref.at[1]),
        (CLASSES - turn, second_ref.at[0], second_ref.at[1]),
    ]

    for kind in range(CORES):
        for d in range(CLASSES):
            step, *units = (d, other_ref.at[d, 0], other_ref.at[d, 1]) if kind else mine[d]
            column = ((low + step) % CLASSES) * CORES + (core + kind) % CORES

            def place(step, carry):
                found = []
                for row in range(PLACED):
                    row = step * PLACED + row
                    tile = row * count + column
                    for slot in (0, 1):
                        block = table[2 * tile + slot]
                        west = jnp.where(column > 0, table[jnp.maximum(2 * tile - 2, 0) + slot], number)
                        east = jnp.where(
                            column < count - 1, table[jnp.minimum(2 * tile + 2, 2 * ROWS * count - 2) + slot], number
                        )
                        line = shifted[0, pl.ds(block, 1), :] + shifted[1, pl.ds(west, 1), :] + shifted[2, pl.ds(east, 1), :]
                        sides = [rim[index & 1, pl.ds(index >> 1, 1), :] for index in (west, east)]
                        found.append((row, slot, blocks_ref[block], jnp.where(west_half, sides[0], sides[1]), line))
                for row, slot, values, side, line in found:
                    start = pl.multiple_of(row * tile_rows, tile_rows)
                    units[slot][pl.ds(start, tile_rows), :] = values
                    lines[0, slot, pl.ds(row, 1), :] = side
                    lines[1, slot, pl.ds(row, 1), :] = line
                return carry

            lax.fori_loop(0, ROWS // PLACED, place, 0)
            for slot in (0, 1):
                for k in (0, 1):
                    units[slot][pixels + k * ROWS : pixels + (k + 1) * ROWS, :] = lines[k, slot].astype(jnp.bfloat16)


def pack(here, dest, params, blocks):
    number, tile_rows, tile_cols = blocks.shape
    unit = (ROWS * tile_rows + 2 * ROWS, tile_cols)
    return pl.pallas_call(
        pack_kernel,
        out_shape=[pltpu.VMEM(lead + unit, jnp.bfloat16) for lead in ((2,), (2,), (2,), (2,), (CLASSES, 2))],
        in_specs=[SMEM, SMEM, VMEM, pl.BlockSpec(memory_space=pltpu.HBM)],
        out_specs=[VMEM] * 5,
        scratch_shapes=[
            pltpu.VMEM((number + 1, tile_rows, tile_cols), jnp.bfloat16),
            pltpu.SemaphoreType.DMA,
            pltpu.SMEM((2 * ROWS * CLASSES * CORES,), jnp.int32),
            pltpu.VMEM((3, number + 8, tile_cols), jnp.float32),
            pltpu.VMEM((2, number // 2, tile_cols), jnp.float32),
            pltpu.VMEM((2, number // 2 + 8, tile_cols), jnp.float32),
            pltpu.VMEM((2, 2, ROWS, tile_cols), jnp.float32),
        ],
        cost_estimate=pl.CostEstimate(flops=0, bytes_accessed=6 << 20, transcendentals=0),
        compiler_params=pltpu.CompilerParams(vmem_limit_bytes=8 << 20),
        name="pack",
    )(here, *[pltpu.with_memory_space_constraint(a, pltpu.HBM) for a in (dest, params, blocks)])


def join_kernel(here_ref, swapped_ref, first_own, second_own, far_own, first_ref, second_ref, far_ref):
    core = here_ref[1]
    turn = first_turn(core)
    first_ref[0:2] = first_own[...]
    first_ref[2:4] = swapped_ref[turn]
    second_ref[0:2] = second_own[...]
    second_ref[2:4] = swapped_ref[CLASSES - turn]
    far_ref[0:2] = far_own[...]
    far_ref[2:4] = swapped_ref[CLASSES // 2]


def join(here, swapped, *own):
    unit = swapped.shape[2:]
    return pl.pallas_call(
        join_kernel,
        out_shape=[pltpu.VMEM((n,) + unit, swapped.dtype) for n in (4, 4, 4)],
        in_specs=[SMEM] + [VMEM] * 4,
        out_specs=[VMEM] * 3,
        cost_estimate=pl.CostEstimate(flops=0, bytes_accessed=2 << 20, transcendentals=0),
        compiler_params=pltpu.CompilerParams(vmem_limit_bytes=4 << 20),
        name="join",
    )(here, *in_vmem(swapped, *own))


def copies_kernel(height_ref, albedo_ref, rows_ref, out_ref):
    tile_rows = height_ref.shape[0]
    for row in range(ROWS):
        out_ref[row, :tile_rows, :] = height_ref[...]
        out_ref[row, tile_rows : 2 * tile_rows, :] = albedo_ref[...]
        out_ref[row, 2 * tile_rows :, :] = rows_ref[...]


def make_copies(height, albedo, rows):
    return pl.pallas_call(
        copies_kernel,
        out_shape=pltpu.VMEM((ROWS, 2 * height.shape[0] + ROWS, height.shape[1]), jnp.float32),
        in_specs=[VMEM] * 3,
        out_specs=VMEM,
        cost_estimate=pl.CostEstimate(flops=0, bytes_accessed=1 << 20, transcendentals=0),
        compiler_params=pltpu.CompilerParams(vmem_limit_bytes=4 << 20),
        name="copies",
    )(*in_vmem(height, albedo, rows))


def turned(rows):
    size = rows.shape[1]
    return jnp.transpose(jnp.concatenate([rows, jnp.zeros((size - rows.shape[0], size), rows.dtype)]))


def maps_kernel(column_ref, got_ref, maps_ref, tall, side):
    tile_cols = got_ref.shape[2]
    tile_rows = (got_ref.shape[1] - ROWS) // 2
    pixels = ROWS * tile_rows
    column = column_ref[0]
    lane = lax.broadcasted_iota(jnp.int32, (tile_rows, tile_cols), 1)

    def finish(part, p, q, albedo):
        maps_ref[0, part, :] = p
        maps_ref[1, part, :] = q
        maps_ref[2, part, :] = 1.0 / jnp.sqrt(1.0 + p * p + q * q)
        maps_ref[3, part, :] = albedo

    for row in range(ROWS):
        tall[8 + row * tile_rows : 8 + (row + 1) * tile_rows, :] = got_ref[row, :tile_rows, :]
    tall[7:8, :] = got_ref[0, 0:1, :]
    tall[8 + pixels : 9 + pixels, :] = got_ref[ROWS - 1, tile_rows - 1 : tile_rows, :]
    beside, beyond, shade, mine = [
        jnp.concatenate([got_ref[row, 2 * tile_rows + k : 2 * tile_rows + k + 1, :] for row in range(ROWS)]) for k in range(4)
    ]
    side[...] = turned(beside)
    for row in range(ROWS):
        start = 8 + row * tile_rows
        height = tall[start : start + tile_rows, :]
        west = pltpu.roll(side[:tile_rows, :], (tile_cols - row) % tile_cols, 1)
        east = pltpu.roll(side[tile_rows:, :], tile_cols - 1 - row, 1)
        before = jnp.where(lane == 0, jnp.where(column == 0, height, west), pltpu.roll(height, 1, 1))
        after = jnp.where(
            lane == tile_cols - 1,
            jnp.where(column == CLASSES * CORES - 1, height, east),
            pltpu.roll(height, tile_cols - 1, 1),
        )
        p = (after - before) * 0.5
        q = (tall[start + 1 : start + 1 + tile_rows, :] - tall[start - 1 : start - 1 + tile_rows, :]) * 0.5
        finish(slice(row * tile_rows, (row + 1) * tile_rows), p, q, got_ref[row, tile_rows : 2 * tile_rows, :])

    lane = lax.broadcasted_iota(jnp.int32, (ROWS, tile_cols), 1)
    p = jnp.where(lane < tile_rows, mine - beyond, beyond - mine) * 0.5
    lower = jnp.concatenate([pltpu.roll(beside, tile_rows - 1, 1)[1:], beside[ROWS - 1 :]])
    upper = jnp.concatenate([beside[:1], pltpu.roll(beside, tile_cols - tile_rows + 1, 1)[:-1]])
    place = lane % tile_rows
    following = jnp.where(place == tile_rows - 1, lower, pltpu.roll(beside, tile_cols - 1, 1))
    preceding = jnp.where(place == 0, upper, pltpu.roll(beside, 1, 1))
    finish(slice(pixels, pixels + ROWS), p, (following - preceding) * 0.5, shade)


def make_maps(column, got):
    tile_cols = got.shape[2]
    pixels = ROWS * (got.shape[1] - ROWS) // 2
    return pl.pallas_call(
        maps_kernel,
        out_shape=pltpu.VMEM((4, pixels + ROWS, tile_cols), jnp.float32),
        in_specs=[SMEM, VMEM],
        out_specs=VMEM,
        scratch_shapes=[
            pltpu.VMEM((pixels + 16, tile_cols), jnp.float32),
            pltpu.VMEM((tile_cols, tile_cols), jnp.float32),
        ],
        cost_estimate=pl.CostEstimate(flops=0, bytes_accessed=3 << 20, transcendentals=0),
        compiler_params=pltpu.CompilerParams(vmem_limit_bytes=4 << 20),
        name="maps",
    )(column, *in_vmem(got))


def add_block(maps, totals, values, bright):
    pw, qw, w, albedo = maps
    sum_x, sum_y, sum_z, shade = totals
    sx, sy, sz, vx, vy, vz, mix, gain = values
    mix2, rest = mix * 2.0, (1.0 - mix) * 0.5
    vx, vy, vz = vx * 2.0, vy * 2.0, vz * 2.0
    ci = sz * w - sx * pw - sy * qw
    ce = vz * w - vx * pw - vy * qw
    square = ci * ci + SMOOTH
    inv_root = lax.rsqrt(square)
    mu = ci + square * inv_root
    inv = 1.0 / (mu + ce)
    k = mix2 * inv
    shading = mu * (k + rest)
    weight = gain * albedo
    gs = weight * (weight * shading - bright.astype(jnp.float32))
    shade = shade + gs * shading
    gi = (gs * (k * (ce * inv) + rest)) * (mu * inv_root)
    ge = (gs * k) * (mu * inv)
    return (
        sum_x + (gi * sx - ge * vx),
        sum_y + (gi * sy - ge * vy),
        sum_z + (gi * sz - ge * vz),
        shade,
    )


def terms_kernel(scale, with_sums, picks, *refs):
    column_ref, maps_ref, *refs = refs
    sums_ref = None
    if with_sums:
        sums_ref, *refs = refs
    got, refs = refs[: len(picks)], refs[len(picks) :]
    out_ref, lines, params, sem, *refs = refs
    units = [ref.at[pick] for ref, some in zip(got, picks) for pick in some]
    tile_cols = maps_ref.shape[2]
    pixels = maps_ref.shape[1] - ROWS
    tile_rows = pixels // ROWS
    for index, unit in enumerate(units):
        lines[index * ROWS : (index + 1) * ROWS, :] = unit[pixels + ROWS :, :].astype(jnp.float32)
    copy = pltpu.make_async_copy(lines, params, sem)
    copy.start()
    copy.wait()

    def run(part, size, values_of):
        p, q, w, albedo = (maps_ref[k, part, :] for k in range(4))
        if with_sums:
            totals = tuple(sums_ref[k, part, :] for k in range(4))
        else:
            totals = (jnp.zeros((size, tile_cols), jnp.float32),) * 4
        maps = (p * w, q * w, w, albedo)
        for number, unit in enumerate(units):
            totals = add_block(maps, totals, values_of(number), unit[part, :])
        if scale is None:
            for k, total in enumerate(totals):
                out_ref[k, part, :] = total
            return None
        sum_x, sum_y, sum_z, shade = totals
        up = (w * w * w) * (sum_z - p * sum_x - q * sum_y)
        half_x = (-(w * sum_x) - p * up) * (0.5 * scale)
        half_y = (-(w * sum_y) - q * up) * (0.5 * scale)
        return half_x, half_y, shade * scale / albedo

    def strip(index, carry):
        first = pl.multiple_of(index * STRIP, STRIP)
        row = index // (tile_rows // STRIP)
        result = run(pl.ds(first, STRIP), STRIP, lambda number: [params[number * ROWS + row, k] for k in range(PARAMS)])
        if result is not None:
            slope_x, slope_y, _ = refs
            slope_x[pl.ds(first, STRIP), :] = result[0]
            slope_y[pl.ds(pl.multiple_of(first + 8, 8), STRIP), :] = result[1]
            for half in range(STRIP // 8):
                out_ref[index * (STRIP // 8) + half, 8:16, :] = result[2][half * 8 : half * 8 + 8]
        return carry

    lax.fori_loop(0, pixels // STRIP, strip, 0)

    west_half = lax.broadcasted_iota(jnp.int32, (ROWS, tile_cols), 1) < tile_rows

    def side_values(number):
        rows = lines[number * ROWS : (number + 1) * ROWS, :]
        values = []
        for k in range(PARAMS):
            west, east = (
                jnp.broadcast_to(rows[:, n * PARAMS + k : n * PARAMS + k + 1], (ROWS, tile_cols)) for n in (1, 2)
            )
            values.append(jnp.where(west_half, west, east))
        return values

    result = run(slice(pixels, pixels + ROWS), ROWS, side_values)
    if result is None:
        return

    slope_x, slope_y, side = refs
    column = column_ref[0]
    side[...] = turned(result[0])
    slope_y[7:8, :] = -slope_y[8:9, :]
    slope_y[8 + pixels : 9 + pixels, :] = -slope_y[7 + pixels : 8 + pixels, :]
    lane = lax.broadcasted_iota(jnp.int32, (tile_rows, tile_cols), 1)
    for row in range(ROWS):
        start = row * tile_rows
        here = slope_x[start : start + tile_rows, :]
        west = pltpu.roll(side[:tile_rows, :], (tile_cols - row) % tile_cols, 1)
        east = pltpu.roll(side[tile_rows:, :], tile_cols - 1 - row, 1)
        before = jnp.where(lane == 0, jnp.where(column == 0, -here, west), pltpu.roll(here, 1, 1))
        after = jnp.where(
            lane == tile_cols - 1,
            jnp.where(column == CLASSES * CORES - 1, -here, east),
            pltpu.roll(here, tile_cols - 1, 1),
        )
        spread = before - after + slope_y[start + 7 : start + 7 + tile_rows, :] - slope_y[start + 9 : start + 9 + tile_rows, :]
        for group in range(tile_rows // 8):
            out_ref[row * (tile_rows // 8) + group, 0:8, :] = spread[group * 8 : group * 8 + 8]


def terms(column, maps, sums, got, scale):
    arrays, picks = zip(*got)
    count = sum(len(some) for some in picks)
    given = [maps] + ([] if sums is None else [sums]) + list(arrays)
    rows, cols = maps.shape[1:]
    scratch = [
        pltpu.VMEM((count * ROWS, cols), jnp.float32),
        pltpu.SMEM((count * ROWS, cols), jnp.float32),
        pltpu.SemaphoreType.DMA,
    ]
    if scale is None:
        out = (4, rows, cols)
    else:
        out = ((rows - ROWS) // 8, 16, cols)
        scratch += [pltpu.VMEM((rows - ROWS, cols), jnp.float32), pltpu.VMEM((rows - ROWS + 16, cols), jnp.float32)]
        scratch += [pltpu.VMEM((cols, cols), jnp.float32)]
    return pl.pallas_call(
        lambda *refs: terms_kernel(scale, sums is not None, picks, *refs),
        out_shape=pltpu.VMEM(out, jnp.float32),
        in_specs=[SMEM] + [VMEM] * len(given),
        out_specs=VMEM,
        scratch_shapes=scratch,
        cost_estimate=pl.CostEstimate(flops=60 * count * rows * cols, bytes_accessed=4 << 20, transcendentals=0),
        compiler_params=pltpu.CompilerParams(vmem_limit_bytes=4 << 20),
    )(column, *in_vmem(*given))


EACH2 = [(0,), (1,)]
EACH4 = EACH2 + [(2,), (3,)]


def body(heights, albedo, blocks, block_params, block_dest):
    column_here = lax.axis_index(("zl", "c"))
    tile_rows, tile_cols = heights.shape[1:]
    block_count = block_dest.shape[2]

    height, shade = heights[0], albedo[0]
    first, last = jnp.stack([height[:, 0], height[:, 1], shade[:, 0]]), jnp.stack([height[:, -1], height[:, -2], shade[:, -1]])
    from_west = column_shift(last, 1)
    from_east = column_shift(first, -1)

    here = jnp.stack([lax.axis_index("zl"), lax.axis_index("c")]).astype(jnp.int32)
    near, *own, other = pack(
        here,
        block_dest.reshape(block_count),
        block_params.reshape(block_count, PARAMS).T,
        blocks.reshape(block_count, tile_rows, tile_cols),
    )
    swapped = lax.ppermute(other, "c", [(0, 1), (1, 0)])
    to_first, to_second, to_far = join(here, swapped, *own)
    far = ring_shift(to_far, 2)
    next0 = ring_shift(to_first, 1)
    next1 = ring_shift(to_second, -1)

    beside = jnp.concatenate([from_west, from_east], axis=1)
    mine = jnp.concatenate([first[:1], last[:1]], axis=1)
    rows = jnp.concatenate([beside, mine, jnp.zeros((ROWS - 4, tile_cols), jnp.float32)])
    copies = make_copies(height, shade, rows)
    gathered = lax.all_to_all(copies, "y", split_axis=0, concat_axis=0, tiled=True)
    column = column_here.reshape(1).astype(jnp.int32)
    maps = make_maps(column, gathered)

    sums = terms(column, maps, None, [(near, EACH2), (swapped, [(0, 0), (0, 1)]), (far, EACH4)], None)
    sums = terms(column, maps, sums, [(next0, EACH4)], None)
    parts = terms(column, maps, sums, [(next1, EACH4)], 1.0 / block_count)
    summed = jnp.sum(lax.all_to_all(parts, ("y",) + IMG, split_axis=0, concat_axis=0, tiled=True), axis=0)
    half = tile_rows // (HALVES * DEPTH)
    return (summed[None, :half], summed[None, half:])


def solution(mesh):
    physical = Mesh(mesh.devices.reshape(ROWS, CLASSES, CORES, HALVES, DEPTH), TILE + IMG)
    placed = (
        P(TILE, None, None),
        P(TILE, None, None),
        P(TILE, IMG, None, None, None),
        P(TILE, IMG, None, None),
        P(TILE, IMG, None, None),
    )

    return jax.shard_map(
        body,
        mesh=physical,
        in_specs=placed,
        out_specs=(P(TILE, IMG, None), P(TILE, IMG, None)),
        check_vma=False,
    )
```

```python
import jax
import jax.numpy as jnp
from jax import lax
from jax.experimental import pallas as pl
from jax.experimental.pallas import tpu as pltpu
from jax.sharding import Mesh
from jax.sharding import PartitionSpec as P


SMOOTH = 0.0025
PARAMS = 8
STRIP = 16
PLACED = 2
ROWS, CLASSES, CORES, HALVES, DEPTH = 8, 4, 2, 2, 4
RING = CLASSES * HALVES
TILE = ("y", "zl", "c")
IMG = ("zh", "x")

SMEM = pl.BlockSpec(memory_space=pltpu.SMEM)
VMEM = pl.BlockSpec(memory_space=pltpu.VMEM)


def ring_shift(value, steps):
    pairs = []
    for low in range(CLASSES):
        for core in range(CORES):
            for high in range(HALVES):
                z = (high * CLASSES + low + steps * (1 - 2 * core)) % RING
                source = (low * CORES + core) * HALVES + high
                pairs.append((source, ((z % CLASSES) * CORES + core) * HALVES + z // CLASSES))
    return lax.ppermute(value, ("zl", "c", "zh"), pairs)


BETWEEN = [pair for k in range(1, CLASSES * CORES - 1, 2) for pair in ((k, k + 1), (k + 1, k))]


def in_vmem(*arrays):
    return [pltpu.with_memory_space_constraint(a, pltpu.VMEM) for a in arrays]


def fill_table(dest_ref, table):
    number = dest_ref.shape[0]

    def clear(index, carry):
        table[index] = number
        return carry

    lax.fori_loop(0, table.shape[0], clear, 0, unroll=8)

    def note(index, carry):
        place = dest_ref[index] * 2
        second = (table[place] < number).astype(jnp.int32)
        table[place + second] = index
        return carry

    lax.fori_loop(0, number, note, 0, unroll=4)


def first_turn(core):
    return 1 + core * (CLASSES - 2)


def pack_kernel(
    here_ref, dest_ref, params_ref, blocks_hbm, near_ref, first_ref, second_ref, far_ref, other_ref,
    blocks_ref, sem, table, shifted, columns, rim, lines,
):
    number, tile_rows, tile_cols = blocks_hbm.shape
    fetch = pltpu.make_async_copy(blocks_hbm, blocks_ref.at[:number], sem)
    fetch.start()
    blocks_ref[number] = jnp.zeros((tile_rows, tile_cols), jnp.bfloat16)
    for part in range(3):
        shifted[part, number:, :] = jnp.zeros((8, tile_cols), jnp.float32)
    for part in range(2):
        rim[part, number // 2 :, :] = jnp.zeros((8, tile_cols), jnp.float32)
    fill_table(dest_ref, table)
    upright = params_ref[...].astype(jnp.float32)
    upright = jnp.concatenate([upright, jnp.zeros((PARAMS, tile_cols - number), jnp.float32)], axis=1)
    plain = turned(upright)[:number]
    for k in range(3):
        shifted[k, :number, :] = plain if k == 0 else pltpu.roll(plain, k * PARAMS, 1)

    fetch.wait()

    lane8 = lax.broadcasted_iota(jnp.int32, (8, tile_cols), 1)
    sub8 = lax.broadcasted_iota(jnp.int32, (8, tile_cols), 0)
    pick = jnp.where(((sub8 == 0) & (lane8 == tile_cols - 1)) | ((sub8 == 1) & (lane8 == 0)), 1.0, 0.0).astype(jnp.bfloat16)
    flat = lax.dot_general(
        pick,
        blocks_ref[:number].reshape(number * tile_rows, tile_cols),
        (((1,), (1,)), ((), ())),
        preferred_element_type=jnp.float32,
    )
    pairs = number // 2
    for m in range(pairs):
        part = slice(m * tile_cols, (m + 1) * tile_cols)
        columns[0, m : m + 1, :] = flat[0:1, part]
        columns[1, m : m + 1, :] = flat[1:2, part]
    left_half = lax.broadcasted_iota(jnp.int32, (pairs, tile_cols), 1) < tile_rows
    last, first = columns[0], columns[1]
    rim[0, :pairs, :] = jnp.where(left_half, last, pltpu.roll(first, tile_rows, 1))
    rim[1, :pairs, :] = jnp.where(left_half, pltpu.roll(last, tile_rows, 1), first)

    low, core = here_ref[0], here_ref[1]
    count = CLASSES * CORES
    west_half = lax.broadcasted_iota(jnp.int32, (1, tile_cols), 1) < tile_rows
    pixels = ROWS * tile_rows
    turn = first_turn(core)
    mine = [
        (0, near_ref.at[0], near_ref.at[1]),
        (turn, first_ref.at[0], first_ref.at[1]),
        (CLASSES // 2, far_ref.at[0], far_ref.at[1]),
        (CLASSES - turn, second_ref.at[0], second_ref.at[1]),
    ]

    for kind in range(CORES):
        for d in range(CLASSES):
            step, *units = (d, other_ref.at[d, 0], other_ref.at[d, 1]) if kind else mine[d]
            column = ((low + step) % CLASSES) * CORES + (core + kind) % CORES

            def place(step, carry):
                found = []
                for row in range(PLACED):
                    row = step * PLACED + row
                    tile = row * count + column
                    for slot in (0, 1):
                        block = table[2 * tile + slot]
                        west = jnp.where(column > 0, table[jnp.maximum(2 * tile - 2, 0) + slot], number)
                        east = jnp.where(
                            column < count - 1, table[jnp.minimum(2 * tile + 2, 2 * ROWS * count - 2) + slot], number
                        )
                        line = shifted[0, pl.ds(block, 1), :] + shifted[1, pl.ds(west, 1), :] + shifted[2, pl.ds(east, 1), :]
                        sides = [rim[index & 1, pl.ds(index >> 1, 1), :] for index in (west, east)]
                        found.append((row, slot, blocks_ref[block], jnp.where(west_half, sides[0], sides[1]), line))
                for row, slot, values, side, line in found:
                    start = pl.multiple_of(row * tile_rows, tile_rows)
                    units[slot][pl.ds(start, tile_rows), :] = values
                    lines[0, slot, pl.ds(row, 1), :] = side
                    lines[1, slot, pl.ds(row, 1), :] = line
                return carry

            lax.fori_loop(0, ROWS // PLACED, place, 0)
            for slot in (0, 1):
                for k in (0, 1):
                    units[slot][pixels + k * ROWS : pixels + (k + 1) * ROWS, :] = lines[k, slot].astype(jnp.bfloat16)


def pack(here, dest, params, blocks):
    number, tile_rows, tile_cols = blocks.shape
    unit = (ROWS * tile_rows + 2 * ROWS, tile_cols)
    return pl.pallas_call(
        pack_kernel,
        out_shape=[pltpu.VMEM(lead + unit, jnp.bfloat16) for lead in ((2,), (2,), (2,), (2,), (CLASSES, 2))],
        in_specs=[SMEM, SMEM, VMEM, pl.BlockSpec(memory_space=pltpu.HBM)],
        out_specs=[VMEM] * 5,
        scratch_shapes=[
            pltpu.VMEM((number + 1, tile_rows, tile_cols), jnp.bfloat16),
            pltpu.SemaphoreType.DMA,
            pltpu.SMEM((2 * ROWS * CLASSES * CORES,), jnp.int32),
            pltpu.VMEM((3, number + 8, tile_cols), jnp.float32),
            pltpu.VMEM((2, number // 2, tile_cols), jnp.float32),
            pltpu.VMEM((2, number // 2 + 8, tile_cols), jnp.float32),
            pltpu.VMEM((2, 2, ROWS, tile_cols), jnp.float32),
        ],
        cost_estimate=pl.CostEstimate(flops=0, bytes_accessed=6 << 20, transcendentals=0),
        compiler_params=pltpu.CompilerParams(vmem_limit_bytes=8 << 20),
        name="pack",
    )(here, *[pltpu.with_memory_space_constraint(a, pltpu.HBM) for a in (dest, params, blocks)])


def join_kernel(here_ref, swapped_ref, first_own, second_own, far_own, first_ref, second_ref, far_ref):
    core = here_ref[1]
    turn = first_turn(core)
    first_ref[0:2] = first_own[...]
    first_ref[2:4] = swapped_ref[turn]
    second_ref[0:2] = second_own[...]
    second_ref[2:4] = swapped_ref[CLASSES - turn]
    far_ref[0:2] = far_own[...]
    far_ref[2:4] = swapped_ref[CLASSES // 2]


def join(here, swapped, *own):
    unit = swapped.shape[2:]
    return pl.pallas_call(
        join_kernel,
        out_shape=[pltpu.VMEM((n,) + unit, swapped.dtype) for n in (4, 4, 4)],
        in_specs=[SMEM] + [VMEM] * 4,
        out_specs=[VMEM] * 3,
        cost_estimate=pl.CostEstimate(flops=0, bytes_accessed=2 << 20, transcendentals=0),
        compiler_params=pltpu.CompilerParams(vmem_limit_bytes=4 << 20),
        name="join",
    )(here, *in_vmem(swapped, *own))


def copies_kernel(height_ref, albedo_ref, rows_ref, out_ref):
    tile_rows = height_ref.shape[0]
    for row in range(ROWS):
        out_ref[row, :tile_rows, :] = height_ref[...]
        out_ref[row, tile_rows : 2 * tile_rows, :] = albedo_ref[...]
        out_ref[row, 2 * tile_rows :, :] = rows_ref[...]


def make_copies(height, albedo, rows):
    return pl.pallas_call(
        copies_kernel,
        out_shape=pltpu.VMEM((ROWS, 2 * height.shape[0] + ROWS, height.shape[1]), jnp.float32),
        in_specs=[VMEM] * 3,
        out_specs=VMEM,
        cost_estimate=pl.CostEstimate(flops=0, bytes_accessed=1 << 20, transcendentals=0),
        compiler_params=pltpu.CompilerParams(vmem_limit_bytes=4 << 20),
        name="copies",
    )(*in_vmem(height, albedo, rows))


def turned(rows):
    size = rows.shape[1]
    return jnp.transpose(jnp.concatenate([rows, jnp.zeros((size - rows.shape[0], size), rows.dtype)]))


def maps_kernel(column_ref, got_ref, maps_ref, tall, side):
    tile_cols = got_ref.shape[2]
    tile_rows = (got_ref.shape[1] - ROWS) // 2
    pixels = ROWS * tile_rows
    column = column_ref[0]
    lane = lax.broadcasted_iota(jnp.int32, (tile_rows, tile_cols), 1)

    def finish(part, p, q, albedo):
        maps_ref[0, part, :] = p
        maps_ref[1, part, :] = q
        maps_ref[2, part, :] = 1.0 / jnp.sqrt(1.0 + p * p + q * q)
        maps_ref[3, part, :] = albedo

    for row in range(ROWS):
        tall[8 + row * tile_rows : 8 + (row + 1) * tile_rows, :] = got_ref[row, :tile_rows, :]
    tall[7:8, :] = got_ref[0, 0:1, :]
    tall[8 + pixels : 9 + pixels, :] = got_ref[ROWS - 1, tile_rows - 1 : tile_rows, :]
    beside, beyond, shade, mine = [
        jnp.concatenate([got_ref[row, 2 * tile_rows + k : 2 * tile_rows + k + 1, :] for row in range(ROWS)]) for k in range(4)
    ]
    side[...] = turned(beside)
    for row in range(ROWS):
        start = 8 + row * tile_rows
        height = tall[start : start + tile_rows, :]
        west = pltpu.roll(side[:tile_rows, :], (tile_cols - row) % tile_cols, 1)
        east = pltpu.roll(side[tile_rows:, :], tile_cols - 1 - row, 1)
        before = jnp.where(lane == 0, jnp.where(column == 0, height, west), pltpu.roll(height, 1, 1))
        after = jnp.where(
            lane == tile_cols - 1,
            jnp.where(column == CLASSES * CORES - 1, height, east),
            pltpu.roll(height, tile_cols - 1, 1),
        )
        p = (after - before) * 0.5
        q = (tall[start + 1 : start + 1 + tile_rows, :] - tall[start - 1 : start - 1 + tile_rows, :]) * 0.5
        finish(slice(row * tile_rows, (row + 1) * tile_rows), p, q, got_ref[row, tile_rows : 2 * tile_rows, :])

    lane = lax.broadcasted_iota(jnp.int32, (ROWS, tile_cols), 1)
    p = jnp.where(lane < tile_rows, mine - beyond, beyond - mine) * 0.5
    lower = jnp.concatenate([pltpu.roll(beside, tile_rows - 1, 1)[1:], beside[ROWS - 1 :]])
    upper = jnp.concatenate([beside[:1], pltpu.roll(beside, tile_cols - tile_rows + 1, 1)[:-1]])
    place = lane % tile_rows
    following = jnp.where(place == tile_rows - 1, lower, pltpu.roll(beside, tile_cols - 1, 1))
    preceding = jnp.where(place == 0, upper, pltpu.roll(beside, 1, 1))
    finish(slice(pixels, pixels + ROWS), p, (following - preceding) * 0.5, shade)


def make_maps(column, got):
    tile_cols = got.shape[2]
    pixels = ROWS * (got.shape[1] - ROWS) // 2
    return pl.pallas_call(
        maps_kernel,
        out_shape=pltpu.VMEM((4, pixels + ROWS, tile_cols), jnp.float32),
        in_specs=[SMEM, VMEM],
        out_specs=VMEM,
        scratch_shapes=[
            pltpu.VMEM((pixels + 16, tile_cols), jnp.float32),
            pltpu.VMEM((tile_cols, tile_cols), jnp.float32),
        ],
        cost_estimate=pl.CostEstimate(flops=0, bytes_accessed=3 << 20, transcendentals=0),
        compiler_params=pltpu.CompilerParams(vmem_limit_bytes=4 << 20),
        name="maps",
    )(column, *in_vmem(got))


def add_block(maps, totals, values, bright):
    pw, qw, w, albedo = maps
    sum_x, sum_y, sum_z, shade = totals
    sx, sy, sz, vx, vy, vz, mix, gain = values
    mix2, rest = mix * 2.0, (1.0 - mix) * 0.5
    vx, vy, vz = vx * 2.0, vy * 2.0, vz * 2.0
    ci = sz * w - sx * pw - sy * qw
    ce = vz * w - vx * pw - vy * qw
    square = ci * ci + SMOOTH
    inv_root = lax.rsqrt(square)
    mu = ci + square * inv_root
    inv = 1.0 / (mu + ce)
    k = mix2 * inv
    shading = mu * (k + rest)
    weight = gain * albedo
    gs = weight * (weight * shading - bright.astype(jnp.float32))
    shade = shade + gs * shading
    gi = (gs * (k * (ce * inv) + rest)) * (mu * inv_root)
    ge = (gs * k) * (mu * inv)
    return (
        sum_x + (gi * sx - ge * vx),
        sum_y + (gi * sy - ge * vy),
        sum_z + (gi * sz - ge * vz),
        shade,
    )


def terms_kernel(scale, with_sums, picks, *refs):
    column_ref, maps_ref, *refs = refs
    sums_ref = None
    if with_sums:
        sums_ref, *refs = refs
    got, refs = refs[: len(picks)], refs[len(picks) :]
    out_ref, lines, params, sem, *refs = refs
    units = [ref.at[pick] for ref, some in zip(got, picks) for pick in some]
    tile_cols = maps_ref.shape[2]
    pixels = maps_ref.shape[1] - ROWS
    tile_rows = pixels // ROWS
    for index, unit in enumerate(units):
        lines[index * ROWS : (index + 1) * ROWS, :] = unit[pixels + ROWS :, :].astype(jnp.float32)
    copy = pltpu.make_async_copy(lines, params, sem)
    copy.start()
    copy.wait()

    def run(part, size, values_of):
        p, q, w, albedo = (maps_ref[k, part, :] for k in range(4))
        if with_sums:
            totals = tuple(sums_ref[k, part, :] for k in range(4))
        else:
            totals = (jnp.zeros((size, tile_cols), jnp.float32),) * 4
        maps = (p * w, q * w, w, albedo)
        for number, unit in enumerate(units):
            totals = add_block(maps, totals, values_of(number), unit[part, :])
        if scale is None:
            for k, total in enumerate(totals):
                out_ref[k, part, :] = total
            return None
        sum_x, sum_y, sum_z, shade = totals
        up = (w * w * w) * (sum_z - p * sum_x - q * sum_y)
        half_x = (-(w * sum_x) - p * up) * (0.5 * scale)
        half_y = (-(w * sum_y) - q * up) * (0.5 * scale)
        return half_x, half_y, shade * scale / albedo

    def strip(index, carry):
        first = pl.multiple_of(index * STRIP, STRIP)
        row = index // (tile_rows // STRIP)
        result = run(pl.ds(first, STRIP), STRIP, lambda number: [params[number * ROWS + row, k] for k in range(PARAMS)])
        if result is not None:
            slope_x, slope_y, _ = refs
            slope_x[pl.ds(first, STRIP), :] = result[0]
            slope_y[pl.ds(pl.multiple_of(first + 8, 8), STRIP), :] = result[1]
            for half in range(STRIP // 8):
                out_ref[index * (STRIP // 8) + half, 8:16, :] = result[2][half * 8 : half * 8 + 8]
        return carry

    lax.fori_loop(0, pixels // STRIP, strip, 0)

    west_half = lax.broadcasted_iota(jnp.int32, (ROWS, tile_cols), 1) < tile_rows

    def side_values(number):
        rows = lines[number * ROWS : (number + 1) * ROWS, :]
        values = []
        for k in range(PARAMS):
            west, east = (
                jnp.broadcast_to(rows[:, n * PARAMS + k : n * PARAMS + k + 1], (ROWS, tile_cols)) for n in (1, 2)
            )
            values.append(jnp.where(west_half, west, east))
        return values

    result = run(slice(pixels, pixels + ROWS), ROWS, side_values)
    if result is None:
        return

    slope_x, slope_y, side = refs
    column = column_ref[0]
    side[...] = turned(result[0])
    slope_y[7:8, :] = -slope_y[8:9, :]
    slope_y[8 + pixels : 9 + pixels, :] = -slope_y[7 + pixels : 8 + pixels, :]
    lane = lax.broadcasted_iota(jnp.int32, (tile_rows, tile_cols), 1)
    for row in range(ROWS):
        start = row * tile_rows
        here = slope_x[start : start + tile_rows, :]
        west = pltpu.roll(side[:tile_rows, :], (tile_cols - row) % tile_cols, 1)
        east = pltpu.roll(side[tile_rows:, :], tile_cols - 1 - row, 1)
        before = jnp.where(lane == 0, jnp.where(column == 0, -here, west), pltpu.roll(here, 1, 1))
        after = jnp.where(
            lane == tile_cols - 1,
            jnp.where(column == CLASSES * CORES - 1, -here, east),
            pltpu.roll(here, tile_cols - 1, 1),
        )
        spread = before - after + slope_y[start + 7 : start + 7 + tile_rows, :] - slope_y[start + 9 : start + 9 + tile_rows, :]
        for group in range(tile_rows // 8):
            out_ref[row * (tile_rows // 8) + group, 0:8, :] = spread[group * 8 : group * 8 + 8]


def terms(column, maps, sums, got, scale):
    arrays, picks = zip(*got)
    count = sum(len(some) for some in picks)
    given = [maps] + ([] if sums is None else [sums]) + list(arrays)
    rows, cols = maps.shape[1:]
    scratch = [
        pltpu.VMEM((count * ROWS, cols), jnp.float32),
        pltpu.SMEM((count * ROWS, cols), jnp.float32),
        pltpu.SemaphoreType.DMA,
    ]
    if scale is None:
        out = (4, rows, cols)
    else:
        out = ((rows - ROWS) // 8, 16, cols)
        scratch += [pltpu.VMEM((rows - ROWS, cols), jnp.float32), pltpu.VMEM((rows - ROWS + 16, cols), jnp.float32)]
        scratch += [pltpu.VMEM((cols, cols), jnp.float32)]
    return pl.pallas_call(
        lambda *refs: terms_kernel(scale, sums is not None, picks, *refs),
        out_shape=pltpu.VMEM(out, jnp.float32),
        in_specs=[SMEM] + [VMEM] * len(given),
        out_specs=VMEM,
        scratch_shapes=scratch,
        cost_estimate=pl.CostEstimate(flops=60 * count * rows * cols, bytes_accessed=4 << 20, transcendentals=0),
        compiler_params=pltpu.CompilerParams(vmem_limit_bytes=4 << 20),
    )(column, *in_vmem(*given))


EACH2 = [(0,), (1,)]
EACH4 = EACH2 + [(2,), (3,)]


def body(heights, albedo, blocks, block_params, block_dest):
    column_here = lax.axis_index(("zl", "c"))
    tile_rows, tile_cols = heights.shape[1:]
    block_count = block_dest.shape[2]

    height, shade = heights[0], albedo[0]
    first, last = jnp.stack([height[:, 0], height[:, 1], shade[:, 0]]), jnp.stack([height[:, -1], height[:, -2], shade[:, -1]])
    even = lax.axis_index("c") == 0
    inward, outward = jnp.where(even, last, first), jnp.where(even, first, last)
    across = lax.ppermute(inward, "c", [(0, 1), (1, 0)])
    beyond = lax.ppermute(outward, ("zl", "c"), BETWEEN)
    from_west, from_east = jnp.where(even, beyond, across), jnp.where(even, across, beyond)

    here = jnp.stack([lax.axis_index("zl"), lax.axis_index("c")]).astype(jnp.int32)
    near, *own, other = pack(
        here,
        block_dest.reshape(block_count),
        block_params.reshape(block_count, PARAMS).T,
        blocks.reshape(block_count, tile_rows, tile_cols),
    )
    swapped = lax.ppermute(other, "c", [(0, 1), (1, 0)])
    to_first, to_second, to_far = join(here, swapped, *own)
    far = ring_shift(to_far, 2)
    next0 = ring_shift(to_first, 1)
    next1 = ring_shift(to_second, -1)

    beside = jnp.concatenate([from_west, from_east], axis=1)
    mine = jnp.concatenate([first[:1], last[:1]], axis=1)
    rows = jnp.concatenate([beside, mine, jnp.zeros((ROWS - 4, tile_cols), jnp.float32)])
    copies = make_copies(height, shade, rows)
    gathered = lax.all_to_all(copies, "y", split_axis=0, concat_axis=0, tiled=True)
    column = column_here.reshape(1).astype(jnp.int32)
    maps = make_maps(column, gathered)

    sums = terms(column, maps, None, [(near, EACH2), (swapped, [(0, 0), (0, 1)]), (far, EACH4)], None)
    sums = terms(column, maps, sums, [(next0, EACH4)], None)
    parts = terms(column, maps, sums, [(next1, EACH4)], 1.0 / block_count)
    summed = jnp.sum(lax.all_to_all(parts, ("y",) + IMG, split_axis=0, concat_axis=0, tiled=True), axis=0)
    half = tile_rows // (HALVES * DEPTH)
    return (summed[None, :half], summed[None, half:])


def solution(mesh):
    physical = Mesh(mesh.devices.reshape(ROWS, CLASSES, CORES, HALVES, DEPTH), TILE + IMG)
    placed = (
        P(TILE, None, None),
        P(TILE, None, None),
        P(TILE, IMG, None, None, None),
        P(TILE, IMG, None, None),
        P(TILE, IMG, None, None),
    )

    return jax.shard_map(
        body,
        mesh=physical,
        in_specs=placed,
        out_specs=(P(TILE, IMG, None), P(TILE, IMG, None)),
        check_vma=False,
    )
```
